128 devices in a mesh: chain: 32 (over z, x, core), group: 4 (over y).
Axes of the slice: x: 4, y: 4, z: 4, core: 2. Of those that a mesh axis runs over, the one named last changes fastest.
Arguments:
- points: bfloat16 [262144, 384], P(('chain', 'group')), may hold values from -6 to 6
- norm_gains: float32 [4, 384], replicated, may hold values from 0.1 to 1.9
- qkv_weight: bfloat16 [2, 384, 1152], replicated, may hold values from -8 to 8
- proj_weight: bfloat16 [2, 384, 384], replicated, may hold values from -0.75 to 0.75
- up_weight: bfloat16 [2, 384, 1536], replicated, may hold values from -0.3125 to 0.3125
- down_weight: bfloat16 [2, 1536, 384], replicated, may hold values from -0.15625 to 0.15625
- dest_slot: int32 [2048], P(('chain', 'group')), may hold values from 0 to 31, as said below
- owner_from: int32 [3072], P(('chain', 'group')), may hold values from -1 to 31, as said below
Outputs:
- features: bfloat16 [262144, 384], P(('chain', 'group'))
The draws below stay inside these ranges and needn't reach their ends.
Inputs may be any that keep to these rules, and one draw needn't show every extreme that they name: `dest_slot`: the 16 entries of one device are distinct. An entry o + e sends the tile to the owner at index o of chain in the same group as its e-th tile from this device; at most 1 tiles go from one device to one owner, and that many do in every draw. Together with owner_from it describes one assignment. `owner_from`: an owner's live slots come first; -1 marks an empty slot; a live entry c + e names the e-th tile that device c of chain in the same group sends here. Owners hold from 0 to 24 live tiles, and some owner holds 24 in every draw. Every tile of every device has exactly one slot.
All inputs are finite; a program needn't handle non-finite values.
Results may differ from the reference program's by a relative error of at most 0.015.
Values may be sent and summed in bfloat16 or wider, within the bound.
No kernel may reach another device: no remote copies, remote signals or barrier semaphores. Data moves between devices by JAX's collectives and lax.ppermute only.
A program may use at most 128 MiB of HBM per device.

```python
import jax
import jax.numpy as jnp
from jax import lax

D = 384
HEADS = 6
HEAD_DIM = 64
FF = 1536
PATCH = 1024
TILE = 128
TILES_DEV = 16
SLOTS = 24
CHAIN_LEN = 32
OWNER_GROUPS = 4
PEER_TILES = 1
ROWS = 262144
TILES = 2048
OWNER_SLOTS = 3072


def routing_tables(key):
    folded = jax.random.fold_in(key, 31)
    group_keys = jax.random.split(folded, OWNER_GROUPS)

    def one_group(group_key):
        keys_all = jax.random.split(group_key, 5)
        chain_count = CHAIN_LEN
        entry_total = CHAIN_LEN * TILES_DEV
        extra_most = SLOTS - TILES_DEV
        pairing = jax.random.permutation(keys_all[0], chain_count)
        shifts = jax.random.randint(keys_all[1], (chain_count // 2,), 0, extra_most + 1)
        shifts = shifts.at[0].set(extra_most)
        counts = jnp.zeros((chain_count,), jnp.int32)
        counts = counts.at[pairing[0::2]].set(TILES_DEV + shifts)
        counts = counts.at[pairing[1::2]].set(TILES_DEV - shifts)
        ordering = jax.random.permutation(keys_all[2], chain_count)
        ordered = counts[ordering]
        ending = jnp.cumsum(ordered)
        starting = ending - ordered
        entries = jnp.arange(entry_total, dtype=jnp.int32)
        position = jnp.sum((ending[None, :] <= entries[:, None]).astype(jnp.int32), axis=1)
        owners = ordering[position]
        offset = entries - starting[position]
        sources = entries % chain_count
        repeat_index = offset // chain_count
        ranking = jax.random.randint(keys_all[3], (entry_total,), 0, 4096) * entry_total + entries
        same_owner = owners[None, :] == owners[:, None]
        slot_index = jnp.sum((same_owner & (ranking[None, :] < ranking[:, None])).astype(jnp.int32), axis=1)
        tile_scores = jax.random.randint(keys_all[4], (chain_count, TILES_DEV), 0, 4096) * TILES_DEV + jnp.arange(TILES_DEV, dtype=jnp.int32)[None, :]
        tile_order = jnp.argsort(tile_scores, axis=1, stable=True).astype(jnp.int32)
        tiles_sent = tile_order[sources, entries // chain_count]
        destination = jnp.zeros((chain_count, TILES_DEV), jnp.int32).at[sources, tiles_sent].set(owners * PEER_TILES + repeat_index)
        anchor = jnp.full((chain_count, SLOTS), -1, jnp.int32).at[owners, slot_index].set(sources * PEER_TILES + repeat_index)
        return (destination, anchor)
    destination, anchor = jax.vmap(one_group)(group_keys)
    return (jnp.transpose(destination, (1, 0, 2)).reshape(-1), jnp.transpose(anchor, (1, 0, 2)).reshape(-1))


def draw_dest_slot(key, part):
    return routing_tables(key)[0]


def draw_owner_from(key, part):
    return routing_tables(key)[1]


def draw_points(key, part):
    folded = jax.random.fold_in(key, 5)
    first_key = jax.random.fold_in(folded, 0)
    values = jnp.clip(jax.random.normal(first_key, (ROWS, D), jnp.float32), -6.0, 6.0)
    return values.astype(jnp.bfloat16)


def draw_qkv_weight(key, part):
    folded = jax.random.fold_in(key, 11)
    drawn = jnp.clip(jax.random.normal(folded, (2, D, 3 * D), jnp.float32), -6.0, 6.0) * D ** (-0.5)
    queries = 2.0 * drawn[:, :, :D]
    keys_part = drawn[:, :, D:2 * D]
    return jnp.concatenate([queries, keys_part, drawn[:, :, 2 * D:]], axis=2).astype(jnp.bfloat16)


def gaussian(rng, dims, scale, bound, kind=jnp.bfloat16):
    result = jax.random.normal(rng, dims, jnp.float32) * scale
    return jnp.minimum(jnp.maximum(result, -bound), bound).astype(kind)


def setup_inputs(seed: int = 0) -> dict:
    seeds = jax.random.split(jax.random.key(seed), 9)
    return {
        "points": draw_points(jax.random.fold_in(seeds[8], 71), 0),
        "norm_gains": jnp.clip(1.0 + 0.18 * jax.random.normal(seeds[1], (4, D), jnp.float32), 0.1, 1.9),
        "qkv_weight": draw_qkv_weight(jax.random.fold_in(seeds[8], 71), 0),
        "proj_weight": gaussian(seeds[3], (2, D, D), HEAD_DIM ** -0.5, 0.75),
        "up_weight": gaussian(seeds[4], (2, D, FF), D ** -0.5, 0.3125),
        "down_weight": gaussian(seeds[5], (2, FF, D), FF ** -0.5, 0.15625),
        "dest_slot": draw_dest_slot(jax.random.fold_in(seeds[8], 71), 0),
        "owner_from": draw_owner_from(jax.random.fold_in(seeds[8], 71), 0),
    }


norm_epsilon = 1e-05
masked_score = -1000000000.0

def layer_norm(values, gain_row):
    floats = values.astype(jnp.float32)
    center = floats - lax.optimization_barrier(jnp.mean(floats, axis=-1, keepdims=True))
    spread = lax.optimization_barrier(jnp.mean(center * center, axis=-1, keepdims=True))
    return (center * lax.rsqrt(spread + norm_epsilon) * gain_row).astype(jnp.bfloat16)

def project_heads(values, gain_row, weights):
    normed = layer_norm(values, gain_row)
    return jnp.dot(normed, weights, preferred_element_type=jnp.float32).astype(jnp.bfloat16)

def attend(queries, keys_in, values_in, key_live):
    query_count = queries.shape[0]
    key_count = keys_in.shape[0]
    query_heads = queries.reshape(query_count, HEADS, HEAD_DIM).astype(jnp.float32)
    key_heads = keys_in.reshape(key_count, HEADS, HEAD_DIM).astype(jnp.float32)
    value_heads = values_in.reshape(key_count, HEADS, HEAD_DIM).astype(jnp.float32)
    scores = jnp.einsum('qhd,khd->hqk', query_heads, key_heads) * HEAD_DIM ** (-0.5)
    if key_live is not None:
        scores = jnp.where(key_live[None, None, :], scores, masked_score)
    peak = lax.optimization_barrier(jnp.max(scores, axis=-1, keepdims=True))
    exponent = jnp.exp(scores - peak)
    weights = (exponent / lax.optimization_barrier(jnp.sum(exponent, axis=-1, keepdims=True))).astype(jnp.bfloat16)
    mixed = jnp.einsum('hqk,khd->qhd', weights.astype(jnp.float32), value_heads)
    return mixed.reshape(query_count, D).astype(jnp.bfloat16)

def residual_add(base, mixed, weights):
    return (base.astype(jnp.float32) + jnp.dot(mixed, weights, preferred_element_type=jnp.float32)).astype(jnp.bfloat16)

def feed_forward(values, gain_row, weight_up, weight_down):
    normed = layer_norm(values, gain_row)
    hidden = jax.nn.gelu(jnp.dot(normed, weight_up, preferred_element_type=jnp.float32), approximate=False).astype(jnp.bfloat16)
    return residual_add(values, hidden, weight_down)

def reference(points, norm_gains, qkv_weight, proj_weight, up_weight, down_weight, dest_slot, owner_from):
    half_rows = PATCH // 2
    shifted = jnp.roll(points, -half_rows, axis=0).reshape(ROWS // PATCH, PATCH, D)

    def z_block(patch):
        qkv_rows = project_heads(patch, norm_gains[0], qkv_weight[0])
        mixed = attend(qkv_rows[:, :D], qkv_rows[:, D:2 * D], qkv_rows[:, 2 * D:], None)
        inner = residual_add(patch, mixed, proj_weight[0])
        return feed_forward(inner, norm_gains[1], up_weight[0], down_weight[0])
    outer_a = jnp.roll(lax.map(z_block, shifted).reshape(ROWS, D), half_rows, axis=0)
    tile_index = jnp.arange(TILES, dtype=jnp.int32)
    device = tile_index // TILES_DEV
    chain_pos = device // OWNER_GROUPS
    group_pos = device % OWNER_GROUPS
    owner = (dest_slot // PEER_TILES * OWNER_GROUPS + group_pos).astype(jnp.int32)
    wanted = chain_pos * PEER_TILES + dest_slot % PEER_TILES
    owner_table = owner_from.reshape(CHAIN_LEN * OWNER_GROUPS, SLOTS)
    candidates = owner_table[owner]
    slot_pos = lax.optimization_barrier(jnp.sum(jnp.where(candidates == wanted[:, None], jnp.arange(SLOTS, dtype=jnp.int32)[None, :], 0), axis=1)).astype(jnp.int32)
    target = (owner * SLOTS + slot_pos).astype(jnp.int32)
    tile_data = outer_a.reshape(TILES, TILE, D)
    hilbert = jnp.zeros((OWNER_SLOTS, TILE, D), jnp.bfloat16).at[target].set(tile_data)
    live = jnp.repeat(owner_from >= 0, TILE)
    patch_count = OWNER_SLOTS * TILE // PATCH
    patches = hilbert.reshape(patch_count, PATCH, D)
    live_patches = live.reshape(patch_count, PATCH)

    def h_block(paired):
        patch, key_live = paired
        qkv_rows = project_heads(patch, norm_gains[2], qkv_weight[1])
        mixed = attend(qkv_rows[:, :D], qkv_rows[:, D:2 * D], qkv_rows[:, 2 * D:], key_live)
        inner = residual_add(patch, mixed, proj_weight[1])
        return feed_forward(inner, norm_gains[3], up_weight[1], down_weight[1])
    outer_b = lax.map(h_block, (patches, live_patches)).reshape(OWNER_SLOTS, TILE, D)
    return outer_b[target].reshape(ROWS, D)
```

```python
import functools

import jax
import jax.numpy as jnp
from jax import lax
from jax.experimental import pallas as pl
from jax.experimental.pallas import tpu as pltpu
from jax.sharding import PartitionSpec as P

D = 384
HEADS = 6
HEAD_DIM = 64
FF = 1536
PATCH = 1024
TILE = 128
TILES_DEV = 16
SLOTS = 24
PEERS = 32
PAIRS = HEADS // 2
CHUNKS = 2
PART = TILE // CHUNKS
PATCH_TILES = PATCH // TILE
UNIT_TILES = 4
HALF = PATCH // 2
HID = 256

norm_epsilon = 1e-05
masked_score = -1000000000.0
query_scale = HEAD_DIM ** (-0.5) * 1.4426950408889634
f32 = jnp.float32
bf16 = jnp.bfloat16


def norm_rows(values, gain_row):
    center = values - jnp.mean(values, axis=-1, keepdims=True)
    spread = jnp.mean(center * center, axis=-1, keepdims=True)
    return (center * lax.rsqrt(spread + norm_epsilon) * gain_row).astype(bf16)


def gelu(x):
    return (0.5 * x) * (1.0 + lax.erf(x * 0.5 ** 0.5))


def dot(a, b):
    return jnp.dot(a, b, preferred_element_type=f32)


def dot_t(a, b):
    return lax.dot_general(a, b, (((1,), (1,)), ((), ())), preferred_element_type=f32)


def whole(shape):
    zeros = (0,) * len(shape)
    return pl.BlockSpec(shape, lambda *_: zeros)


def layer_of(shape, layer):
    zeros = (0,) * len(shape)
    return pl.BlockSpec((None, *shape), lambda *_: (layer, *zeros))


def qkv_own_kernel(x_ref, gains_ref, w_ref, q_ref, k_ref, v_ref):
    normed = norm_rows(x_ref[...].astype(f32), gains_ref[0:1, :])
    out = dot(normed, w_ref[...])
    q_ref[...] = (out[:, :D] * query_scale).astype(bf16)
    k_ref[...] = out[:, D : 2 * D].astype(bf16)
    v_ref[...] = out[:, 2 * D :].astype(bf16)


def qkv_own(points, gains, qkv_weight):
    rows = points.shape[0]
    ext = jax.ShapeDtypeStruct((rows + PATCH, D), bf16)
    return pl.pallas_call(
        qkv_own_kernel,
        grid=(rows // HALF,),
        in_specs=[
            pl.BlockSpec((HALF, D), lambda i: (i, 0)),
            whole((4, D)),
            layer_of((D, 3 * D), 0),
        ],
        out_specs=[
            pl.BlockSpec((HALF, D), lambda i: (i, 0)),
            pl.BlockSpec((HALF, D), lambda i: (i + 1, 0)),
            pl.BlockSpec((HALF, D), lambda i: (i + 1, 0)),
        ],
        out_shape=[jax.ShapeDtypeStruct((rows, D), bf16), ext, ext],
        name="qkv_own",
    )(points, gains, qkv_weight)


def qkv_halo_kernel(a_ref, b_ref, gains_ref, w_ref, k_in, v_in, k_ref, v_ref):
    first = pl.program_id(0) == 0
    rows = jnp.where(first, a_ref[...].astype(f32), b_ref[...].astype(f32))
    normed = norm_rows(rows, gains_ref[0:1, :])
    out = dot(normed, w_ref[:, D:])
    k_ref[...] = out[:, :D].astype(bf16)
    v_ref[...] = out[:, D:].astype(bf16)


def qkv_halo(before, after, gains, qkv_weight, keys, values):
    last = keys.shape[0] // HALF - 1
    ext = jax.ShapeDtypeStruct(keys.shape, bf16)
    return pl.pallas_call(
        qkv_halo_kernel,
        grid=(2,),
        in_specs=[
            whole((HALF, D)),
            whole((HALF, D)),
            whole((4, D)),
            layer_of((D, 3 * D), 0),
            pl.BlockSpec(memory_space=pl.ANY),
            pl.BlockSpec(memory_space=pl.ANY),
        ],
        out_specs=[pl.BlockSpec((HALF, D), lambda i: (i * last, 0))] * 2,
        out_shape=[ext, ext],
        input_output_aliases={4: 0, 5: 1},
        name="qkv_halo",
    )(before, after, gains, qkv_weight, keys, values)


def qkv_owner_kernel(from_ref, part_ref, gains_ref, w_ref, x_ref, q_ref, k_ref, v_ref):
    step = pl.program_id(0)
    tiles = []
    for t in range(PATCH_TILES):
        source = from_ref[step * PATCH_TILES + t]
        tile = part_ref[jnp.maximum(source, 0)]
        tiles.append(jnp.where(source >= 0, tile.astype(f32), 0.0))
    rows = jnp.concatenate(tiles, axis=0)
    shape = (PATCH_TILES, PART, D)
    x_ref[...] = rows.astype(bf16).reshape(shape)
    normed = norm_rows(rows, gains_ref[2:3, :])
    out = dot(normed, w_ref[...])
    q_ref[...] = (out[:, :D] * query_scale).astype(bf16).reshape(shape)
    k_ref[...] = out[:, D : 2 * D].astype(bf16).reshape(shape)
    v_ref[...] = out[:, 2 * D :].astype(bf16).reshape(shape)


def qkv_owner(owner_from, part, gains, qkv_weight):
    block = pl.BlockSpec((PATCH_TILES, PART, D), lambda i, *_: (i, 0, 0))
    shape = jax.ShapeDtypeStruct((SLOTS, PART, D), bf16)
    return pl.pallas_call(
        qkv_owner_kernel,
        grid_spec=pltpu.PrefetchScalarGridSpec(
            num_scalar_prefetch=1,
            grid=(SLOTS // PATCH_TILES,),
            in_specs=[whole((PEERS, PART, D)), whole((4, D)), layer_of((D, 3 * D), 1)],
            out_specs=[block] * 4,
        ),
        out_shape=[shape] * 4,
        name="qkv_owner",
    )(owner_from, part, gains, qkv_weight)


def block_kernel(units, masked, gain, pieces, table_ref, x_ref, q_ref, *refs):
    k_refs, refs = refs[:pieces], refs[pieces:]
    v_refs, refs = refs[:pieces], refs[pieces:]
    gains_ref, proj_ref, up_ref, down_ref, out_ref, inner_ref, normed_ref = refs
    step = pl.program_id(0)
    count = UNIT_TILES * PART
    lanes = lax.broadcasted_iota(jnp.int32, (1, 128), 1)
    low = lanes < HEAD_DIM
    picks = [low.astype(f32).astype(bf16), (~low).astype(f32).astype(bf16)]

    def attention_parts():
        queries = q_ref[...].reshape(count, D)
        rows = PATCH // pieces
        ones = jnp.ones((rows, 128), bf16)
        extra_q = extra_k = None
        if masked:
            unit = jnp.minimum(step, units - 1)
            base = (unit * UNIT_TILES) // PATCH_TILES * PATCH_TILES
            extra_q = jnp.broadcast_to((lanes == 0).astype(f32).astype(bf16), (count, 128))
            marks = []
            for t in range(PATCH_TILES):
                mark = jnp.where(table_ref[base + t] >= 0, 0.0, masked_score)
                marks.append(jnp.full((rows // PATCH_TILES, 128), mark, f32).astype(bf16))
            extra_k = jnp.concatenate(marks, axis=0)

        def scores(h):
            cols = slice(128 * (h // 2), 128 * (h // 2) + 128)
            q = queries[:, cols] * picks[h % 2]
            if masked:
                q = jnp.concatenate([q, extra_q], axis=1)
            out = []
            for k_ref in k_refs:
                k = k_ref[...].reshape(rows, D)[:, cols]
                if masked:
                    k = jnp.concatenate([k, extra_k], axis=1)
                out.append(dot_t(q, k))
            return out

        def soften(parts):
            peak = functools.reduce(
                jnp.maximum, [jnp.max(s, axis=-1, keepdims=True) for s in parts]
            )
            return [jnp.exp2(s - peak).astype(bf16) for s in parts]

        def mix(h, parts):
            cols = slice(128 * (h // 2), 128 * (h // 2) + 128)
            total = None
            for p, v_ref in zip(parts, v_refs):
                v = v_ref[...].reshape(rows, D)[:, cols]
                one = dot(p, jnp.concatenate([v, ones], axis=1))
                total = one if total is None else total + one
            return total[:, :128] / total[:, 128:]

        return scores, soften, mix

    def join(mixed):
        pairs = [jnp.where(low, mixed[2 * i], mixed[2 * i + 1]) for i in range(PAIRS)]
        joined = jnp.concatenate(pairs, axis=1).astype(bf16)
        base = x_ref[...].reshape(count, D).astype(f32)
        inner = (base + dot(joined, proj_ref[...])).astype(bf16)
        inner_ref[...] = inner
        normed_ref[...] = norm_rows(inner.astype(f32), gains_ref[gain : gain + 1, :])

    def hidden(normed, j):
        return gelu(dot(normed, up_ref[:, HID * j : HID * (j + 1)])).astype(bf16)

    def down(part, j):
        return dot(part, down_ref[HID * j : HID * (j + 1), :])

    def emit(inner, total):
        outer = (inner.astype(f32) + total).astype(bf16)
        for t in range(UNIT_TILES):
            slot = table_ref[(step - 1) * UNIT_TILES + t]

            @pl.when(slot >= 0)
            def _():
                out_ref[jnp.maximum(slot, 0)] = outer[t * PART : (t + 1) * PART]

    @pl.when(step == 0)
    def _():
        scores, soften, mix = attention_parts()
        mixed = []
        s = scores(0)
        for h in range(HEADS):
            later = scores(h + 1) if h + 1 < HEADS else None
            mixed.append(mix(h, soften(s)))
            s = later
        join(mixed)

    @pl.when((step > 0) & (step < units))
    def _():
        scores, soften, mix = attention_parts()
        inner, normed = inner_ref[...], normed_ref[...]
        mixed = []
        total = None
        s = scores(0)
        for h in range(HEADS):
            later = scores(h + 1) if h + 1 < HEADS else None
            part = hidden(normed, h)
            mixed.append(mix(h, soften(s)))
            one = down(part, h)
            total = one if total is None else total + one
            s = later
        emit(inner, total)
        join(mixed)

    @pl.when(step == units)
    def _():
        inner, normed = inner_ref[...], normed_ref[...]
        total = None
        for h in range(HEADS):
            one = down(hidden(normed, h), h)
            total = one if total is None else total + one
        emit(inner, total)


def block(name, table, x, q, keys, values, x_spec, key_spec, units, masked, layer, weights):
    gains, proj_weight, up_weight, down_weight = weights
    pieces = len(keys)
    count = UNIT_TILES * PART
    return pl.pallas_call(
        functools.partial(block_kernel, units, masked, 2 * layer + 1, pieces),
        grid_spec=pltpu.PrefetchScalarGridSpec(
            num_scalar_prefetch=1,
            grid=(units + 1,),
            in_specs=[x_spec, x_spec]
            + [key_spec] * (2 * pieces)
            + [
                whole((4, D)),
                layer_of((D, D), layer),
                layer_of((D, FF), layer),
                layer_of((FF, D), layer),
            ],
            out_specs=whole((PEERS, PART, D)),
            scratch_shapes=[pltpu.VMEM((count, D), bf16), pltpu.VMEM((count, D), bf16)],
        ),
        out_shape=jax.ShapeDtypeStruct((PEERS, PART, D), bf16),
        name=name,
    )(table, x, q, *keys, *values, gains, proj_weight, up_weight, down_weight)


def last_unit(i, units):
    return jnp.minimum(i, units - 1)


def block_a(chunk, table, x, q, keys, values, weights):
    units = TILES_DEV // UNIT_TILES
    x_spec = pl.BlockSpec(
        (UNIT_TILES, PART, D), lambda i, *_: (last_unit(i, units), chunk, 0)
    )
    key_spec = pl.BlockSpec((PATCH, D), lambda i, *_: ((last_unit(i, units) + 1) // 2, 0))
    return block(
        "block_a", table, x, q, [keys], [values], x_spec, key_spec, units, False, 0, weights
    )


def block_b(table, x, q, keys, values, weights):
    units = SLOTS // UNIT_TILES
    x_spec = pl.BlockSpec((UNIT_TILES, PART, D), lambda i, *_: (last_unit(i, units), 0, 0))
    key_spec = pl.BlockSpec(
        (PATCH_TILES, PART, D), lambda i, *_: (last_unit(i, units) // 2, 0, 0)
    )
    return block(
        "block_b", table, x, q, keys, values, x_spec, key_spec, units, True, 1, weights
    )


def home_kernel(table_ref, *refs):
    parts, out_ref, sems = refs[:CHUNKS], refs[CHUNKS], refs[CHUNKS + 1]
    copies = []
    for c, part_ref in enumerate(parts):
        for t in range(TILES_DEV):
            copies.append(
                pltpu.make_async_copy(
                    part_ref.at[table_ref[t]],
                    out_ref.at[t, pl.ds(c * PART, PART)],
                    sems.at[c * TILES_DEV + t],
                )
            )
    for copy in copies:
        copy.start()
    for copy in copies:
        copy.wait()


def home(table, parts):
    return pl.pallas_call(
        home_kernel,
        grid_spec=pltpu.PrefetchScalarGridSpec(
            num_scalar_prefetch=1,
            grid=(1,),
            in_specs=[pl.BlockSpec(memory_space=pl.ANY)] * CHUNKS,
            out_specs=pl.BlockSpec(memory_space=pl.ANY),
            scratch_shapes=[pltpu.SemaphoreType.DMA((CHUNKS * TILES_DEV,))],
        ),
        out_shape=jax.ShapeDtypeStruct((TILES_DEV, TILE, D), bf16),
        name="home",
    )(table, *parts)


def exchange(part):
    return lax.all_to_all(part, "chain", split_axis=0, concat_axis=0, tiled=True)


def body(
    points, norm_gains, qkv_weight, proj_weight, up_weight, down_weight, dest_slot, owner_from
):
    rows = points.shape[0]
    axes = ("chain", "group")
    ring = lax.axis_size(axes)
    before = lax.ppermute(points[rows - HALF :], axes, [(i, (i + 1) % ring) for i in range(ring)])
    after = lax.ppermute(points[:HALF], axes, [((i + 1) % ring, i) for i in range(ring)])
    weights = (norm_gains, proj_weight, up_weight, down_weight)
    q, keys, values = qkv_own(points, norm_gains, qkv_weight)
    keys, values = qkv_halo(before, after, norm_gains, qkv_weight, keys, values)
    tiled = (TILES_DEV, TILE, D)
    x, q = points.reshape(tiled), q.reshape(tiled)
    sent = []
    for chunk in range(CHUNKS):
        packed = block_a(chunk, dest_slot, x, q, keys, values, weights)
        sent.append(exchange(packed))
    owned = [qkv_owner(owner_from, part, norm_gains, qkv_weight) for part in sent]
    owner_keys = [one[2] for one in owned]
    owner_values = [one[3] for one in owned]
    returned = []
    for chunk in range(CHUNKS):
        done = block_b(
            owner_from, owned[chunk][0], owned[chunk][1], owner_keys, owner_values, weights
        )
        returned.append(exchange(done))
    return home(dest_slot, returned).reshape(rows, D)


def solution(mesh):
    placed = (
        P(("chain", "group"), None),
        P(),
        P(),
        P(),
        P(),
        P(),
        P(("chain", "group")),
        P(("chain", "group")),
    )
    return jax.shard_map(
        body, mesh=mesh, in_specs=placed, out_specs=P(("chain", "group"), None), check_vma=False
    )
```

```python
import functools

import jax
import jax.numpy as jnp
from jax import lax
from jax.experimental import pallas as pl
from jax.experimental.pallas import tpu as pltpu
from jax.sharding import PartitionSpec as P

D = 384
HEADS = 6
HEAD_DIM = 64
FF = 1536
PATCH = 1024
TILE = 128
TILES_DEV = 16
SLOTS = 24
PEERS = 32
PAIRS = HEADS // 2
CHUNKS = 2
PART = TILE // CHUNKS
PATCH_TILES = PATCH // TILE
UNIT_TILES = 4
HALF = PATCH // 2
HID = 256

norm_epsilon = 1e-05
masked_score = -1000000000.0
query_scale = HEAD_DIM ** (-0.5) * 1.4426950408889634
f32 = jnp.float32
bf16 = jnp.bfloat16


def norm_rows(values, gain_row):
    center = values - jnp.mean(values, axis=-1, keepdims=True)
    spread = jnp.mean(center * center, axis=-1, keepdims=True)
    return (center * lax.rsqrt(spread + norm_epsilon) * gain_row).astype(bf16)


def gelu(x):
    return (0.5 * x) * (1.0 + lax.erf(x * 0.5 ** 0.5))


def dot(a, b):
    return jnp.dot(a, b, preferred_element_type=f32)


def dot_t(a, b):
    return lax.dot_general(a, b, (((1,), (1,)), ((), ())), preferred_element_type=f32)


def dot_lead(a, b):
    return lax.dot_general(a, b, (((0,), (0,)), ((), ())), preferred_element_type=f32)


def dot_cross(a, b):
    return lax.dot_general(a, b, (((0,), (1,)), ((), ())), preferred_element_type=f32)


def whole(shape):
    zeros = (0,) * len(shape)
    return pl.BlockSpec(shape, lambda *_: zeros)


def layer_of(shape, layer):
    zeros = (0,) * len(shape)
    return pl.BlockSpec((None, *shape), lambda *_: (layer, *zeros))


def qkv_own_kernel(x_ref, gains_ref, w_ref, q_ref, k_ref, v_ref):
    normed = norm_rows(x_ref[...].astype(f32), gains_ref[0:1, :])
    out = dot(normed, w_ref[:, : 2 * D])
    q_ref[...] = (out[:, :D] * query_scale).astype(bf16)
    k_ref[...] = out[:, D:].astype(bf16)
    v_ref[...] = dot_cross(w_ref[:, 2 * D :], normed).astype(bf16)


def qkv_own(points, gains, qkv_weight):
    rows = points.shape[0]
    return pl.pallas_call(
        qkv_own_kernel,
        grid=(rows // HALF,),
        in_specs=[
            pl.BlockSpec((HALF, D), lambda i: (i, 0)),
            whole((4, D)),
            layer_of((D, 3 * D), 0),
        ],
        out_specs=[
            pl.BlockSpec((HALF, D), lambda i: (i, 0)),
            pl.BlockSpec((HALF, D), lambda i: (i + 1, 0)),
            pl.BlockSpec((D, HALF), lambda i: (0, i + 1)),
        ],
        out_shape=[
            jax.ShapeDtypeStruct((rows, D), bf16),
            jax.ShapeDtypeStruct((rows + PATCH, D), bf16),
            jax.ShapeDtypeStruct((D, rows + PATCH), bf16),
        ],
        name="qkv_own",
    )(points, gains, qkv_weight)


def qkv_halo_kernel(a_ref, b_ref, gains_ref, w_ref, k_in, v_in, k_ref, v_ref):
    first = pl.program_id(0) == 0
    rows = jnp.where(first, a_ref[...].astype(f32), b_ref[...].astype(f32))
    normed = norm_rows(rows, gains_ref[0:1, :])
    k_ref[...] = dot(normed, w_ref[:, D : 2 * D]).astype(bf16)
    v_ref[...] = dot_cross(w_ref[:, 2 * D :], normed).astype(bf16)


def qkv_halo(before, after, gains, qkv_weight, keys, values):
    last = keys.shape[0] // HALF - 1
    return pl.pallas_call(
        qkv_halo_kernel,
        grid=(2,),
        in_specs=[
            whole((HALF, D)),
            whole((HALF, D)),
            whole((4, D)),
            layer_of((D, 3 * D), 0),
            pl.BlockSpec(memory_space=pl.ANY),
            pl.BlockSpec(memory_space=pl.ANY),
        ],
        out_specs=[
            pl.BlockSpec((HALF, D), lambda i: (i * last, 0)),
            pl.BlockSpec((D, HALF), lambda i: (0, i * last)),
        ],
        out_shape=[
            jax.ShapeDtypeStruct(keys.shape, bf16),
            jax.ShapeDtypeStruct(values.shape, bf16),
        ],
        input_output_aliases={4: 0, 5: 1},
        name="qkv_halo",
    )(before, after, gains, qkv_weight, keys, values)


def qkv_owner_kernel(from_ref, part_ref, gains_ref, w_ref, x_ref, q_ref, k_ref, v_ref):
    step = pl.program_id(0)
    tiles = []
    for t in range(PATCH_TILES):
        source = from_ref[step * PATCH_TILES + t]
        tile = part_ref[jnp.maximum(source, 0)]
        tiles.append(jnp.where(source >= 0, tile.astype(f32), 0.0))
    rows = jnp.concatenate(tiles, axis=0)
    shape = (PATCH_TILES, PART, D)
    x_ref[...] = rows.astype(bf16).reshape(shape)
    normed = norm_rows(rows, gains_ref[2:3, :])
    out = dot(normed, w_ref[:, : 2 * D])
    q_ref[...] = (out[:, :D] * query_scale).astype(bf16).reshape(shape)
    k_ref[...] = out[:, D:].astype(bf16).reshape(shape)
    v_ref[...] = dot_cross(w_ref[:, 2 * D :], normed).astype(bf16)


def qkv_owner(owner_from, part, gains, qkv_weight):
    patches = SLOTS // PATCH_TILES
    count = PATCH_TILES * PART
    block = pl.BlockSpec((PATCH_TILES, PART, D), lambda i, *_: (i, 0, 0))
    shape = jax.ShapeDtypeStruct((SLOTS, PART, D), bf16)
    return pl.pallas_call(
        qkv_owner_kernel,
        grid_spec=pltpu.PrefetchScalarGridSpec(
            num_scalar_prefetch=1,
            grid=(patches,),
            in_specs=[
                pl.BlockSpec(memory_space=pltpu.VMEM),
                whole((4, D)),
                layer_of((D, 3 * D), 1),
            ],
            out_specs=[block] * 3 + [pl.BlockSpec((None, D, count), lambda i, *_: (i, 0, 0))],
        ),
        out_shape=[shape] * 3 + [jax.ShapeDtypeStruct((patches, D, count), bf16)],
        compiler_params=pltpu.CompilerParams(vmem_limit_bytes=24 << 20),
        name="qkv_owner",
    )(owner_from, part, gains, qkv_weight)


def block_kernel(units, masked, layer, pieces, table_ref, x_ref, q_ref, *refs):
    k_refs, refs = refs[:pieces], refs[pieces:]
    v_refs, refs = refs[:pieces], refs[pieces:]
    gains_ref, *sources, out_ref, mixed_ref, proj_ref, up_ref, down_ref, sems = refs
    step = pl.program_id(0)
    count = UNIT_TILES * PART
    rows = PATCH // pieces
    lanes = lax.broadcasted_iota(jnp.int32, (1, 128), 1)
    low = lanes < HEAD_DIM
    picks = [low.astype(f32).astype(bf16), (~low).astype(f32).astype(bf16)]
    fetches = [
        pltpu.make_async_copy(source.at[layer], target, sems.at[i])
        for i, (source, target) in enumerate(zip(sources, (proj_ref, up_ref, down_ref)))
    ]

    def attention_parts():
        queries = q_ref[...].reshape(count, D)
        ones = jnp.ones((16, rows), bf16)
        extra_q = extra_k = None
        if masked:
            base = (step * UNIT_TILES) // PATCH_TILES * PATCH_TILES
            extra_q = jnp.broadcast_to((lanes == 0).astype(f32).astype(bf16), (count, 128))
            marks = []
            for t in range(PATCH_TILES):
                mark = jnp.where(table_ref[base + t] >= 0, 0.0, masked_score)
                marks.append(jnp.full((rows // PATCH_TILES, 128), mark, f32).astype(bf16))
            extra_k = jnp.concatenate(marks, axis=0)

        def scores(h):
            cols = slice(128 * (h // 2), 128 * (h // 2) + 128)
            q = queries[:, cols] * picks[h % 2]
            if masked:
                q = jnp.concatenate([q, extra_q], axis=1)
            out = []
            for k_ref in k_refs:
                k = k_ref[...].reshape(rows, D)[:, cols]
                if masked:
                    k = jnp.concatenate([k, extra_k], axis=1)
                out.append(dot_t(k, q))
            return out

        def soften(parts):
            peak = functools.reduce(
                jnp.maximum, [jnp.max(s, axis=0, keepdims=True) for s in parts]
            )
            return [jnp.exp2(s - peak).astype(bf16) for s in parts]

        def mix(h, parts):
            cols = slice(HEAD_DIM * h, HEAD_DIM * (h + 1))
            total = None
            for p, v_ref in zip(parts, v_refs):
                one = dot(jnp.concatenate([v_ref[cols, :], ones], axis=0), p)
                total = one if total is None else total + one
            mixed_ref[cols, :] = (total[:HEAD_DIM] / total[HEAD_DIM : HEAD_DIM + 1]).astype(bf16)

        return scores, soften, mix

    def join(mixed):
        base = x_ref[...].reshape(count, D).astype(f32)
        inner = (base + dot_lead(mixed, proj_ref[...])).astype(bf16)
        gain = gains_ref[2 * layer + 1 : 2 * layer + 2, :]
        return inner, norm_rows(inner.astype(f32), gain)

    def hidden(normed, j):
        return gelu(dot(normed, up_ref[:, HID * j : HID * (j + 1)])).astype(bf16)

    def down(part, j):
        return dot(part, down_ref[HID * j : HID * (j + 1), :])

    def emit(inner, total):
        outer = (inner.astype(f32) + total).astype(bf16)
        for t in range(UNIT_TILES):
            slot = table_ref[(step - 1) * UNIT_TILES + t]

            @pl.when(slot >= 0)
            def _():
                out_ref[jnp.maximum(slot, 0)] = outer[t * PART : (t + 1) * PART]

    @pl.when(step == 0)
    def _():
        for fetch in fetches:
            fetch.start()
        scores, soften, mix = attention_parts()
        s = scores(0)
        for h in range(HEADS):
            later = scores(h + 1) if h + 1 < HEADS else None
            mix(h, soften(s))
            s = later
        for fetch in fetches:
            fetch.wait()

    @pl.when((step > 0) & (step < units))
    def _():
        mixed = mixed_ref[...]
        scores, soften, mix = attention_parts()
        s = scores(0)
        inner, normed = join(mixed)
        total = None
        for h in range(HEADS):
            later = scores(h + 1) if h + 1 < HEADS else None
            part = hidden(normed, h)
            mix(h, soften(s))
            one = down(part, h)
            total = one if total is None else total + one
            s = later
        emit(inner, total)

    @pl.when(step == units)
    def _():
        inner, normed = join(mixed_ref[...])
        total = None
        for h in range(HEADS):
            one = down(hidden(normed, h), h)
            total = one if total is None else total + one
        emit(inner, total)


def block(name, table, x, q, keys, values, specs, units, masked, layer, weights):
    gains, *matrices = weights
    pieces = len(keys)
    count = UNIT_TILES * PART
    x_spec, q_spec, key_spec, value_spec = specs
    return pl.pallas_call(
        functools.partial(block_kernel, units, masked, layer, pieces),
        grid_spec=pltpu.PrefetchScalarGridSpec(
            num_scalar_prefetch=1,
            grid=(units + 1,),
            in_specs=[x_spec, q_spec]
            + [key_spec] * pieces
            + [value_spec] * pieces
            + [whole((4, D))]
            + [pl.BlockSpec(memory_space=pl.ANY)] * len(matrices),
            out_specs=whole((PEERS, PART, D)),
            scratch_shapes=[
                pltpu.VMEM((D, count), bf16),
                pltpu.VMEM((D, D), bf16),
                pltpu.VMEM((D, FF), bf16),
                pltpu.VMEM((FF, D), bf16),
                pltpu.SemaphoreType.DMA((len(matrices),)),
            ],
        ),
        out_shape=jax.ShapeDtypeStruct((PEERS, PART, D), bf16),
        name=name,
    )(table, x, q, *keys, *values, gains, *matrices)


def now(i, units):
    return jnp.minimum(i, units - 1)


def prior(i):
    return jnp.maximum(i - 1, 0)


def block_a(chunk, table, x, q, keys, values, weights):
    units = TILES_DEV // UNIT_TILES
    shape = (UNIT_TILES, PART, D)
    specs = [
        pl.BlockSpec(shape, lambda i, *_: (prior(i), chunk, 0)),
        pl.BlockSpec(shape, lambda i, *_: (now(i, units), chunk, 0)),
        pl.BlockSpec((PATCH, D), lambda i, *_: ((now(i, units) + 1) // 2, 0)),
        pl.BlockSpec((D, PATCH), lambda i, *_: (0, (now(i, units) + 1) // 2)),
    ]
    return block("block_a", table, x, q, [keys], [values], specs, units, False, 0, weights)


def block_b(table, x, q, keys, values, weights):
    units = SLOTS // UNIT_TILES
    shape = (UNIT_TILES, PART, D)
    patch = (PATCH_TILES, PART, D)
    flat = (None, D, PATCH_TILES * PART)
    specs = [
        pl.BlockSpec(shape, lambda i, *_: (prior(i), 0, 0)),
        pl.BlockSpec(shape, lambda i, *_: (now(i, units), 0, 0)),
        pl.BlockSpec(patch, lambda i, *_: (now(i, units) // 2, 0, 0)),
        pl.BlockSpec(flat, lambda i, *_: (now(i, units) // 2, 0, 0)),
    ]
    return block("block_b", table, x, q, keys, values, specs, units, True, 1, weights)


def home_kernel(table_ref, *refs):
    parts, out_ref = refs[:CHUNKS], refs[CHUNKS]
    for t in range(TILES_DEV):
        for c, part_ref in enumerate(parts):
            out_ref[t, c * PART : (c + 1) * PART] = part_ref[table_ref[t]]


def home(table, parts):
    return pl.pallas_call(
        home_kernel,
        grid_spec=pltpu.PrefetchScalarGridSpec(
            num_scalar_prefetch=1,
            grid=(1,),
            in_specs=[pl.BlockSpec(memory_space=pltpu.VMEM)] * CHUNKS,
            out_specs=whole((TILES_DEV, TILE, D)),
        ),
        out_shape=jax.ShapeDtypeStruct((TILES_DEV, TILE, D), bf16),
        compiler_params=pltpu.CompilerParams(vmem_limit_bytes=12 << 20),
        name="home",
    )(table, *parts)


def exchange(part):
    return lax.all_to_all(part, "chain", split_axis=0, concat_axis=0, tiled=True)


def body(
    points, norm_gains, qkv_weight, proj_weight, up_weight, down_weight, dest_slot, owner_from
):
    rows = points.shape[0]
    axes = ("chain", "group")
    ring = lax.axis_size(axes)
    before = lax.ppermute(points[rows - HALF :], axes, [(i, (i + 1) % ring) for i in range(ring)])
    after = lax.ppermute(points[:HALF], axes, [((i + 1) % ring, i) for i in range(ring)])
    weights = (norm_gains, proj_weight, up_weight, down_weight)
    q, keys, values = qkv_own(points, norm_gains, qkv_weight)
    keys, values = qkv_halo(before, after, norm_gains, qkv_weight, keys, values)
    tiled = (TILES_DEV, TILE, D)
    x, q = points.reshape(tiled), q.reshape(tiled)
    sent = []
    for chunk in range(CHUNKS):
        packed = block_a(chunk, dest_slot, x, q, keys, values, weights)
        sent.append(exchange(packed))
    owned = [qkv_owner(owner_from, part, norm_gains, qkv_weight) for part in sent]
    owner_keys = [one[2] for one in owned]
    owner_values = [one[3] for one in owned]
    returned = []
    for chunk in range(CHUNKS):
        done = block_b(
            owner_from, owned[chunk][0], owned[chunk][1], owner_keys, owner_values, weights
        )
        returned.append(exchange(done))
    return home(dest_slot, returned).reshape(rows, D)


def solution(mesh):
    placed = (
        P(("chain", "group"), None),
        P(),
        P(),
        P(),
        P(),
        P(),
        P(("chain", "group")),
        P(("chain", "group")),
    )
    return jax.shard_map(
        body, mesh=mesh, in_specs=placed, out_specs=P(("chain", "group"), None), check_vma=False
    )
```

```python
import functools

import jax
import jax.numpy as jnp
from jax import lax
from jax.experimental import pallas as pl
from jax.experimental.pallas import tpu as pltpu
from jax.sharding import PartitionSpec as P

D = 384
HEADS = 6
HEAD_DIM = 64
FF = 1536
PATCH = 1024
TILE = 128
TILES_DEV = 16
SLOTS = 24
PEERS = 32
PAIRS = HEADS // 2
CHUNKS = 2
PART = TILE // CHUNKS
PATCH_TILES = PATCH // TILE
UNIT_TILES = 4
HALF = PATCH // 2
HID = 256

norm_epsilon = 1e-05
masked_score = -1000000000.0
query_scale = HEAD_DIM ** (-0.5) * 1.4426950408889634
f32 = jnp.float32
bf16 = jnp.bfloat16


def norm_rows(values, gain_row):
    center = values - jnp.mean(values, axis=-1, keepdims=True)
    spread = jnp.mean(center * center, axis=-1, keepdims=True)
    return (center * lax.rsqrt(spread + norm_epsilon) * gain_row).astype(bf16)


def gelu(x):
    return (0.5 * x) * (1.0 + lax.erf(x * 0.5 ** 0.5))


def dot(a, b):
    return jnp.dot(a, b, preferred_element_type=f32)


def dot_t(a, b):
    return lax.dot_general(a, b, (((1,), (1,)), ((), ())), preferred_element_type=f32)


def whole(shape):
    zeros = (0,) * len(shape)
    return pl.BlockSpec(shape, lambda *_: zeros)


def layer_of(shape, layer):
    zeros = (0,) * len(shape)
    return pl.BlockSpec((None, *shape), lambda *_: (layer, *zeros))


def qkv_rows(norms, w_ref, store):
    normed = norms[0]()
    for i in range(len(norms)):
        later = norms[i + 1]() if i + 1 < len(norms) else None
        store(i, dot(normed, w_ref[...]))
        normed = later


def qkv_own_kernel(x_ref, gains_ref, w_ref, q_ref, k_ref, v_ref):
    spans = [slice(i * HALF, (i + 1) * HALF) for i in range(x_ref.shape[0] // HALF)]
    norms = [lambda s=s: norm_rows(x_ref[s, :].astype(f32), gains_ref[0:1, :]) for s in spans]

    def store(i, out):
        q_ref[spans[i], :] = (out[:, :D] * query_scale).astype(bf16)
        k_ref[spans[i], :] = out[:, D : 2 * D].astype(bf16)
        v_ref[spans[i], :] = out[:, 2 * D :].astype(bf16)

    qkv_rows(norms, w_ref, store)


def qkv_own(points, gains, qkv_weight):
    rows = points.shape[0]
    block = pl.BlockSpec((PATCH, D), lambda i: (i, 0))
    return pl.pallas_call(
        qkv_own_kernel,
        grid=(rows // PATCH,),
        in_specs=[block, whole((4, D)), layer_of((D, 3 * D), 0)],
        out_specs=[block] * 3,
        out_shape=[pltpu.HBM((n, D), bf16) for n in (rows, rows + PATCH, rows + PATCH)],
        name="qkv_own",
    )(points, gains, qkv_weight)


def qkv_halo_kernel(a_ref, b_ref, gains_ref, w_ref, k_in, v_in, k_ref, v_ref):
    norms = [
        lambda r=r: norm_rows(r[...].astype(f32), gains_ref[0:1, :]) for r in (a_ref, b_ref)
    ]

    def store(i, out):
        span = slice(i * HALF, (i + 1) * HALF)
        k_ref[span, :] = out[:, :D].astype(bf16)
        v_ref[span, :] = out[:, D:].astype(bf16)

    qkv_rows(norms, w_ref.at[:, D:], store)


def qkv_halo(before, after, gains, qkv_weight, keys, values):
    last = keys.shape[0] // PATCH - 1
    ext = pltpu.HBM(keys.shape, bf16)
    return pl.pallas_call(
        qkv_halo_kernel,
        grid=(1,),
        in_specs=[
            pl.BlockSpec(memory_space=pltpu.VMEM),
            pl.BlockSpec(memory_space=pltpu.VMEM),
            whole((4, D)),
            layer_of((D, 3 * D), 0),
            pl.BlockSpec(memory_space=pltpu.HBM),
            pl.BlockSpec(memory_space=pltpu.HBM),
        ],
        out_specs=[pl.BlockSpec((PATCH, D), lambda i: (last, 0))] * 2,
        out_shape=[ext, ext],
        input_output_aliases={4: 0, 5: 1},
        compiler_params=pltpu.CompilerParams(vmem_limit_bytes=24 << 20),
        name="qkv_halo",
    )(before, after, gains, qkv_weight, keys, values)


def qkv_owner_kernel(from_ref, part_ref, gains_ref, w_ref, x_ref, q_ref, k_ref, v_ref, normed_ref):
    patches = SLOTS // PATCH_TILES
    shape = (PATCH_TILES, PART, D)

    def prepare(p):
        tiles = []
        for t in range(PATCH_TILES):
            source = from_ref[p * PATCH_TILES + t]
            tile = part_ref[jnp.maximum(source, 0)]
            tiles.append(jnp.where(source >= 0, tile.astype(f32), 0.0))
        rows = jnp.concatenate(tiles, axis=0)
        x_ref[pl.ds(p * PATCH_TILES, PATCH_TILES)] = rows.astype(bf16).reshape(shape)
        return norm_rows(rows, gains_ref[2:3, :])

    normed_ref[0] = prepare(0)

    @pl.loop(0, patches)
    def _(p):
        normed_ref[(p + 1) % 2] = prepare(jnp.minimum(p + 1, patches - 1))
        out = dot(normed_ref[p % 2], w_ref[1])
        tiles = pl.ds(p * PATCH_TILES, PATCH_TILES)
        q_ref[tiles] = (out[:, :D] * query_scale).astype(bf16).reshape(shape)
        k_ref[tiles] = out[:, D : 2 * D].astype(bf16).reshape(shape)
        v_ref[tiles] = out[:, 2 * D :].astype(bf16).reshape(shape)


def qkv_owner(owner_from, part, gains, qkv_weight):
    return pl.pallas_call(
        qkv_owner_kernel,
        grid_spec=pltpu.PrefetchScalarGridSpec(
            num_scalar_prefetch=1,
            grid=(1,),
            in_specs=[pl.BlockSpec(memory_space=pltpu.VMEM)] * 3,
            out_specs=[whole((SLOTS, PART, D))] * 4,
            scratch_shapes=[pltpu.VMEM((2, PATCH_TILES * PART, D), bf16)],
        ),
        out_shape=[pltpu.HBM((SLOTS, PART, D), bf16)] * 4,
        compiler_params=pltpu.CompilerParams(vmem_limit_bytes=24 << 20),
        name="qkv_owner",
    )(owner_from, part, gains, qkv_weight)


def block_kernel(units, masked, layer, pieces, table_ref, x_ref, q_ref, *refs):
    k_refs, refs = refs[:pieces], refs[pieces:]
    v_refs, refs = refs[:pieces], refs[pieces:]
    gains_ref, *sources, out_ref = refs[:5]
    mixed_ref, normed_ref, rising_ref, total_ref, proj_ref, up_ref, down_ref, sems = refs[5:]
    step = pl.program_id(0)
    count = UNIT_TILES * PART
    rows = PATCH // pieces
    lanes = lax.broadcasted_iota(jnp.int32, (1, 128), 1)
    low = lanes < HEAD_DIM
    picks = [low.astype(f32).astype(bf16), (~low).astype(f32).astype(bf16)]
    fetches = [
        pltpu.make_async_copy(source.at[layer], target, sems.at[i])
        for i, (source, target) in enumerate(zip(sources, (proj_ref, up_ref, down_ref)))
    ]

    def attention_parts():
        queries = q_ref[...].reshape(count, D)
        ones = jnp.ones((rows, 128), bf16)
        extra_q = extra_k = None
        if masked:
            base = (step * UNIT_TILES) // PATCH_TILES * PATCH_TILES
            extra_q = jnp.broadcast_to((lanes == 0).astype(f32).astype(bf16), (count, 128))
            marks = []
            for t in range(PATCH_TILES):
                mark = jnp.where(table_ref[base + t] >= 0, 0.0, masked_score)
                marks.append(jnp.full((rows // PATCH_TILES, 128), mark, f32).astype(bf16))
            extra_k = jnp.concatenate(marks, axis=0)

        def scores(h):
            cols = slice(128 * (h // 2), 128 * (h // 2) + 128)
            q = queries[:, cols] * picks[h % 2]
            if masked:
                q = jnp.concatenate([q, extra_q], axis=1)
            out = []
            for k_ref in k_refs:
                k = k_ref[...].reshape(rows, D)[:, cols]
                if masked:
                    k = jnp.concatenate([k, extra_k], axis=1)
                out.append(dot_t(q, k))
            return out

        def soften(parts):
            peak = functools.reduce(
                jnp.maximum, [jnp.max(s, axis=-1, keepdims=True) for s in parts]
            )
            return [jnp.exp2(s - peak).astype(bf16) for s in parts]

        def mix(h, parts):
            cols = slice(128 * (h // 2), 128 * (h // 2) + 128)
            total = None
            for p, v_ref in zip(parts, v_refs):
                v = v_ref[...].reshape(rows, D)[:, cols]
                one = dot(p, jnp.concatenate([v, ones], axis=1))
                total = one if total is None else total + one
            own = (total[:, :128] / total[:, 128:]).astype(bf16) * picks[h % 2]
            if h % 2:
                own = own + mixed_ref[:, cols]
            mixed_ref[:, cols] = own

        return scores, soften, mix

    def join(mixed):
        base = x_ref[...].reshape(count, D).astype(f32)
        inner = (base + dot(mixed, proj_ref[...])).astype(bf16)
        gain = gains_ref[2 * layer + 1 : 2 * layer + 2, :]
        return inner, norm_rows(inner.astype(f32), gain)

    def hidden(normed, j):
        return gelu(dot(normed, up_ref[:, HID * j : HID * (j + 1)])).astype(bf16)

    def down(part, j):
        return dot(part, down_ref[HID * j : HID * (j + 1), :])

    def emit(inner, total):
        outer = (inner.astype(f32) + total).astype(bf16)
        for t in range(UNIT_TILES):
            slot = table_ref[(step - 1) * UNIT_TILES + t]

            @pl.when(slot >= 0)
            def _():
                out_ref[jnp.maximum(slot, 0)] = outer[t * PART : (t + 1) * PART]

    @pl.when(step == 0)
    def _():
        for fetch in fetches:
            fetch.start()
        scores, soften, mix = attention_parts()
        s = scores(0)
        for h in range(HEADS):
            later = scores(h + 1) if h + 1 < HEADS else None
            mix(h, soften(s))
            s = later
        for fetch in fetches:
            fetch.wait()

    @pl.when((step > 0) & (step < units))
    def _():
        mixed = mixed_ref[...]
        scores, soften, mix = attention_parts()
        s = scores(0)
        inner, normed = join(mixed)
        total = None
        for h in range(HEADS):
            later = scores(h + 1) if h + 1 < HEADS else None
            part = hidden(normed, h)
            mix(h, soften(s))
            one = down(part, h)
            total = one if total is None else total + one
            s = later
        emit(inner, total)

    @pl.when(step == units)
    def _():
        inner, normed = join(mixed_ref[...])
        normed_ref[...] = normed
        rising_ref[0] = dot(normed, up_ref[:, :HID])
        total_ref[...] = jnp.zeros_like(total_ref)

        @pl.loop(0, FF // HID)
        def _(j):
            after = pl.multiple_of(jnp.minimum(j + 1, FF // HID - 1) * HID, HID)
            rising_ref[(j + 1) % 2] = dot(normed_ref[...], up_ref[:, pl.ds(after, HID)])
            part = gelu(rising_ref[j % 2]).astype(bf16)
            total_ref[...] += dot(part, down_ref[pl.ds(pl.multiple_of(j * HID, HID), HID), :])

        emit(inner, total_ref[...])


def block(name, table, x, q, keys, values, specs, units, masked, layer, weights):
    gains, *matrices = weights
    pieces = len(keys)
    count = UNIT_TILES * PART
    return pl.pallas_call(
        functools.partial(block_kernel, units, masked, layer, pieces),
        grid_spec=pltpu.PrefetchScalarGridSpec(
            num_scalar_prefetch=1,
            grid=(units + 1,),
            in_specs=specs
            + [whole((4, D))]
            + [pl.BlockSpec(memory_space=pl.ANY)] * len(matrices),
            out_specs=whole((PEERS, PART, D)),
            scratch_shapes=[
                pltpu.VMEM((count, D), bf16),
                pltpu.VMEM((count, D), bf16),
                pltpu.VMEM((2, count, HID), f32),
                pltpu.VMEM((count, D), f32),
                pltpu.VMEM((D, D), bf16),
                pltpu.VMEM((D, FF), bf16),
                pltpu.VMEM((FF, D), bf16),
                pltpu.SemaphoreType.DMA((len(matrices),)),
            ],
        ),
        out_shape=jax.ShapeDtypeStruct((PEERS, PART, D), bf16),
        name=name,
    )(table, x, q, *keys, *values, gains, *matrices)


def now(i, units):
    return jnp.minimum(i, units - 1)


def prior(i):
    return jnp.maximum(i - 1, 0)


def block_a(chunk, table, x, q, keys, values, weights):
    units = TILES_DEV // UNIT_TILES
    shape = (UNIT_TILES, PART, D)
    own = TILES_DEV * TILE // HALF

    def first(i, *_):
        patch = (now(i, units) + 1) // 2
        return patch + patch // 2, 0

    def second(i, *_):
        patch = (now(i, units) + 1) // 2
        return jnp.where(patch == 1, 2, own + patch // 2), 0

    key_specs = [pl.BlockSpec((HALF, D), first), pl.BlockSpec((HALF, D), second)]
    specs = [
        pl.BlockSpec(shape, lambda i, *_: (prior(i), chunk, 0)),
        pl.BlockSpec(shape, lambda i, *_: (now(i, units), chunk, 0)),
        *key_specs,
        *key_specs,
    ]
    return block(
        "block_a", table, x, q, [keys] * 2, [values] * 2, specs, units, False, 0, weights
    )


def block_b(table, x, q, keys, values, weights):
    units = SLOTS // UNIT_TILES
    shape = (UNIT_TILES, PART, D)
    patch = (PATCH_TILES, PART, D)
    key_spec = pl.BlockSpec(patch, lambda i, *_: (now(i, units) // 2, 0, 0))
    specs = [
        pl.BlockSpec(shape, lambda i, *_: (prior(i), 0, 0)),
        pl.BlockSpec(shape, lambda i, *_: (now(i, units), 0, 0)),
    ] + [key_spec] * (2 * CHUNKS)
    return block("block_b", table, x, q, keys, values, specs, units, True, 1, weights)


def home_kernel(table_ref, *refs):
    parts, out_ref = refs[:CHUNKS], refs[CHUNKS]
    for t in range(TILES_DEV):
        for c, part_ref in enumerate(parts):
            out_ref[t, c * PART : (c + 1) * PART] = part_ref[table_ref[t]]


def home(table, parts):
    return pl.pallas_call(
        home_kernel,
        grid_spec=pltpu.PrefetchScalarGridSpec(
            num_scalar_prefetch=1,
            grid=(1,),
            in_specs=[pl.BlockSpec(memory_space=pltpu.VMEM)] * CHUNKS,
            out_specs=whole((TILES_DEV, TILE, D)),
        ),
        out_shape=jax.ShapeDtypeStruct((TILES_DEV, TILE, D), bf16),
        compiler_params=pltpu.CompilerParams(vmem_limit_bytes=12 << 20),
        name="home",
    )(table, *parts)


def exchange(part):
    return lax.all_to_all(part, "chain", split_axis=0, concat_axis=0, tiled=True)


def body(
    points, norm_gains, qkv_weight, proj_weight, up_weight, down_weight, dest_slot, owner_from
):
    rows = points.shape[0]
    axes = ("chain", "group")
    ring = lax.axis_size(axes)
    before = lax.ppermute(points[rows - HALF :], axes, [(i, (i + 1) % ring) for i in range(ring)])
    after = lax.ppermute(points[:HALF], axes, [((i + 1) % ring, i) for i in range(ring)])
    weights = (norm_gains, proj_weight, up_weight, down_weight)
    q, keys, values = qkv_own(points, norm_gains, qkv_weight)
    keys, values = qkv_halo(before, after, norm_gains, qkv_weight, keys, values)
    tiled = (TILES_DEV, TILE, D)
    x, q = points.reshape(tiled), q.reshape(tiled)
    sent = []
    for chunk in range(CHUNKS):
        packed = block_a(chunk, dest_slot, x, q, keys, values, weights)
        sent.append(exchange(packed))
    owned = [qkv_owner(owner_from, part, norm_gains, qkv_weight) for part in sent]
    owner_keys = [one[2] for one in owned]
    owner_values = [one[3] for one in owned]
    returned = []
    for chunk in range(CHUNKS):
        done = block_b(
            owner_from, owned[chunk][0], owned[chunk][1], owner_keys, owner_values, weights
        )
        returned.append(exchange(done))
    return home(dest_slot, returned).reshape(rows, D)


def solution(mesh):
    placed = (
        P(("chain", "group"), None),
        P(),
        P(),
        P(),
        P(),
        P(),
        P(("chain", "group")),
        P(("chain", "group")),
    )
    return jax.shard_map(
        body, mesh=mesh, in_specs=placed, out_specs=P(("chain", "group"), None), check_vma=False
    )
```

```python
import functools

import jax
import jax.numpy as jnp
from jax import lax
from jax.experimental import pallas as pl
from jax.experimental.pallas import tpu as pltpu
from jax.sharding import PartitionSpec as P

D = 384
HEADS = 6
HEAD_DIM = 64
FF = 1536
PATCH = 1024
TILE = 128
TILES_DEV = 16
SLOTS = 24
PEERS = 32
PAIRS = HEADS // 2
CHUNKS = 2
PART = TILE // CHUNKS
PATCH_TILES = PATCH // TILE
UNIT_TILES = 4
HALF = PATCH // 2
HID = 256

norm_epsilon = 1e-05
masked_score = -1000000000.0
query_scale = HEAD_DIM ** (-0.5) * 1.4426950408889634
f32 = jnp.float32
bf16 = jnp.bfloat16


def norm_rows(values, gain_row):
    center = values - jnp.mean(values, axis=-1, keepdims=True)
    spread = jnp.mean(center * center, axis=-1, keepdims=True)
    return (center * lax.rsqrt(spread + norm_epsilon) * gain_row).astype(bf16)


def gelu(x):
    return (0.5 * x) * (1.0 + lax.erf(x * 0.5 ** 0.5))


def dot(a, b):
    return jnp.dot(a, b, preferred_element_type=f32)


def dot_t(a, b):
    return lax.dot_general(a, b, (((1,), (1,)), ((), ())), preferred_element_type=f32)


def whole(shape):
    zeros = (0,) * len(shape)
    return pl.BlockSpec(shape, lambda *_: zeros)


def layer_of(shape, layer):
    zeros = (0,) * len(shape)
    return pl.BlockSpec((None, *shape), lambda *_: (layer, *zeros))


def qkv_rows(norms, w_ref, store):
    normed = norms[0]()
    for i in range(len(norms)):
        later = norms[i + 1]() if i + 1 < len(norms) else None
        store(i, dot(normed, w_ref[...]))
        normed = later


def now(i, units):
    return jnp.minimum(i, units - 1)


def prior(i):
    return jnp.maximum(i - 1, 0)


def qkv_own_kernel(x_ref, gains_ref, w_ref, q_ref, k_ref, v_ref):
    spans = [slice(i * HALF, (i + 1) * HALF) for i in range(x_ref.shape[0] // HALF)]
    norms = [lambda s=s: norm_rows(x_ref[s, :].astype(f32), gains_ref[0:1, :]) for s in spans]

    def store(i, out):
        q_ref[spans[i], :] = (out[:, :D] * query_scale).astype(bf16)
        k_ref[spans[i], :] = out[:, D : 2 * D].astype(bf16)
        v_ref[spans[i], :] = out[:, 2 * D :].astype(bf16)

    qkv_rows(norms, w_ref, store)


def qkv_own(points, gains, qkv_weight):
    rows = points.shape[0]
    block = pl.BlockSpec((PATCH, D), lambda i: (i, 0))
    return pl.pallas_call(
        qkv_own_kernel,
        grid=(rows // PATCH,),
        in_specs=[block, whole((4, D)), layer_of((D, 3 * D), 0)],
        out_specs=[block] * 3,
        out_shape=[pltpu.HBM((n, D), bf16) for n in (rows, rows + PATCH, rows + PATCH)],
        name="qkv_own",
    )(points, gains, qkv_weight)


def qkv_halo_kernel(a_ref, b_ref, gains_ref, w_ref, k_in, v_in, k_ref, v_ref):
    norms = [
        lambda r=r: norm_rows(r[...].astype(f32), gains_ref[0:1, :]) for r in (a_ref, b_ref)
    ]

    def store(i, out):
        span = slice(i * HALF, (i + 1) * HALF)
        k_ref[span, :] = out[:, :D].astype(bf16)
        v_ref[span, :] = out[:, D:].astype(bf16)

    qkv_rows(norms, w_ref.at[:, D:], store)


def qkv_halo(before, after, gains, qkv_weight, keys, values):
    last = keys.shape[0] // PATCH - 1
    ext = pltpu.HBM(keys.shape, bf16)
    return pl.pallas_call(
        qkv_halo_kernel,
        grid=(1,),
        in_specs=[
            pl.BlockSpec(memory_space=pltpu.VMEM),
            pl.BlockSpec(memory_space=pltpu.VMEM),
            whole((4, D)),
            layer_of((D, 3 * D), 0),
            pl.BlockSpec(memory_space=pltpu.HBM),
            pl.BlockSpec(memory_space=pltpu.HBM),
        ],
        out_specs=[pl.BlockSpec((PATCH, D), lambda i: (last, 0))] * 2,
        out_shape=[ext, ext],
        input_output_aliases={4: 0, 5: 1},
        compiler_params=pltpu.CompilerParams(vmem_limit_bytes=24 << 20),
        name="qkv_halo",
    )(before, after, gains, qkv_weight, keys, values)


def qkv_owner_kernel(from_ref, part_ref, gains_ref, w_ref, x_ref, q_ref, k_ref, v_ref):
    patch = pl.program_id(0)
    shape = (PATCH_TILES, PART, D)
    tiles = []
    for t in range(PATCH_TILES):
        source = from_ref[patch * PATCH_TILES + t]
        tile = part_ref[jnp.maximum(source, 0)]
        tiles.append(jnp.where(source >= 0, tile.astype(f32), 0.0))
    rows = jnp.concatenate(tiles, axis=0)
    x_ref[...] = rows.astype(bf16).reshape(shape)
    out = dot(norm_rows(rows, gains_ref[2:3, :]), w_ref[...])
    q_ref[...] = (out[:, :D] * query_scale).astype(bf16).reshape(shape)
    k_ref[...] = out[:, D : 2 * D].astype(bf16).reshape(shape)
    v_ref[...] = out[:, 2 * D :].astype(bf16).reshape(shape)


def qkv_owner(owner_from, part, gains, qkv_weight):
    block = pl.BlockSpec((PATCH_TILES, PART, D), lambda i, *_: (i, 0, 0))
    return pl.pallas_call(
        qkv_owner_kernel,
        grid_spec=pltpu.PrefetchScalarGridSpec(
            num_scalar_prefetch=1,
            grid=(SLOTS // PATCH_TILES,),
            in_specs=[
                pl.BlockSpec(memory_space=pltpu.VMEM),
                whole((4, D)),
                layer_of((D, 3 * D), 1),
            ],
            out_specs=[block] * 4,
        ),
        out_shape=[pltpu.HBM((SLOTS, PART, D), bf16)] * 4,
        compiler_params=pltpu.CompilerParams(vmem_limit_bytes=24 << 20),
        name="qkv_owner",
    )(owner_from, part, gains, qkv_weight)


def block_kernel(units, masked, layer, pieces, table_ref, x_ref, q_ref, *refs):
    k_refs, refs = refs[:pieces], refs[pieces:]
    v_refs, refs = refs[:pieces], refs[pieces:]
    gains_ref, *sources, out_ref, mixed_ref, proj_ref, up_ref, down_ref, sems = refs
    step = pl.program_id(0)
    count = UNIT_TILES * PART
    rows = PATCH // pieces
    lanes = lax.broadcasted_iota(jnp.int32, (1, 128), 1)
    low = lanes < HEAD_DIM
    picks = [low.astype(f32).astype(bf16), (~low).astype(f32).astype(bf16)]
    fetches = [
        pltpu.make_async_copy(source.at[layer], target, sems.at[i])
        for i, (source, target) in enumerate(zip(sources, (proj_ref, up_ref, down_ref)))
    ]

    def attention_parts():
        queries = q_ref[...].reshape(count, D)
        ones = jnp.ones((rows, 128), bf16)
        extra_q = extra_k = None
        if masked:
            base = (step * UNIT_TILES) // PATCH_TILES * PATCH_TILES
            extra_q = jnp.broadcast_to((lanes == 0).astype(f32).astype(bf16), (count, 128))
            marks = []
            for t in range(PATCH_TILES):
                mark = jnp.where(table_ref[base + t] >= 0, 0.0, masked_score)
                marks.append(jnp.full((rows // PATCH_TILES, 128), mark, f32).astype(bf16))
            extra_k = jnp.concatenate(marks, axis=0)

        def scores(h):
            cols = slice(128 * (h // 2), 128 * (h // 2) + 128)
            q = queries[:, cols] * picks[h % 2]
            if masked:
                q = jnp.concatenate([q, extra_q], axis=1)
            out = []
            for k_ref in k_refs:
                k = k_ref[...].reshape(rows, D)[:, cols]
                if masked:
                    k = jnp.concatenate([k, extra_k], axis=1)
                out.append(dot_t(q, k))
            return out

        def soften(parts):
            peak = functools.reduce(
                jnp.maximum, [jnp.max(s, axis=-1, keepdims=True) for s in parts]
            )
            return [jnp.exp2(s - peak).astype(bf16) for s in parts]

        def mix(h, parts):
            cols = slice(128 * (h // 2), 128 * (h // 2) + 128)
            total = None
            for p, v_ref in zip(parts, v_refs):
                v = v_ref[...].reshape(rows, D)[:, cols]
                one = dot(p, jnp.concatenate([v, ones], axis=1))
                total = one if total is None else total + one
            own = (total[:, :128] / total[:, 128:]).astype(bf16) * picks[h % 2]
            if h % 2:
                own = own + mixed_ref[:, cols]
            mixed_ref[:, cols] = own

        return scores, soften, mix

    def attention_steps():
        scores, soften, mix = attention_parts()
        s = scores(0)
        yield
        for h in range(HEADS):
            later = None
            if h + 1 < HEADS:
                later = scores(h + 1)
                yield
            weights = soften(s)
            yield
            mix(h, weights)
            yield
            s = later

    def forward_steps(mixed, result):
        base = x_ref[...].reshape(count, D).astype(f32)
        gain = gains_ref[2 * layer + 1 : 2 * layer + 2, :]
        inner = (base + dot(mixed, proj_ref[...])).astype(bf16)
        yield
        normed = norm_rows(inner.astype(f32), gain)
        yield

        def rise(j):
            return dot(normed, up_ref[:, HID * j : HID * (j + 1)])

        total = None
        up = rise(0)
        yield
        for j in range(FF // HID):
            later = None
            if j + 1 < FF // HID:
                later = rise(j + 1)
                yield
            one = dot(gelu(up).astype(bf16), down_ref[HID * j : HID * (j + 1), :])
            total = one if total is None else total + one
            yield
            up = later
        result.extend((inner, total))

    def weave(first, *others, delay=0):
        done = object()
        streams = [first]
        for _ in range(delay):
            next(first)
        streams = [first, *others]
        while streams:
            for stream in list(streams):
                if next(stream, done) is done:
                    streams.remove(stream)

    def emit(inner, total):
        outer = (inner.astype(f32) + total).astype(bf16)
        for t in range(UNIT_TILES):
            slot = table_ref[(step - 1) * UNIT_TILES + t]

            @pl.when(slot >= 0)
            def _():
                out_ref[jnp.maximum(slot, 0)] = outer[t * PART : (t + 1) * PART]

    @pl.when(step == 0)
    def _():
        for fetch in fetches:
            fetch.start()
        weave(attention_steps())
        for fetch in fetches:
            fetch.wait()

    @pl.when((step > 0) & (step < units))
    def _():
        result = []
        weave(attention_steps(), forward_steps(mixed_ref[...], result), delay=0)
        emit(*result)

    @pl.when(step == units)
    def _():
        result = []
        weave(forward_steps(mixed_ref[...], result))
        emit(*result)


def block(name, table, x, q, keys, values, specs, units, masked, layer, weights):
    gains, *matrices = weights
    pieces = len(keys)
    count = UNIT_TILES * PART
    return pl.pallas_call(
        functools.partial(block_kernel, units, masked, layer, pieces),
        grid_spec=pltpu.PrefetchScalarGridSpec(
            num_scalar_prefetch=1,
            grid=(units + 1,),
            in_specs=specs
            + [whole((4, D))]
            + [pl.BlockSpec(memory_space=pl.ANY)] * len(matrices),
            out_specs=whole((PEERS, PART, D)),
            scratch_shapes=[
                pltpu.VMEM((count, D), bf16),
                pltpu.VMEM((D, D), bf16),
                pltpu.VMEM((D, FF), bf16),
                pltpu.VMEM((FF, D), bf16),
                pltpu.SemaphoreType.DMA((len(matrices),)),
            ],
        ),
        out_shape=jax.ShapeDtypeStruct((PEERS, PART, D), bf16),
        name=name,
    )(table, x, q, *keys, *values, gains, *matrices)


def block_a(chunk, table, x, q, keys, values, weights):
    units = TILES_DEV // UNIT_TILES
    shape = (UNIT_TILES, PART, D)
    own = TILES_DEV * TILE // HALF

    def first(i, *_):
        patch = (now(i, units) + 1) // 2
        return patch + patch // 2, 0

    def second(i, *_):
        patch = (now(i, units) + 1) // 2
        return jnp.where(patch == 1, 2, own + patch // 2), 0

    key_specs = [pl.BlockSpec((HALF, D), first), pl.BlockSpec((HALF, D), second)]
    specs = [
        pl.BlockSpec(shape, lambda i, *_: (prior(i), chunk, 0)),
        pl.BlockSpec(shape, lambda i, *_: (now(i, units), chunk, 0)),
        *key_specs,
        *key_specs,
    ]
    return block(
        "block_a", table, x, q, [keys] * 2, [values] * 2, specs, units, False, 0, weights
    )


def block_b(table, x, q, keys, values, weights):
    units = SLOTS // UNIT_TILES
    shape = (UNIT_TILES, PART, D)
    patch = (PATCH_TILES, PART, D)
    key_spec = pl.BlockSpec(patch, lambda i, *_: (now(i, units) // 2, 0, 0))
    specs = [
        pl.BlockSpec(shape, lambda i, *_: (prior(i), 0, 0)),
        pl.BlockSpec(shape, lambda i, *_: (now(i, units), 0, 0)),
    ] + [key_spec] * (2 * CHUNKS)
    return block("block_b", table, x, q, keys, values, specs, units, True, 1, weights)


def home_kernel(table_ref, *refs):
    parts, out_ref = refs[:CHUNKS], refs[CHUNKS]
    @pl.loop(0, TILES_DEV)
    def _(t):
        for c, part_ref in enumerate(parts):
            out_ref[t, c * PART : (c + 1) * PART] = part_ref[table_ref[t]]


def home(table, parts):
    return pl.pallas_call(
        home_kernel,
        grid_spec=pltpu.PrefetchScalarGridSpec(
            num_scalar_prefetch=1,
            grid=(1,),
            in_specs=[pl.BlockSpec(memory_space=pltpu.VMEM)] * CHUNKS,
            out_specs=whole((TILES_DEV, TILE, D)),
        ),
        out_shape=jax.ShapeDtypeStruct((TILES_DEV, TILE, D), bf16),
        compiler_params=pltpu.CompilerParams(vmem_limit_bytes=12 << 20),
        name="home",
    )(table, *parts)


def exchange(part):
    return lax.all_to_all(part, "chain", split_axis=0, concat_axis=0, tiled=True)


def body(
    points, norm_gains, qkv_weight, proj_weight, up_weight, down_weight, dest_slot, owner_from
):
    rows = points.shape[0]
    axes = ("chain", "group")
    ring = lax.axis_size(axes)
    before = lax.ppermute(points[rows - HALF :], axes, [(i, (i + 1) % ring) for i in range(ring)])
    after = lax.ppermute(points[:HALF], axes, [((i + 1) % ring, i) for i in range(ring)])
    weights = (norm_gains, proj_weight, up_weight, down_weight)
    q, keys, values = qkv_own(points, norm_gains, qkv_weight)
    keys, values = qkv_halo(before, after, norm_gains, qkv_weight, keys, values)
    tiled = (TILES_DEV, TILE, D)
    x, q = points.reshape(tiled), q.reshape(tiled)
    sent = []
    for chunk in range(CHUNKS):
        packed = block_a(chunk, dest_slot, x, q, keys, values, weights)
        sent.append(exchange(packed))
    owned = [qkv_owner(owner_from, part, norm_gains, qkv_weight) for part in sent]
    owner_keys = [one[2] for one in owned]
    owner_values = [one[3] for one in owned]
    returned = []
    for chunk in range(CHUNKS):
        done = block_b(
            owner_from, owned[chunk][0], owned[chunk][1], owner_keys, owner_values, weights
        )
        returned.append(exchange(done))
    return home(dest_slot, returned).reshape(rows, D)


def solution(mesh):
    placed = (
        P(("chain", "group"), None),
        P(),
        P(),
        P(),
        P(),
        P(),
        P(("chain", "group")),
        P(("chain", "group")),
    )
    return jax.shard_map(
        body, mesh=mesh, in_specs=placed, out_specs=P(("chain", "group"), None), check_vma=False
    )
```

```python
import functools

import jax
import jax.numpy as jnp
from jax import lax
from jax.experimental import pallas as pl
from jax.experimental.pallas import tpu as pltpu
from jax.sharding import PartitionSpec as P

D = 384
HEADS = 6
HEAD_DIM = 64
FF = 1536
PATCH = 1024
TILE = 128
TILES_DEV = 16
SLOTS = 24
PEERS = 32
PAIRS = HEADS // 2
CHUNKS = 2
PART = TILE // CHUNKS
PATCH_TILES = PATCH // TILE
UNIT_TILES = 4
HALF = PATCH // 2
HID = 256

norm_epsilon = 1e-05
masked_score = -1000000000.0
query_scale = HEAD_DIM ** (-0.5) * 1.4426950408889634
f32 = jnp.float32
bf16 = jnp.bfloat16


def norm_rows(values, gain_row):
    center = values - jnp.mean(values, axis=-1, keepdims=True)
    spread = jnp.mean(center * center, axis=-1, keepdims=True)
    return (center * lax.rsqrt(spread + norm_epsilon) * gain_row).astype(bf16)


def gelu(x):
    return (0.5 * x) * (1.0 + lax.erf(x * 0.5 ** 0.5))


def dot(a, b):
    return jnp.dot(a, b, preferred_element_type=f32)


def dot_t(a, b):
    return lax.dot_general(a, b, (((1,), (1,)), ((), ())), preferred_element_type=f32)


def whole(shape):
    zeros = (0,) * len(shape)
    return pl.BlockSpec(shape, lambda *_: zeros)


def layer_of(shape, layer):
    zeros = (0,) * len(shape)
    return pl.BlockSpec((None, *shape), lambda *_: (layer, *zeros))


def qkv_rows(norms, w_ref, store):
    normed = norms[0]()
    for i in range(len(norms)):
        later = norms[i + 1]() if i + 1 < len(norms) else None
        store(i, dot(normed, w_ref[...]))
        normed = later


def now(i, units):
    return jnp.minimum(i, units - 1)


def prior(i):
    return jnp.maximum(i - 1, 0)


def qkv_own_kernel(x_ref, gains_ref, w_ref, q_ref, k_ref, v_ref):
    spans = [slice(i * HALF, (i + 1) * HALF) for i in range(x_ref.shape[0] // HALF)]
    norms = [lambda s=s: norm_rows(x_ref[s, :].astype(f32), gains_ref[0:1, :]) for s in spans]

    def store(i, out):
        q_ref[spans[i], :] = (out[:, :D] * query_scale).astype(bf16)
        k_ref[spans[i], :] = out[:, D : 2 * D].astype(bf16)
        v_ref[spans[i], :] = out[:, 2 * D :].astype(bf16)

    qkv_rows(norms, w_ref, store)


def qkv_own(points, gains, qkv_weight):
    rows = points.shape[0]
    block = pl.BlockSpec((PATCH, D), lambda i: (i, 0))
    return pl.pallas_call(
        qkv_own_kernel,
        grid=(rows // PATCH,),
        in_specs=[block, whole((4, D)), layer_of((D, 3 * D), 0)],
        out_specs=[block] * 3,
        out_shape=[pltpu.HBM((n, D), bf16) for n in (rows, rows + PATCH, rows + PATCH)],
        name="qkv_own",
    )(points, gains, qkv_weight)


def qkv_halo_kernel(a_ref, b_ref, gains_ref, w_ref, k_in, v_in, after_in, k_ref, v_ref):
    norms = [
        lambda r=r: norm_rows(r[...].astype(f32), gains_ref[0:1, :]) for r in (a_ref, b_ref)
    ]

    def store(i, out):
        span = slice(i * HALF, (i + 1) * HALF)
        k_ref[span, :] = out[:, :D].astype(bf16)
        v_ref[span, :] = out[:, D:].astype(bf16)

    qkv_rows(norms, w_ref.at[:, D:], store)


def qkv_halo(before, after, gains, qkv_weight, keys, values, earlier):
    last = keys.shape[0] // PATCH - 1
    ext = pltpu.HBM(keys.shape, bf16)
    return pl.pallas_call(
        qkv_halo_kernel,
        grid=(1,),
        in_specs=[
            pl.BlockSpec(memory_space=pltpu.VMEM),
            pl.BlockSpec(memory_space=pltpu.VMEM),
            whole((4, D)),
            layer_of((D, 3 * D), 0),
            pl.BlockSpec(memory_space=pltpu.HBM),
            pl.BlockSpec(memory_space=pltpu.HBM),
            pl.BlockSpec(memory_space=pl.ANY),
        ],
        out_specs=[pl.BlockSpec((PATCH, D), lambda i: (last, 0))] * 2,
        out_shape=[ext, ext],
        input_output_aliases={4: 0, 5: 1},
        compiler_params=pltpu.CompilerParams(vmem_limit_bytes=24 << 20),
        name="qkv_halo",
    )(before, after, gains, qkv_weight, keys, values, earlier)


def qkv_owner_kernel(from_ref, part_ref, gains_ref, w_ref, x_ref, q_ref, k_ref, v_ref):
    patch = pl.program_id(0)
    shape = (PATCH_TILES, PART, D)
    tiles = []
    for t in range(PATCH_TILES):
        source = from_ref[patch * PATCH_TILES + t]
        tile = part_ref[jnp.maximum(source, 0)]
        tiles.append(jnp.where(source >= 0, tile.astype(f32), 0.0))
    rows = jnp.concatenate(tiles, axis=0)
    x_ref[...] = rows.astype(bf16).reshape(shape)
    out = dot(norm_rows(rows, gains_ref[2:3, :]), w_ref[...])
    q_ref[...] = (out[:, :D] * query_scale).astype(bf16).reshape(shape)
    k_ref[...] = out[:, D : 2 * D].astype(bf16).reshape(shape)
    v_ref[...] = out[:, 2 * D :].astype(bf16).reshape(shape)


def qkv_owner(owner_from, part, gains, qkv_weight):
    block = pl.BlockSpec((PATCH_TILES, PART, D), lambda i, *_: (i, 0, 0))
    return pl.pallas_call(
        qkv_owner_kernel,
        grid_spec=pltpu.PrefetchScalarGridSpec(
            num_scalar_prefetch=1,
            grid=(SLOTS // PATCH_TILES,),
            in_specs=[
                pl.BlockSpec(memory_space=pltpu.VMEM),
                whole((4, D)),
                layer_of((D, 3 * D), 1),
            ],
            out_specs=[block] * 4,
        ),
        out_shape=[pltpu.HBM((SLOTS, PART, D), bf16)] * 4,
        compiler_params=pltpu.CompilerParams(vmem_limit_bytes=24 << 20),
        name="qkv_owner",
    )(owner_from, part, gains, qkv_weight)


def forward_rows(inner, normed, up_ref, down_ref):
    def rise(j):
        return dot(normed, up_ref[:, HID * j : HID * (j + 1)])

    total = None
    up = rise(0)
    for j in range(FF // HID):
        later = rise(j + 1) if j + 1 < FF // HID else None
        one = dot(gelu(up).astype(bf16), down_ref[HID * j : HID * (j + 1), :])
        total = one if total is None else total + one
        up = later
    return (inner.astype(f32) + total).astype(bf16)


def forward_owner_kernel(
    from_ref, part_ref, gains_ref, up_ref, down_ref, w_ref, x_ref, q_ref, k_ref, v_ref
):
    unit = pl.program_id(0)
    shape = (UNIT_TILES, PART, D)
    tiles = []
    for t in range(UNIT_TILES):
        source = from_ref[unit * UNIT_TILES + t]
        tile = part_ref[jnp.maximum(source, 0)]
        tiles.append(jnp.where(source >= 0, tile.astype(f32), 0.0))
    rows = jnp.concatenate(tiles, axis=0)
    outer = forward_rows(rows, norm_rows(rows, gains_ref[1:2, :]), up_ref, down_ref)
    x_ref[...] = outer.reshape(shape)
    out = dot(norm_rows(outer.astype(f32), gains_ref[2:3, :]), w_ref[...])
    q_ref[...] = (out[:, :D] * query_scale).astype(bf16).reshape(shape)
    k_ref[...] = out[:, D : 2 * D].astype(bf16).reshape(shape)
    v_ref[...] = out[:, 2 * D :].astype(bf16).reshape(shape)


def forward_owner(owner_from, part, weights, qkv_weight):
    gains, _, up_weight, down_weight = weights
    block = pl.BlockSpec((UNIT_TILES, PART, D), lambda i, *_: (i, 0, 0))
    return pl.pallas_call(
        forward_owner_kernel,
        grid_spec=pltpu.PrefetchScalarGridSpec(
            num_scalar_prefetch=1,
            grid=(SLOTS // UNIT_TILES,),
            in_specs=[
                pl.BlockSpec(memory_space=pltpu.VMEM),
                whole((4, D)),
                layer_of((D, FF), 0),
                layer_of((FF, D), 0),
                layer_of((D, 3 * D), 1),
            ],
            out_specs=[block] * 4,
        ),
        out_shape=[pltpu.HBM((SLOTS, PART, D), bf16)] * 4,
        compiler_params=pltpu.CompilerParams(vmem_limit_bytes=30 << 20),
        name="forward_owner",
    )(owner_from, part, gains, up_weight, down_weight, qkv_weight)


def attention_parts(masked, first_tile, table_ref, q_ref, k_refs, v_refs, mixed_ref):
    pieces = len(k_refs)
    count = UNIT_TILES * PART
    rows = PATCH // pieces
    lanes = lax.broadcasted_iota(jnp.int32, (1, 128), 1)
    low = lanes < HEAD_DIM
    picks = [low.astype(f32).astype(bf16), (~low).astype(f32).astype(bf16)]
    queries = q_ref[...].reshape(count, D)
    ones = jnp.ones((rows, 128), bf16)
    extra_q = extra_k = None
    if masked:
        base = first_tile // PATCH_TILES * PATCH_TILES
        extra_q = jnp.broadcast_to((lanes == 0).astype(f32).astype(bf16), (count, 128))
        marks = []
        for t in range(PATCH_TILES):
            mark = jnp.where(table_ref[base + t] >= 0, 0.0, masked_score)
            marks.append(jnp.full((rows // PATCH_TILES, 128), mark, f32).astype(bf16))
        extra_k = jnp.concatenate(marks, axis=0)

    def scores(h):
        cols = slice(128 * (h // 2), 128 * (h // 2) + 128)
        q = queries[:, cols] * picks[h % 2]
        if masked:
            q = jnp.concatenate([q, extra_q], axis=1)
        out = []
        for k_ref in k_refs:
            k = k_ref[...].reshape(rows, D)[:, cols]
            if masked:
                k = jnp.concatenate([k, extra_k], axis=1)
            out.append(dot_t(q, k))
        return out

    def soften(parts):
        peak = functools.reduce(
            jnp.maximum, [jnp.max(s, axis=-1, keepdims=True) for s in parts]
        )
        return [jnp.exp2(s - peak).astype(bf16) for s in parts]

    def mix(h, parts):
        cols = slice(128 * (h // 2), 128 * (h // 2) + 128)
        total = None
        for p, v_ref in zip(parts, v_refs):
            v = v_ref[...].reshape(rows, D)[:, cols]
            one = dot(p, jnp.concatenate([v, ones], axis=1))
            total = one if total is None else total + one
        own = (total[:, :128] / total[:, 128:]).astype(bf16) * picks[h % 2]
        if h % 2:
            own = own + mixed_ref[:, cols]
        mixed_ref[:, cols] = own

    return scores, soften, mix


def block_kernel(units, masked, layer, pieces, table_ref, x_ref, q_ref, *refs):
    k_refs, refs = refs[:pieces], refs[pieces:]
    v_refs, refs = refs[:pieces], refs[pieces:]
    gains_ref, *sources, out_ref, mixed_ref, proj_ref, up_ref, down_ref, sems = refs
    step = pl.program_id(0)
    count = UNIT_TILES * PART
    fetches = [
        pltpu.make_async_copy(source.at[layer], target, sems.at[i])
        for i, (source, target) in enumerate(zip(sources, (proj_ref, up_ref, down_ref)))
    ]

    def attention_steps():
        scores, soften, mix = attention_parts(
            masked, step * UNIT_TILES, table_ref, q_ref, k_refs, v_refs, mixed_ref
        )
        s = scores(0)
        yield
        for h in range(HEADS):
            later = None
            if h + 1 < HEADS:
                later = scores(h + 1)
                yield
            weights = soften(s)
            yield
            mix(h, weights)
            yield
            s = later

    def forward_steps(mixed, result):
        base = x_ref[...].reshape(count, D).astype(f32)
        gain = gains_ref[2 * layer + 1 : 2 * layer + 2, :]
        inner = (base + dot(mixed, proj_ref[...])).astype(bf16)
        yield
        normed = norm_rows(inner.astype(f32), gain)
        yield

        def rise(j):
            return dot(normed, up_ref[:, HID * j : HID * (j + 1)])

        total = None
        up = rise(0)
        yield
        for j in range(FF // HID):
            later = None
            if j + 1 < FF // HID:
                later = rise(j + 1)
                yield
            one = dot(gelu(up).astype(bf16), down_ref[HID * j : HID * (j + 1), :])
            total = one if total is None else total + one
            yield
            up = later
        result.extend((inner, total))

    def weave(first, *others, delay=0):
        done = object()
        streams = [first]
        for _ in range(delay):
            next(first)
        streams = [first, *others]
        while streams:
            for stream in list(streams):
                if next(stream, done) is done:
                    streams.remove(stream)

    def emit(inner, total):
        outer = (inner.astype(f32) + total).astype(bf16)
        for t in range(UNIT_TILES):
            slot = table_ref[(step - 1) * UNIT_TILES + t]

            @pl.when(slot >= 0)
            def _():
                out_ref[jnp.maximum(slot, 0)] = outer[t * PART : (t + 1) * PART]

    @pl.when(step == 0)
    def _():
        for fetch in fetches:
            fetch.start()
        weave(attention_steps())
        for fetch in fetches:
            fetch.wait()

    @pl.when((step > 0) & (step < units))
    def _():
        result = []
        weave(attention_steps(), forward_steps(mixed_ref[...], result), delay=0)
        emit(*result)

    @pl.when(step == units)
    def _():
        result = []
        weave(forward_steps(mixed_ref[...], result))
        emit(*result)


def attention_kernel(place, masked, pieces, table_ref, x_ref, q_ref, *refs):
    k_refs, refs = refs[:pieces], refs[pieces:]
    v_refs, refs = refs[:pieces], refs[pieces:]
    proj_ref, out_ref, mixed_ref, tiles_ref, sems = refs[0], *refs[-4:]
    step = pl.program_id(0)
    units = pl.num_programs(0)
    count = UNIT_TILES * PART
    first_tile = place(step) * UNIT_TILES
    scores, soften, mix = attention_parts(
        masked, first_tile, table_ref, q_ref, k_refs, v_refs, mixed_ref
    )
    s = scores(0)
    for h in range(HEADS):
        later = scores(h + 1) if h + 1 < HEADS else None
        mix(h, soften(s))
        s = later
    base = x_ref[...].reshape(count, D).astype(f32)
    inner = (base + dot(mixed_ref[...], proj_ref[...])).astype(bf16)
    tiles_ref[pl.ds(step * UNIT_TILES, UNIT_TILES)] = inner.reshape(UNIT_TILES, PART, D)

    def copy_of(unit, t, act):
        slot = table_ref[place(unit) * UNIT_TILES + t]

        @pl.when(slot >= 0)
        def _():
            i = unit * UNIT_TILES + t
            act(
                pltpu.make_async_copy(
                    tiles_ref.at[i], out_ref.at[jnp.maximum(slot, 0)], sems.at[i]
                )
            )

    for t in range(UNIT_TILES):
        copy_of(step, t, lambda copy: copy.start())

    @pl.when(step == units - 1)
    def _():
        @pl.loop(0, units)
        def _(unit):
            for t in range(UNIT_TILES):
                copy_of(unit, t, lambda copy: copy.wait())


def attention(name, table, x, q, keys, values, specs, units, place, masked, layer, proj, packed):
    pieces = len(keys)
    args = [table, x, q, *keys, *values, proj]
    specs = [*specs, layer_of((D, D), layer)]
    aliases = {}
    if packed is not None:
        aliases = {len(args): 0}
        args.append(packed)
        specs.append(pl.BlockSpec(memory_space=pltpu.HBM))
    return pl.pallas_call(
        functools.partial(attention_kernel, place, masked, pieces),
        grid_spec=pltpu.PrefetchScalarGridSpec(
            num_scalar_prefetch=1,
            grid=(units,),
            in_specs=specs,
            out_specs=pl.BlockSpec(memory_space=pltpu.HBM),
            scratch_shapes=[
                pltpu.VMEM((UNIT_TILES * PART, D), bf16),
                pltpu.VMEM((units * UNIT_TILES, PART, D), bf16),
                pltpu.SemaphoreType.DMA((units * UNIT_TILES,)),
            ],
        ),
        out_shape=pltpu.HBM((PEERS, PART, D), bf16),
        input_output_aliases=aliases,
        name=name,
    )(*args)


def block(name, table, x, q, keys, values, specs, units, masked, layer, weights):
    gains, *matrices = weights
    pieces = len(keys)
    count = UNIT_TILES * PART
    return pl.pallas_call(
        functools.partial(block_kernel, units, masked, layer, pieces),
        grid_spec=pltpu.PrefetchScalarGridSpec(
            num_scalar_prefetch=1,
            grid=(units + 1,),
            in_specs=specs
            + [whole((4, D))]
            + [pl.BlockSpec(memory_space=pl.ANY)] * len(matrices),
            out_specs=whole((PEERS, PART, D)),
            scratch_shapes=[
                pltpu.VMEM((count, D), bf16),
                pltpu.VMEM((D, D), bf16),
                pltpu.VMEM((D, FF), bf16),
                pltpu.VMEM((FF, D), bf16),
                pltpu.SemaphoreType.DMA((len(matrices),)),
            ],
        ),
        out_shape=jax.ShapeDtypeStruct((PEERS, PART, D), bf16),
        name=name,
    )(table, x, q, *keys, *values, gains, *matrices)


def specs_a(chunk, x_place, place):
    shape = (UNIT_TILES, PART, D)
    own = TILES_DEV * TILE // HALF

    def first(i, *_):
        patch = (place(i) + 1) // 2
        return patch + patch // 2, 0

    def second(i, *_):
        patch = (place(i) + 1) // 2
        return jnp.where(patch == 1, 2, own + patch // 2), 0

    key_specs = [pl.BlockSpec((HALF, D), first), pl.BlockSpec((HALF, D), second)]
    return [
        pl.BlockSpec(shape, lambda i, *_: (x_place(i), chunk, 0)),
        pl.BlockSpec(shape, lambda i, *_: (place(i), chunk, 0)),
        *key_specs,
        *key_specs,
    ]


def attention_a(name, chunk, place, table, x, q, keys, values, proj, packed):
    specs = specs_a(chunk, place, place)
    return attention(
        name, table, x, q, [keys] * 2, [values] * 2, specs, 2, place, False, 0, proj, packed
    )


def block_a(chunk, table, x, q, keys, values, weights):
    units = TILES_DEV // UNIT_TILES
    specs = specs_a(chunk, prior, lambda i: now(i, units))
    return block(
        "block_a", table, x, q, [keys] * 2, [values] * 2, specs, units, False, 0, weights
    )


def specs_b(x_place, place):
    shape = (UNIT_TILES, PART, D)
    patch = (PATCH_TILES, PART, D)
    key_spec = pl.BlockSpec(patch, lambda i, *_: (place(i) // 2, 0, 0))
    return [
        pl.BlockSpec(shape, lambda i, *_: (x_place(i), 0, 0)),
        pl.BlockSpec(shape, lambda i, *_: (place(i), 0, 0)),
    ] + [key_spec] * (2 * CHUNKS)


def attention_b(table, x, q, keys, values, proj):
    units = SLOTS // UNIT_TILES

    def place(i):
        return i

    specs = specs_b(place, place)
    return attention(
        "attention_b", table, x, q, keys, values, specs, units, place, True, 1, proj, None
    )


def block_b(table, x, q, keys, values, weights):
    units = SLOTS // UNIT_TILES
    specs = specs_b(prior, lambda i: now(i, units))
    return block(
        "block_b", table, x, q, keys, values, specs, units, True, 1, weights
    )


def forward_home_kernel(table_ref, part_ref, gains_ref, up_ref, down_ref, out_ref):
    step = pl.program_id(0)
    tiles = [part_ref[table_ref[step * UNIT_TILES + t]] for t in range(UNIT_TILES)]
    rows = jnp.concatenate(tiles, axis=0)
    normed = norm_rows(rows.astype(f32), gains_ref[3:4, :])
    out_ref[...] = forward_rows(rows, normed, up_ref, down_ref).reshape(UNIT_TILES, PART, D)


def forward_home(table, part, weights):
    gains, _, up_weight, down_weight = weights
    return pl.pallas_call(
        forward_home_kernel,
        grid_spec=pltpu.PrefetchScalarGridSpec(
            num_scalar_prefetch=1,
            grid=(TILES_DEV // UNIT_TILES,),
            in_specs=[
                pl.BlockSpec(memory_space=pltpu.VMEM),
                whole((4, D)),
                layer_of((D, FF), 1),
                layer_of((FF, D), 1),
            ],
            out_specs=pl.BlockSpec((UNIT_TILES, PART, D), lambda i, *_: (i, 0, 0)),
        ),
        out_shape=pltpu.HBM((TILES_DEV, TILE, D), bf16),
        compiler_params=pltpu.CompilerParams(vmem_limit_bytes=30 << 20),
        name="forward_home",
    )(table, part, gains, up_weight, down_weight)


def home_kernel(table_ref, part_ref, done_in, out_ref):
    for t in range(TILES_DEV):
        out_ref[t] = part_ref[table_ref[t]]


def home(table, part, done):
    return pl.pallas_call(
        home_kernel,
        grid_spec=pltpu.PrefetchScalarGridSpec(
            num_scalar_prefetch=1,
            grid=(1,),
            in_specs=[
                pl.BlockSpec(memory_space=pltpu.VMEM),
                pl.BlockSpec(memory_space=pltpu.HBM),
            ],
            out_specs=pl.BlockSpec((TILES_DEV, PART, D), lambda i, *_: (0, 1, 0)),
        ),
        out_shape=pltpu.HBM((TILES_DEV, TILE, D), bf16),
        input_output_aliases={2: 0},
        compiler_params=pltpu.CompilerParams(vmem_limit_bytes=12 << 20),
        name="home",
    )(table, part, done)


def exchange(part):
    return lax.all_to_all(part, "chain", split_axis=0, concat_axis=0, tiled=True)


def body(
    points, norm_gains, qkv_weight, proj_weight, up_weight, down_weight, dest_slot, owner_from
):
    rows = points.shape[0]
    axes = ("chain", "group")
    ring = lax.axis_size(axes)
    before = lax.ppermute(points[rows - HALF :], axes, [(i, (i + 1) % ring) for i in range(ring)])
    after = lax.ppermute(points[:HALF], axes, [((i + 1) % ring, i) for i in range(ring)])
    weights = (norm_gains, proj_weight, up_weight, down_weight)
    tiled = (TILES_DEV, TILE, D)
    x = points.reshape(tiled)
    q, keys, values = qkv_own(points, norm_gains, qkv_weight)
    q = q.reshape(tiled)
    packed = attention_a(
        "attention_a_middle", 0, lambda i: i + 1, dest_slot, x, q, keys, values, proj_weight, None
    )
    keys, values = qkv_halo(before, after, norm_gains, qkv_weight, keys, values, packed)
    packed = attention_a(
        "attention_a_edges", 0, lambda i: 3 * i, dest_slot, x, q, keys, values, proj_weight, packed
    )
    early = exchange(packed)
    late = exchange(block_a(1, dest_slot, x, q, keys, values, weights))
    owned = [
        forward_owner(owner_from, early, weights, qkv_weight),
        qkv_owner(owner_from, late, norm_gains, qkv_weight),
    ]
    xs, qs, owner_keys, owner_values = zip(*owned)
    early = exchange(
        attention_b(owner_from, xs[0], qs[0], owner_keys, owner_values, proj_weight)
    )
    late = exchange(block_b(owner_from, xs[1], qs[1], owner_keys, owner_values, weights))
    done = forward_home(dest_slot, early, weights)
    return home(dest_slot, late, done).reshape(rows, D)


def solution(mesh):
    placed = (
        P(("chain", "group"), None),
        P(),
        P(),
        P(),
        P(),
        P(),
        P(("chain", "group")),
        P(("chain", "group")),
    )
    return jax.shard_map(
        body, mesh=mesh, in_specs=placed, out_specs=P(("chain", "group"), None), check_vma=False
    )
```

```python
import functools

import jax
import jax.numpy as jnp
from jax import lax
from jax.experimental import pallas as pl
from jax.experimental.pallas import tpu as pltpu
from jax.sharding import PartitionSpec as P

D = 384
HEADS = 6
HEAD_DIM = 64
FF = 1536
PATCH = 1024
TILE = 128
TILES_DEV = 16
SLOTS = 24
PEERS = 32
PAIRS = HEADS // 2
CHUNKS = 2
PART = TILE // CHUNKS
PATCH_TILES = PATCH // TILE
UNIT_TILES = 4
HALF = PATCH // 2
HID = 256
FULL_VMEM = 65000 << 10

norm_epsilon = 1e-05
masked_score = -1000000000.0
query_scale = HEAD_DIM ** (-0.5) * 1.4426950408889634
f32 = jnp.float32
bf16 = jnp.bfloat16


def norm_rows(values, gain_row):
    center = values - jnp.mean(values, axis=-1, keepdims=True)
    spread = jnp.mean(center * center, axis=-1, keepdims=True)
    return (center * lax.rsqrt(spread + norm_epsilon) * gain_row).astype(bf16)


def gelu(x):
    return (0.5 * x) * (1.0 + lax.erf(x * 0.5 ** 0.5))


def dot(a, b):
    return jnp.dot(a, b, preferred_element_type=f32)


def dot_t(a, b):
    return lax.dot_general(a, b, (((1,), (1,)), ((), ())), preferred_element_type=f32)


def whole(shape):
    zeros = (0,) * len(shape)
    return pl.BlockSpec(shape, lambda *_: zeros)


def layer_of(shape, layer):
    zeros = (0,) * len(shape)
    return pl.BlockSpec((None, *shape), lambda *_: (layer, *zeros))


def qkv_rows(norms, w_ref, store):
    normed = norms[0]()
    for i in range(len(norms)):
        later = norms[i + 1]() if i + 1 < len(norms) else None
        store(i, dot(normed, w_ref[...]))
        normed = later


def now(i, units):
    return jnp.minimum(i, units - 1)


def prior(i):
    return jnp.maximum(i - 1, 0)


def qkv_own_kernel(x_ref, gains_ref, w_ref, q_ref, k_ref, v_ref):
    spans = [slice(i * HALF, (i + 1) * HALF) for i in range(x_ref.shape[0] // HALF)]
    norms = [lambda s=s: norm_rows(x_ref[s, :].astype(f32), gains_ref[0:1, :]) for s in spans]

    def store(i, out):
        q_ref[spans[i], :] = (out[:, :D] * query_scale).astype(bf16)
        k_ref[spans[i], :] = out[:, D : 2 * D].astype(bf16)
        v_ref[spans[i], :] = out[:, 2 * D :].astype(bf16)

    qkv_rows(norms, w_ref, store)


def qkv_own(points, gains, qkv_weight):
    rows = points.shape[0]
    block = pl.BlockSpec((PATCH, D), lambda i: (i, 0))
    return pl.pallas_call(
        qkv_own_kernel,
        grid=(rows // PATCH,),
        in_specs=[block, whole((4, D)), layer_of((D, 3 * D), 0)],
        out_specs=[block] * 3,
        out_shape=[pltpu.HBM((n, D), bf16) for n in (rows, rows + PATCH, rows + PATCH)],
        name="qkv_own",
    )(points, gains, qkv_weight)


def qkv_halo_kernel(a_ref, b_ref, gains_ref, w_ref, k_in, v_in, after_in, k_ref, v_ref):
    norms = [
        lambda r=r: norm_rows(r[...].astype(f32), gains_ref[0:1, :]) for r in (a_ref, b_ref)
    ]

    def store(i, out):
        span = slice(i * HALF, (i + 1) * HALF)
        k_ref[span, :] = out[:, :D].astype(bf16)
        v_ref[span, :] = out[:, D:].astype(bf16)

    qkv_rows(norms, w_ref.at[:, D:], store)


def qkv_halo(before, after, gains, qkv_weight, keys, values, earlier):
    last = keys.shape[0] // PATCH - 1
    ext = pltpu.HBM(keys.shape, bf16)
    return pl.pallas_call(
        qkv_halo_kernel,
        grid=(1,),
        in_specs=[
            pl.BlockSpec(memory_space=pltpu.VMEM),
            pl.BlockSpec(memory_space=pltpu.VMEM),
            whole((4, D)),
            layer_of((D, 3 * D), 0),
            pl.BlockSpec(memory_space=pltpu.HBM),
            pl.BlockSpec(memory_space=pltpu.HBM),
            pl.BlockSpec(memory_space=pltpu.HBM),
        ],
        out_specs=[pl.BlockSpec((PATCH, D), lambda i: (last, 0))] * 2,
        out_shape=[ext, ext],
        input_output_aliases={4: 0, 5: 1},
        compiler_params=pltpu.CompilerParams(vmem_limit_bytes=24 << 20),
        name="qkv_halo",
    )(before, after, gains, qkv_weight, keys, values, earlier)


def gather_specs(count):
    def spec(t):
        return pl.BlockSpec(
            (None, PART, D), lambda i, table: (jnp.maximum(table[i * count + t], 0), 0, 0)
        )

    return [spec(t) for t in range(count)]


def live_rows(table_ref, step, tile_refs):
    tiles = []
    for t, tile_ref in enumerate(tile_refs):
        live = table_ref[step * len(tile_refs) + t] >= 0
        tiles.append(jnp.where(live, tile_ref[...].astype(f32), 0.0))
    return jnp.concatenate(tiles, axis=0)


def qkv_owner_kernel(from_ref, *refs):
    part_refs, refs = refs[:PATCH_TILES], refs[PATCH_TILES:]
    gains_ref, w_ref, x_ref, q_ref, k_ref, v_ref = refs
    shape = (PATCH_TILES, PART, D)
    rows = live_rows(from_ref, pl.program_id(0), part_refs)
    x_ref[...] = rows.astype(bf16).reshape(shape)
    out = dot(norm_rows(rows, gains_ref[2:3, :]), w_ref[...])
    q_ref[...] = (out[:, :D] * query_scale).astype(bf16).reshape(shape)
    k_ref[...] = out[:, D : 2 * D].astype(bf16).reshape(shape)
    v_ref[...] = out[:, 2 * D :].astype(bf16).reshape(shape)


def qkv_owner(owner_from, part, gains, qkv_weight):
    block = pl.BlockSpec((PATCH_TILES, PART, D), lambda i, *_: (i, 0, 0))
    return pl.pallas_call(
        qkv_owner_kernel,
        grid_spec=pltpu.PrefetchScalarGridSpec(
            num_scalar_prefetch=1,
            grid=(SLOTS // PATCH_TILES,),
            in_specs=gather_specs(PATCH_TILES) + [whole((4, D)), layer_of((D, 3 * D), 1)],
            out_specs=[block] * 4,
        ),
        out_shape=[pltpu.HBM((SLOTS, PART, D), bf16)] * 4,
        name="qkv_owner",
    )(owner_from, *[part] * PATCH_TILES, gains, qkv_weight)


def forward_rows(inner, normed, up_ref, down_ref):
    def rise(j):
        return dot(normed, up_ref[:, HID * j : HID * (j + 1)])

    total = None
    up = rise(0)
    for j in range(FF // HID):
        later = rise(j + 1) if j + 1 < FF // HID else None
        one = dot(gelu(up).astype(bf16), down_ref[HID * j : HID * (j + 1), :])
        total = one if total is None else total + one
        up = later
    return (inner.astype(f32) + total).astype(bf16)


def forward_owner_kernel(from_ref, *refs):
    part_refs, refs = refs[:UNIT_TILES], refs[UNIT_TILES:]
    gains_ref, up_ref, down_ref, w_ref, x_ref, q_ref, k_ref, v_ref = refs
    shape = (UNIT_TILES, PART, D)
    rows = live_rows(from_ref, pl.program_id(0), part_refs)
    outer = forward_rows(rows, norm_rows(rows, gains_ref[1:2, :]), up_ref, down_ref)
    x_ref[...] = outer.reshape(shape)
    out = dot(norm_rows(outer.astype(f32), gains_ref[2:3, :]), w_ref[...])
    q_ref[...] = (out[:, :D] * query_scale).astype(bf16).reshape(shape)
    k_ref[...] = out[:, D : 2 * D].astype(bf16).reshape(shape)
    v_ref[...] = out[:, 2 * D :].astype(bf16).reshape(shape)


def forward_owner(owner_from, part, weights, qkv_weight):
    gains, _, up_weight, down_weight = weights
    block = pl.BlockSpec((UNIT_TILES, PART, D), lambda i, *_: (i, 0, 0))
    return pl.pallas_call(
        forward_owner_kernel,
        grid_spec=pltpu.PrefetchScalarGridSpec(
            num_scalar_prefetch=1,
            grid=(SLOTS // UNIT_TILES,),
            in_specs=gather_specs(UNIT_TILES)
            + [
                whole((4, D)),
                layer_of((D, FF), 0),
                layer_of((FF, D), 0),
                layer_of((D, 3 * D), 1),
            ],
            out_specs=[block] * 4,
        ),
        out_shape=[pltpu.HBM((SLOTS, PART, D), bf16)] * 4,
        compiler_params=pltpu.CompilerParams(vmem_limit_bytes=FULL_VMEM),
        name="forward_owner",
    )(owner_from, *[part] * UNIT_TILES, gains, up_weight, down_weight, qkv_weight)


def attention_parts(masked, first_tile, table_ref, q_ref, k_refs, v_refs, mixed_ref):
    pieces = len(k_refs)
    count = UNIT_TILES * PART
    rows = PATCH // pieces
    lanes = lax.broadcasted_iota(jnp.int32, (1, 128), 1)
    low = lanes < HEAD_DIM
    picks = [low.astype(f32).astype(bf16), (~low).astype(f32).astype(bf16)]
    queries = q_ref[...].reshape(count, D)
    ones = jnp.ones((rows, 128), bf16)
    extra_q = extra_k = None
    if masked:
        base = first_tile // PATCH_TILES * PATCH_TILES
        extra_q = jnp.broadcast_to((lanes == 0).astype(f32).astype(bf16), (count, 128))
        marks = []
        for t in range(PATCH_TILES):
            mark = jnp.where(table_ref[base + t] >= 0, 0.0, masked_score)
            marks.append(jnp.full((rows // PATCH_TILES, 128), mark, f32).astype(bf16))
        extra_k = jnp.concatenate(marks, axis=0)

    def scores(h):
        cols = slice(128 * (h // 2), 128 * (h // 2) + 128)
        q = queries[:, cols] * picks[h % 2]
        if masked:
            q = jnp.concatenate([q, extra_q], axis=1)
        out = []
        for k_ref in k_refs:
            k = k_ref[...].reshape(rows, D)[:, cols]
            if masked:
                k = jnp.concatenate([k, extra_k], axis=1)
            out.append(dot_t(q, k))
        return out

    def soften(parts):
        peak = functools.reduce(
            jnp.maximum, [jnp.max(s, axis=-1, keepdims=True) for s in parts]
        )
        return [jnp.exp2(s - peak).astype(bf16) for s in parts]

    def mix(h, parts):
        cols = slice(128 * (h // 2), 128 * (h // 2) + 128)
        total = None
        for p, v_ref in zip(parts, v_refs):
            v = v_ref[...].reshape(rows, D)[:, cols]
            one = dot(p, jnp.concatenate([v, ones], axis=1))
            total = one if total is None else total + one
        own = (total[:, :128] / total[:, 128:]).astype(bf16) * picks[h % 2]
        if h % 2:
            own = own + mixed_ref[:, cols]
        mixed_ref[:, cols] = own

    return scores, soften, mix


def block_kernel(units, masked, whole_units, layer, pieces, table_ref, x_ref, q_ref, *refs):
    k_refs, refs = refs[:pieces], refs[pieces:]
    v_refs, refs = refs[:pieces], refs[pieces:]
    gains_ref, _, *sources, out_ref, mixed_ref, proj_ref, up_ref, down_ref, sems = refs
    step = pl.program_id(0)
    count = UNIT_TILES * PART
    fetches = [
        pltpu.make_async_copy(source.at[layer], target, sems.at[i])
        for i, (source, target) in enumerate(zip(sources, (proj_ref, up_ref, down_ref)))
    ]

    def attention_steps():
        scores, soften, mix = attention_parts(
            masked, step * UNIT_TILES, table_ref, q_ref, k_refs, v_refs, mixed_ref
        )
        s = scores(0)
        yield
        for h in range(HEADS):
            later = None
            if h + 1 < HEADS:
                later = scores(h + 1)
                yield
            weights = soften(s)
            yield
            mix(h, weights)
            yield
            s = later

    def forward_steps(mixed, result):
        base = x_ref[...].reshape(count, D).astype(f32)
        gain = gains_ref[2 * layer + 1 : 2 * layer + 2, :]
        inner = (base + dot(mixed, proj_ref[...])).astype(bf16)
        yield
        normed = norm_rows(inner.astype(f32), gain)
        yield

        def rise(j):
            return dot(normed, up_ref[:, HID * j : HID * (j + 1)])

        total = None
        up = rise(0)
        yield
        for j in range(FF // HID):
            later = None
            if j + 1 < FF // HID:
                later = rise(j + 1)
                yield
            one = dot(gelu(up).astype(bf16), down_ref[HID * j : HID * (j + 1), :])
            total = one if total is None else total + one
            yield
            up = later
        result.extend((inner, total))

    def weave(first, *others, delay=0):
        done = object()
        streams = [first]
        for _ in range(delay):
            next(first)
        streams = [first, *others]
        while streams:
            for stream in list(streams):
                if next(stream, done) is done:
                    streams.remove(stream)

    def emit(inner, total, unit):
        outer = (inner.astype(f32) + total).astype(bf16)
        for t in range(UNIT_TILES):
            slot = table_ref[unit * UNIT_TILES + t]

            @pl.when(slot >= 0)
            def _():
                out_ref[jnp.maximum(slot, 0)] = outer[t * PART : (t + 1) * PART]

    if whole_units:

        @pl.when(step == 0)
        def _():
            for fetch in fetches:
                fetch.start()

        weave(attention_steps())

        @pl.when(step == 0)
        def _():
            for fetch in fetches:
                fetch.wait()

        result = []
        weave(forward_steps(mixed_ref[...], result))
        emit(*result, step)
        return

    @pl.when(step == 0)
    def _():
        for fetch in fetches:
            fetch.start()
        weave(attention_steps())
        for fetch in fetches:
            fetch.wait()

    @pl.when((step > 0) & (step < units))
    def _():
        result = []
        weave(attention_steps(), forward_steps(mixed_ref[...], result))
        emit(*result, step - 1)

    @pl.when(step == units)
    def _():
        result = []
        weave(forward_steps(mixed_ref[...], result))
        emit(*result, step - 1)


def attention_kernel(place, masked, sets, pieces, table_ref, *refs):
    x_refs, q_refs, refs = refs[:2], refs[2:4], refs[4:]
    key_sets, refs = refs[: 2 * pieces * sets], refs[2 * pieces * sets :]
    proj_ref, out_ref, token_ref, mixed_ref, tiles_ref, sems = refs[0], *refs[-5:]
    token_ref[...] = jnp.zeros_like(token_ref)
    step = pl.program_id(0)
    steps = pl.num_programs(0)
    count = UNIT_TILES * PART
    units = []
    for n in range(2):
        own = key_sets[2 * pieces * (n % sets) : 2 * pieces * (n % sets + 1)]
        units.append(
            attention_parts(
                masked,
                place(step, n) * UNIT_TILES,
                table_ref,
                q_refs[n],
                own[:pieces],
                own[pieces:],
                mixed_ref.at[n],
            )
        )

    def copy_of(at, n, t, act):
        slot = table_ref[place(at, n) * UNIT_TILES + t]

        @pl.when(slot >= 0)
        def _():
            i = (2 * at + n) * UNIT_TILES + t
            act(
                pltpu.make_async_copy(
                    tiles_ref.at[i], out_ref.at[jnp.maximum(slot, 0)], sems.at[i]
                )
            )

    def join(n):
        base = x_refs[n][...].reshape(count, D).astype(f32)
        inner = (base + dot(mixed_ref[n], proj_ref[...])).astype(bf16)
        tiles_ref[pl.ds((2 * step + n) * UNIT_TILES, UNIT_TILES)] = inner.reshape(
            UNIT_TILES, PART, D
        )

    jobs = [(n, h) for n in range(2) for h in range(HEADS)]
    s = units[0][0](0)
    for i, (n, h) in enumerate(jobs):
        later = None
        if i + 1 < len(jobs):
            after, head = jobs[i + 1]
            later = units[after][0](head)
        units[n][2](h, units[n][1](s))
        s = later
        if (n, h) == (1, 1):
            join(0)
    join(1)
    for n in range(2):
        for t in range(UNIT_TILES):
            copy_of(step, n, t, lambda copy: copy.start())

    @pl.when(step == steps - 1)
    def _():
        @pl.loop(0, steps)
        def _(at):
            for n in range(2):
                for t in range(UNIT_TILES):
                    copy_of(at, n, t, lambda copy: copy.wait())


def attention(name, table, x, q, key_sets, specs, steps, place, masked, layer, proj, packed):
    pieces = len(key_sets[0]) // 2
    args = [table, x, x, q, q]
    for one in key_sets:
        args += one
    args.append(proj)
    specs = [*specs, layer_of((D, D), layer)]
    aliases = {}
    if packed is not None:
        aliases = {len(args): 0}
        args.append(packed)
        specs.append(pl.BlockSpec(memory_space=pltpu.HBM))
    tiles = 2 * steps * UNIT_TILES
    return pl.pallas_call(
        functools.partial(attention_kernel, place, masked, len(key_sets), pieces),
        grid_spec=pltpu.PrefetchScalarGridSpec(
            num_scalar_prefetch=1,
            grid=(steps,),
            in_specs=specs,
            out_specs=[pl.BlockSpec(memory_space=pltpu.HBM), whole((8, 128))],
            scratch_shapes=[
                pltpu.VMEM((2, UNIT_TILES * PART, D), bf16),
                pltpu.VMEM((tiles, PART, D), bf16),
                pltpu.SemaphoreType.DMA((tiles,)),
            ],
        ),
        out_shape=[pltpu.HBM((PEERS, PART, D), bf16), jax.ShapeDtypeStruct((8, 128), f32)],
        input_output_aliases=aliases,
        name=name,
    )(*args)


def block(name, table, x, q, keys, values, specs, units, masked, whole_units, layer, weights, token):
    gains, *matrices = weights
    pieces = len(keys)
    count = UNIT_TILES * PART
    return pl.pallas_call(
        functools.partial(block_kernel, units, masked, whole_units, layer, pieces),
        grid_spec=pltpu.PrefetchScalarGridSpec(
            num_scalar_prefetch=1,
            grid=(units if whole_units else units + 1,),
            in_specs=specs
            + [whole((4, D)), whole((8, 128))]
            + [pl.BlockSpec(memory_space=pl.ANY)] * len(matrices),
            out_specs=whole((PEERS, PART, D)),
            scratch_shapes=[
                pltpu.VMEM((count, D), bf16),
                pltpu.VMEM((D, D), bf16),
                pltpu.VMEM((D, FF), bf16),
                pltpu.VMEM((FF, D), bf16),
                pltpu.SemaphoreType.DMA((len(matrices),)),
            ],
        ),
        out_shape=jax.ShapeDtypeStruct((PEERS, PART, D), bf16),
        compiler_params=pltpu.CompilerParams(vmem_limit_bytes=FULL_VMEM),
        name=name,
    )(table, x, q, *keys, *values, gains, token, *matrices)


def specs_a(chunk, x_place, place):
    shape = (UNIT_TILES, PART, D)
    own = TILES_DEV * TILE // HALF

    def first(i, *_):
        patch = (place(i) + 1) // 2
        return patch + patch // 2, 0

    def second(i, *_):
        patch = (place(i) + 1) // 2
        return jnp.where(patch == 1, 2, own + patch // 2), 0

    key_specs = [pl.BlockSpec((HALF, D), first), pl.BlockSpec((HALF, D), second)]
    return [
        pl.BlockSpec(shape, lambda i, *_: (x_place(i), chunk, 0)),
        pl.BlockSpec(shape, lambda i, *_: (place(i), chunk, 0)),
        *key_specs,
        *key_specs,
    ]


def attention_a(name, chunk, places, table, x, q, keys, values, proj, packed):
    first, second = [specs_a(chunk, lambda i, n=n: n, lambda i, n=n: n) for n in places]
    shared = (places[0] + 1) // 2 == (places[1] + 1) // 2
    key_sets = [[keys, keys, values, values]] * (1 if shared else 2)
    specs = [first[0], second[0], first[1], second[1], *first[2:]]
    if not shared:
        specs += second[2:]

    def place(i, n):
        return places[n]

    return attention(
        name, table, x, q, key_sets, specs, 1, place, False, 0, proj, packed
    )


def block_a(chunk, table, x, q, keys, values, weights, token):
    units = TILES_DEV // UNIT_TILES
    specs = specs_a(chunk, lambda i: i, lambda i: i)
    return block(
        "block_a", table, x, q, [keys] * 2, [values] * 2, specs, units, False, True, 0, weights, token
    )


def specs_b(x_place, place):
    shape = (UNIT_TILES, PART, D)
    patch = (PATCH_TILES, PART, D)
    key_spec = pl.BlockSpec(patch, lambda i, *_: (place(i) // 2, 0, 0))
    return [
        pl.BlockSpec(shape, lambda i, *_: (x_place(i), 0, 0)),
        pl.BlockSpec(shape, lambda i, *_: (place(i), 0, 0)),
    ] + [key_spec] * (2 * CHUNKS)


def attention_b(table, x, q, keys, values, proj):
    def place(i, n):
        return 2 * i + n

    first, second = [specs_b(lambda i, n=n: place(i, n), lambda i, n=n: place(i, n)) for n in (0, 1)]
    specs = [first[0], second[0], first[1], second[1], *first[2:]]
    return attention(
        "attention_b",
        table,
        x,
        q,
        [[*keys, *values]],
        specs,
        SLOTS // PATCH_TILES,
        place,
        True,
        1,
        proj,
        None,
    )


def block_b(table, x, q, keys, values, weights, token):
    units = SLOTS // UNIT_TILES
    specs = specs_b(prior, lambda i: now(i, units))
    return block(
        "block_b", table, x, q, keys, values, specs, units, True, False, 1, weights, token
    )


def forward_home_kernel(table_ref, *refs):
    part_refs, refs = refs[:UNIT_TILES], refs[UNIT_TILES:]
    gains_ref, up_ref, down_ref, out_ref = refs
    rows = live_rows(table_ref, pl.program_id(0), part_refs)
    normed = norm_rows(rows, gains_ref[3:4, :])
    out_ref[...] = forward_rows(rows, normed, up_ref, down_ref).reshape(UNIT_TILES, PART, D)


def forward_home(table, part, weights):
    gains, _, up_weight, down_weight = weights
    return pl.pallas_call(
        forward_home_kernel,
        grid_spec=pltpu.PrefetchScalarGridSpec(
            num_scalar_prefetch=1,
            grid=(TILES_DEV // UNIT_TILES,),
            in_specs=gather_specs(UNIT_TILES)
            + [whole((4, D)), layer_of((D, FF), 1), layer_of((FF, D), 1)],
            out_specs=pl.BlockSpec((UNIT_TILES, PART, D), lambda i, *_: (i, 0, 0)),
        ),
        out_shape=pltpu.HBM((TILES_DEV, TILE, D), bf16),
        compiler_params=pltpu.CompilerParams(vmem_limit_bytes=FULL_VMEM),
        name="forward_home",
    )(table, *[part] * UNIT_TILES, gains, up_weight, down_weight)


def home_kernel(table_ref, part_ref, done_in, out_ref, tiles_ref, in_sems, out_sems):
    arriving = [
        pltpu.make_async_copy(part_ref.at[table_ref[t]], tiles_ref.at[t], in_sems.at[t])
        for t in range(TILES_DEV)
    ]
    leaving = [
        pltpu.make_async_copy(
            tiles_ref.at[t], out_ref.at[t, pl.ds(PART, PART)], out_sems.at[t]
        )
        for t in range(TILES_DEV)
    ]
    for copy in arriving:
        copy.start()
    for copy, onward in zip(arriving, leaving):
        copy.wait()
        onward.start()
    for onward in leaving:
        onward.wait()


def home(table, part, done):
    hbm = pl.BlockSpec(memory_space=pltpu.HBM)
    return pl.pallas_call(
        home_kernel,
        grid_spec=pltpu.PrefetchScalarGridSpec(
            num_scalar_prefetch=1,
            grid=(1,),
            in_specs=[hbm, hbm],
            out_specs=hbm,
            scratch_shapes=[
                pltpu.VMEM((TILES_DEV, PART, D), bf16),
                pltpu.SemaphoreType.DMA((TILES_DEV,)),
                pltpu.SemaphoreType.DMA((TILES_DEV,)),
            ],
        ),
        out_shape=pltpu.HBM((TILES_DEV, TILE, D), bf16),
        input_output_aliases={2: 0},
        name="home",
    )(table, part, done)


def exchange(part):
    return lax.all_to_all(part, "chain", split_axis=0, concat_axis=0, tiled=True)


def body(
    points, norm_gains, qkv_weight, proj_weight, up_weight, down_weight, dest_slot, owner_from
):
    rows = points.shape[0]
    axes = ("chain", "group")
    ring = lax.axis_size(axes)
    before = lax.ppermute(points[rows - HALF :], axes, [(i, (i + 1) % ring) for i in range(ring)])
    after = lax.ppermute(points[:HALF], axes, [((i + 1) % ring, i) for i in range(ring)])
    weights = (norm_gains, proj_weight, up_weight, down_weight)
    tiled = (TILES_DEV, TILE, D)
    x = points.reshape(tiled)
    q, keys, values = qkv_own(points, norm_gains, qkv_weight)
    q = q.reshape(tiled)
    packed, token = attention_a(
        "attention_a_middle", 0, (1, 2), dest_slot, x, q, keys, values, proj_weight, None
    )
    keys, values = qkv_halo(before, after, norm_gains, qkv_weight, keys, values, token)
    packed, token = attention_a(
        "attention_a_edges", 0, (0, 3), dest_slot, x, q, keys, values, proj_weight, packed
    )
    early = exchange(packed)
    late = exchange(block_a(1, dest_slot, x, q, keys, values, weights, token))
    owned = [
        forward_owner(owner_from, early, weights, qkv_weight),
        qkv_owner(owner_from, late, norm_gains, qkv_weight),
    ]
    xs, qs, owner_keys, owner_values = zip(*owned)
    packed, token = attention_b(owner_from, xs[0], qs[0], owner_keys, owner_values, proj_weight)
    early = exchange(packed)
    late = exchange(block_b(owner_from, xs[1], qs[1], owner_keys, owner_values, weights, token))
    done = forward_home(dest_slot, early, weights)
    return home(dest_slot, late, done).reshape(rows, D)


def solution(mesh):
    placed = (
        P(("chain", "group"), None),
        P(),
        P(),
        P(),
        P(),
        P(),
        P(("chain", "group")),
        P(("chain", "group")),
    )
    return jax.shard_map(
        body, mesh=mesh, in_specs=placed, out_specs=P(("chain", "group"), None), check_vma=False
    )
```

```python
import functools

import jax
import jax.numpy as jnp
from jax import lax
from jax.experimental import pallas as pl
from jax.experimental.pallas import tpu as pltpu
from jax.sharding import PartitionSpec as P

D = 384
HEADS = 6
HEAD_DIM = 64
FF = 1536
PATCH = 1024
TILE = 128
TILES_DEV = 16
SLOTS = 24
PEERS = 32
PAIRS = HEADS // 2
CHUNKS = 2
PART = TILE // CHUNKS
PATCH_TILES = PATCH // TILE
UNIT_TILES = 4
HALF = PATCH // 2
HID = 256
FULL_VMEM = 65000 << 10

norm_epsilon = 1e-05
masked_score = -1000000000.0
query_scale = HEAD_DIM ** (-0.5) * 1.4426950408889634
f32 = jnp.float32
bf16 = jnp.bfloat16


def norm_rows(values, gain_row):
    center = values - jnp.mean(values, axis=-1, keepdims=True)
    spread = jnp.mean(center * center, axis=-1, keepdims=True)
    return (center * lax.rsqrt(spread + norm_epsilon) * gain_row).astype(bf16)


def gelu(x):
    return (0.5 * x) * (1.0 + lax.erf(x * 0.5 ** 0.5))


def dot(a, b):
    return jnp.dot(a, b, preferred_element_type=f32)


def dot_t(a, b):
    return lax.dot_general(a, b, (((1,), (1,)), ((), ())), preferred_element_type=f32)


def whole(shape):
    zeros = (0,) * len(shape)
    return pl.BlockSpec(shape, lambda *_: zeros)


def layer_of(shape, layer):
    zeros = (0,) * len(shape)
    return pl.BlockSpec((None, *shape), lambda *_: (layer, *zeros))


def qkv_rows(norms, w_ref, store):
    normed = norms[0]()
    for i in range(len(norms)):
        later = norms[i + 1]() if i + 1 < len(norms) else None
        store(i, dot(normed, w_ref[...]))
        normed = later


def now(i, units):
    return jnp.minimum(i, units - 1)


def prior(i):
    return jnp.maximum(i - 1, 0)


def qkv_own_kernel(x_ref, gains_ref, w_ref, q_ref, k_ref, v_ref):
    spans = [slice(i * HALF, (i + 1) * HALF) for i in range(x_ref.shape[0] // HALF)]
    norms = [lambda s=s: norm_rows(x_ref[s, :].astype(f32), gains_ref[0:1, :]) for s in spans]

    def store(i, out):
        q_ref[spans[i], :] = (out[:, :D] * query_scale).astype(bf16)
        k_ref[spans[i], :] = out[:, D : 2 * D].astype(bf16)
        v_ref[spans[i], :] = out[:, 2 * D :].astype(bf16)

    qkv_rows(norms, w_ref, store)


def qkv_own(points, gains, qkv_weight):
    rows = points.shape[0]
    block = pl.BlockSpec((PATCH, D), lambda i: (i, 0))
    return pl.pallas_call(
        qkv_own_kernel,
        grid=(rows // PATCH,),
        in_specs=[block, whole((4, D)), layer_of((D, 3 * D), 0)],
        out_specs=[block] * 3,
        out_shape=[pltpu.HBM((n, D), bf16) for n in (rows, rows + PATCH, rows + PATCH)],
        name="qkv_own",
    )(points, gains, qkv_weight)


def qkv_halo_kernel(a_ref, b_ref, gains_ref, w_ref, k_in, v_in, after_in, k_ref, v_ref):
    norms = [
        lambda r=r: norm_rows(r[...].astype(f32), gains_ref[0:1, :]) for r in (a_ref, b_ref)
    ]

    def store(i, out):
        span = slice(i * HALF, (i + 1) * HALF)
        k_ref[span, :] = out[:, :D].astype(bf16)
        v_ref[span, :] = out[:, D:].astype(bf16)

    qkv_rows(norms, w_ref.at[:, D:], store)


def qkv_halo(before, after, gains, qkv_weight, keys, values, earlier):
    last = keys.shape[0] // PATCH - 1
    ext = pltpu.HBM(keys.shape, bf16)
    return pl.pallas_call(
        qkv_halo_kernel,
        grid=(1,),
        in_specs=[
            pl.BlockSpec(memory_space=pltpu.VMEM),
            pl.BlockSpec(memory_space=pltpu.VMEM),
            whole((4, D)),
            layer_of((D, 3 * D), 0),
            pl.BlockSpec(memory_space=pltpu.HBM),
            pl.BlockSpec(memory_space=pltpu.HBM),
            pl.BlockSpec(memory_space=pltpu.HBM),
        ],
        out_specs=[pl.BlockSpec((PATCH, D), lambda i: (last, 0))] * 2,
        out_shape=[ext, ext],
        input_output_aliases={4: 0, 5: 1},
        compiler_params=pltpu.CompilerParams(vmem_limit_bytes=24 << 20),
        name="qkv_halo",
    )(before, after, gains, qkv_weight, keys, values, earlier)


def gather_specs(count, repeat=1):
    def spec(t):
        return pl.BlockSpec(
            (None, PART, D),
            lambda i, table: (jnp.maximum(table[i // repeat * count + t], 0), 0, 0),
        )

    return [spec(t) for t in range(count)]


def live_rows(table_ref, step, tile_refs):
    tiles = []
    for t, tile_ref in enumerate(tile_refs):
        live = table_ref[step * len(tile_refs) + t] >= 0
        tiles.append(jnp.where(live, tile_ref[...].astype(f32), 0.0))
    return jnp.concatenate(tiles, axis=0)


def forward_rows(inner, normed, up_ref, down_ref):
    def rise(j):
        return dot(normed, up_ref[:, HID * j : HID * (j + 1)])

    total = None
    up = rise(0)
    for j in range(FF // HID):
        later = rise(j + 1) if j + 1 < FF // HID else None
        one = dot(gelu(up).astype(bf16), down_ref[HID * j : HID * (j + 1), :])
        total = one if total is None else total + one
        up = later
    return (inner.astype(f32) + total).astype(bf16)


def forward_owner_kernel(from_ref, *refs):
    part_refs, refs = refs[:UNIT_TILES], refs[UNIT_TILES:]
    gains_ref, up_ref, down_ref, w_ref, x_ref, q_ref, k_ref, v_ref = refs
    shape = (UNIT_TILES, PART, D)
    rows = live_rows(from_ref, pl.program_id(0), part_refs)
    outer = forward_rows(rows, norm_rows(rows, gains_ref[1:2, :]), up_ref, down_ref)
    x_ref[...] = outer.reshape(shape)
    out = dot(norm_rows(outer.astype(f32), gains_ref[2:3, :]), w_ref[...])
    q_ref[...] = (out[:, :D] * query_scale).astype(bf16).reshape(shape)
    k_ref[...] = out[:, D : 2 * D].astype(bf16).reshape(shape)
    v_ref[...] = out[:, 2 * D :].astype(bf16).reshape(shape)


def forward_owner(owner_from, part, weights, qkv_weight):
    gains, _, up_weight, down_weight = weights
    block = pl.BlockSpec((UNIT_TILES, PART, D), lambda i, *_: (i, 0, 0))
    return pl.pallas_call(
        forward_owner_kernel,
        grid_spec=pltpu.PrefetchScalarGridSpec(
            num_scalar_prefetch=1,
            grid=(SLOTS // UNIT_TILES,),
            in_specs=gather_specs(UNIT_TILES)
            + [
                whole((4, D)),
                layer_of((D, FF), 0),
                layer_of((FF, D), 0),
                layer_of((D, 3 * D), 1),
            ],
            out_specs=[block] * 4,
        ),
        out_shape=[pltpu.HBM((SLOTS, PART, D), bf16)] * 4,
        compiler_params=pltpu.CompilerParams(vmem_limit_bytes=FULL_VMEM),
        name="forward_owner",
    )(owner_from, *[part] * UNIT_TILES, gains, up_weight, down_weight, qkv_weight)


def attention_parts(masked, first_tile, table_ref, q_ref, k_refs, v_refs, mixed_ref):
    pieces = len(k_refs)
    count = UNIT_TILES * PART
    rows = PATCH // pieces
    lanes = lax.broadcasted_iota(jnp.int32, (1, 128), 1)
    low = lanes < HEAD_DIM
    picks = [low.astype(f32).astype(bf16), (~low).astype(f32).astype(bf16)]
    queries = q_ref[...].reshape(count, D)
    ones = jnp.ones((rows, 128), bf16)
    extra_q = extra_k = None
    if masked:
        base = first_tile // PATCH_TILES * PATCH_TILES
        extra_q = jnp.broadcast_to((lanes == 0).astype(f32).astype(bf16), (count, 128))
        marks = []
        for t in range(PATCH_TILES):
            mark = jnp.where(table_ref[base + t] >= 0, 0.0, masked_score)
            marks.append(jnp.full((rows // PATCH_TILES, 128), mark, f32).astype(bf16))
        extra_k = jnp.concatenate(marks, axis=0)

    def scores(h):
        cols = slice(128 * (h // 2), 128 * (h // 2) + 128)
        q = queries[:, cols] * picks[h % 2]
        if masked:
            q = jnp.concatenate([q, extra_q], axis=1)
        out = []
        for k_ref in k_refs:
            k = k_ref[...].reshape(rows, D)[:, cols]
            if masked:
                k = jnp.concatenate([k, extra_k], axis=1)
            out.append(dot_t(q, k))
        return out

    def soften(parts):
        peak = functools.reduce(
            jnp.maximum, [jnp.max(s, axis=-1, keepdims=True) for s in parts]
        )
        return [jnp.exp2(s - peak).astype(bf16) for s in parts]

    def mix(h, parts):
        cols = slice(128 * (h // 2), 128 * (h // 2) + 128)
        total = None
        for p, v_ref in zip(parts, v_refs):
            v = v_ref[...].reshape(rows, D)[:, cols]
            one = dot(p, jnp.concatenate([v, ones], axis=1))
            total = one if total is None else total + one
        own = (total[:, :128] / total[:, 128:]).astype(bf16) * picks[h % 2]
        if h % 2:
            own = own + mixed_ref[:, cols]
        mixed_ref[:, cols] = own

    return scores, soften, mix


def block_kernel(units, masked, whole_units, layer, pieces, table_ref, x_ref, q_ref, *refs):
    k_refs, refs = refs[:pieces], refs[pieces:]
    v_refs, refs = refs[:pieces], refs[pieces:]
    gains_ref, _, *sources, out_ref, mixed_ref, proj_ref, up_ref, down_ref, sems = refs
    step = pl.program_id(0)
    count = UNIT_TILES * PART
    fetches = [
        pltpu.make_async_copy(source.at[layer], target, sems.at[i])
        for i, (source, target) in enumerate(zip(sources, (proj_ref, up_ref, down_ref)))
    ]

    def attention_steps():
        scores, soften, mix = attention_parts(
            masked, step * UNIT_TILES, table_ref, q_ref, k_refs, v_refs, mixed_ref
        )
        s = scores(0)
        yield
        for h in range(HEADS):
            later = None
            if h + 1 < HEADS:
                later = scores(h + 1)
                yield
            weights = soften(s)
            yield
            mix(h, weights)
            yield
            s = later

    def forward_steps(mixed, result):
        base = x_ref[...].reshape(count, D).astype(f32)
        gain = gains_ref[2 * layer + 1 : 2 * layer + 2, :]
        inner = (base + dot(mixed, proj_ref[...])).astype(bf16)
        yield
        normed = norm_rows(inner.astype(f32), gain)
        yield

        def rise(j):
            return dot(normed, up_ref[:, HID * j : HID * (j + 1)])

        total = None
        up = rise(0)
        yield
        for j in range(FF // HID):
            later = None
            if j + 1 < FF // HID:
                later = rise(j + 1)
                yield
            one = dot(gelu(up).astype(bf16), down_ref[HID * j : HID * (j + 1), :])
            total = one if total is None else total + one
            yield
            up = later
        result.extend((inner, total))

    def weave(first, *others, delay=0):
        done = object()
        streams = [first]
        for _ in range(delay):
            next(first)
        streams = [first, *others]
        while streams:
            for stream in list(streams):
                if next(stream, done) is done:
                    streams.remove(stream)

    def emit(inner, total, unit):
        outer = (inner.astype(f32) + total).astype(bf16)
        for t in range(UNIT_TILES):
            slot = table_ref[unit * UNIT_TILES + t]

            @pl.when(slot >= 0)
            def _():
                out_ref[jnp.maximum(slot, 0)] = outer[t * PART : (t + 1) * PART]

    if whole_units:

        @pl.when(step == 0)
        def _():
            for fetch in fetches:
                fetch.start()

        weave(attention_steps())

        @pl.when(step == 0)
        def _():
            for fetch in fetches:
                fetch.wait()

        result = []
        weave(forward_steps(mixed_ref[...], result))
        emit(*result, step)
        return

    @pl.when(step == 0)
    def _():
        for fetch in fetches:
            fetch.start()
        weave(attention_steps())
        for fetch in fetches:
            fetch.wait()

    @pl.when((step > 0) & (step < units))
    def _():
        result = []
        weave(attention_steps(), forward_steps(mixed_ref[...], result))
        emit(*result, step - 1)

    @pl.when(step == units)
    def _():
        result = []
        weave(forward_steps(mixed_ref[...], result))
        emit(*result, step - 1)


def attention_kernel(place, masked, arriving, table_ref, x_ref, q_ref, k_ref, *refs):
    if arriving:
        v_ref, *refs = refs
        part_refs, refs = refs[:PATCH_TILES], refs[PATCH_TILES:]
        gains_ref, w_ref, proj_ref, *refs = refs
        out_ref, token_ref, x1_ref, q1_ref, k1_ref, v1_ref, mixed_ref, tiles_ref, sems = refs
        k_refs, v_refs = [k_ref, k1_ref], [v_ref, v1_ref]
    else:
        k_refs, v_refs = [k_ref, refs[0]], refs[1:3]
        proj_ref = refs[3]
        out_ref, token_ref, mixed_ref, tiles_ref, sems = refs[-5:]
    token_ref[...] = jnp.zeros_like(token_ref)
    step = pl.program_id(0)
    units = pl.num_programs(0)
    count = UNIT_TILES * PART

    if arriving:

        @pl.when(step % 2 == 0)
        def _():
            shape = (PATCH_TILES, PART, D)
            rows = live_rows(table_ref, step // 2, part_refs)
            x1_ref[...] = rows.astype(bf16).reshape(shape)
            out = dot(norm_rows(rows, gains_ref[2:3, :]), w_ref[...])
            q1_ref[...] = (out[:, :D] * query_scale).astype(bf16).reshape(shape)
            k1_ref[...] = out[:, D : 2 * D].astype(bf16).reshape(shape)
            v1_ref[...] = out[:, 2 * D :].astype(bf16).reshape(shape)

    scores, soften, mix = attention_parts(
        masked, place(step) * UNIT_TILES, table_ref, q_ref, k_refs, v_refs, mixed_ref
    )
    s = scores(0)
    for h in range(HEADS):
        later = scores(h + 1) if h + 1 < HEADS else None
        mix(h, soften(s))
        s = later
    base = x_ref[...].reshape(count, D).astype(f32)
    inner = (base + dot(mixed_ref[...], proj_ref[...])).astype(bf16)
    tiles_ref[pl.ds(step * UNIT_TILES, UNIT_TILES)] = inner.reshape(UNIT_TILES, PART, D)

    def copy_of(unit, t, act):
        slot = table_ref[place(unit) * UNIT_TILES + t]

        @pl.when(slot >= 0)
        def _():
            i = unit * UNIT_TILES + t
            act(
                pltpu.make_async_copy(
                    tiles_ref.at[i], out_ref.at[jnp.maximum(slot, 0)], sems.at[i]
                )
            )

    for t in range(UNIT_TILES):
        copy_of(step, t, lambda copy: copy.start())

    @pl.when(step == units - 1)
    def _():
        @pl.loop(0, units)
        def _(unit):
            for t in range(UNIT_TILES):
                copy_of(unit, t, lambda copy: copy.wait())


def attention(name, args, specs, units, place, masked, arriving, packed):
    hbm = pl.BlockSpec(memory_space=pltpu.HBM)
    aliases = {}
    if packed is not None:
        aliases = {len(args): 0}
        args = [*args, packed]
        specs = [*specs, hbm]
    out_specs = [hbm, whole((8, 128))]
    out_shape = [pltpu.HBM((PEERS, PART, D), bf16), jax.ShapeDtypeStruct((8, 128), f32)]
    if arriving:
        out_specs += [pl.BlockSpec((PATCH_TILES, PART, D), lambda i, *_: (i // 2, 0, 0))] * 4
        out_shape += [pltpu.HBM((SLOTS, PART, D), bf16)] * 4
    return pl.pallas_call(
        functools.partial(attention_kernel, place, masked, arriving),
        grid_spec=pltpu.PrefetchScalarGridSpec(
            num_scalar_prefetch=1,
            grid=(units,),
            in_specs=specs,
            out_specs=out_specs,
            scratch_shapes=[
                pltpu.VMEM((UNIT_TILES * PART, D), bf16),
                pltpu.VMEM((units * UNIT_TILES, PART, D), bf16),
                pltpu.SemaphoreType.DMA((units * UNIT_TILES,)),
            ],
        ),
        out_shape=out_shape,
        input_output_aliases=aliases,
        name=name,
    )(*args)


def block(name, table, x, q, keys, values, specs, units, masked, whole_units, layer, weights, token):
    gains, *matrices = weights
    pieces = len(keys)
    count = UNIT_TILES * PART
    return pl.pallas_call(
        functools.partial(block_kernel, units, masked, whole_units, layer, pieces),
        grid_spec=pltpu.PrefetchScalarGridSpec(
            num_scalar_prefetch=1,
            grid=(units if whole_units else units + 1,),
            in_specs=specs
            + [whole((4, D)), whole((8, 128))]
            + [pl.BlockSpec(memory_space=pl.ANY)] * len(matrices),
            out_specs=whole((PEERS, PART, D)),
            scratch_shapes=[
                pltpu.VMEM((count, D), bf16),
                pltpu.VMEM((D, D), bf16),
                pltpu.VMEM((D, FF), bf16),
                pltpu.VMEM((FF, D), bf16),
                pltpu.SemaphoreType.DMA((len(matrices),)),
            ],
        ),
        out_shape=jax.ShapeDtypeStruct((PEERS, PART, D), bf16),
        compiler_params=pltpu.CompilerParams(vmem_limit_bytes=FULL_VMEM),
        name=name,
    )(table, x, q, *keys, *values, gains, token, *matrices)


def specs_a(chunk, x_place, place):
    shape = (UNIT_TILES, PART, D)
    own = TILES_DEV * TILE // HALF

    def first(i, *_):
        patch = (place(i) + 1) // 2
        return patch + patch // 2, 0

    def second(i, *_):
        patch = (place(i) + 1) // 2
        return jnp.where(patch == 1, 2, own + patch // 2), 0

    key_specs = [pl.BlockSpec((HALF, D), first), pl.BlockSpec((HALF, D), second)]
    return [
        pl.BlockSpec(shape, lambda i, *_: (x_place(i), chunk, 0)),
        pl.BlockSpec(shape, lambda i, *_: (place(i), chunk, 0)),
        *key_specs,
        *key_specs,
    ]


def attention_a(name, chunk, place, table, x, q, keys, values, proj, packed):
    args = [table, x, q, keys, keys, values, values, proj]
    specs = [*specs_a(chunk, place, place), layer_of((D, D), 0)]
    return attention(name, args, specs, 2, place, False, False, packed)


def block_a(chunk, table, x, q, keys, values, weights, token):
    units = TILES_DEV // UNIT_TILES
    specs = specs_a(chunk, prior, lambda i: now(i, units))
    return block(
        "block_a", table, x, q, [keys] * 2, [values] * 2, specs, units, False, False, 0, weights, token
    )


def specs_b(x_place, place):
    shape = (UNIT_TILES, PART, D)
    patch = (PATCH_TILES, PART, D)
    key_spec = pl.BlockSpec(patch, lambda i, *_: (place(i) // 2, 0, 0))
    return [
        pl.BlockSpec(shape, lambda i, *_: (x_place(i), 0, 0)),
        pl.BlockSpec(shape, lambda i, *_: (place(i), 0, 0)),
    ] + [key_spec] * (2 * CHUNKS)


def attention_b(table, x, q, keys, values, part, gains, qkv_weight, proj):
    def place(i):
        return i

    x_spec, q_spec, key_spec = specs_b(place, place)[:3]
    specs = [x_spec, q_spec, key_spec, key_spec, *gather_specs(PATCH_TILES, 2)]
    specs += [whole((4, D)), layer_of((D, 3 * D), 1), layer_of((D, D), 1)]
    args = [table, x, q, keys, values, *[part] * PATCH_TILES, gains, qkv_weight, proj]
    units = SLOTS // UNIT_TILES
    return attention("attention_b", args, specs, units, place, True, True, None)


def block_b(table, x, q, keys, values, weights, token):
    units = SLOTS // UNIT_TILES
    specs = specs_b(prior, lambda i: now(i, units))
    return block(
        "block_b", table, x, q, keys, values, specs, units, True, False, 1, weights, token
    )


def forward_home_kernel(table_ref, *refs):
    part_refs, refs = refs[:UNIT_TILES], refs[UNIT_TILES:]
    gains_ref, up_ref, down_ref, out_ref = refs
    rows = live_rows(table_ref, pl.program_id(0), part_refs)
    normed = norm_rows(rows, gains_ref[3:4, :])
    out_ref[...] = forward_rows(rows, normed, up_ref, down_ref).reshape(UNIT_TILES, PART, D)


def forward_home(table, part, weights):
    gains, _, up_weight, down_weight = weights
    return pl.pallas_call(
        forward_home_kernel,
        grid_spec=pltpu.PrefetchScalarGridSpec(
            num_scalar_prefetch=1,
            grid=(TILES_DEV // UNIT_TILES,),
            in_specs=gather_specs(UNIT_TILES)
            + [whole((4, D)), layer_of((D, FF), 1), layer_of((FF, D), 1)],
            out_specs=pl.BlockSpec((UNIT_TILES, PART, D), lambda i, *_: (i, 0, 0)),
        ),
        out_shape=pltpu.HBM((TILES_DEV, TILE, D), bf16),
        compiler_params=pltpu.CompilerParams(vmem_limit_bytes=FULL_VMEM),
        name="forward_home",
    )(table, *[part] * UNIT_TILES, gains, up_weight, down_weight)


def home_kernel(table_ref, part_ref, done_in, out_ref, tiles_ref, in_sems, out_sems):
    arriving = [
        pltpu.make_async_copy(part_ref.at[table_ref[t]], tiles_ref.at[t], in_sems.at[t])
        for t in range(TILES_DEV)
    ]
    leaving = [
        pltpu.make_async_copy(
            tiles_ref.at[t], out_ref.at[t, pl.ds(PART, PART)], out_sems.at[t]
        )
        for t in range(TILES_DEV)
    ]
    for copy in arriving:
        copy.start()
    for copy, onward in zip(arriving, leaving):
        copy.wait()
        onward.start()
    for onward in leaving:
        onward.wait()


def home(table, part, done):
    hbm = pl.BlockSpec(memory_space=pltpu.HBM)
    return pl.pallas_call(
        home_kernel,
        grid_spec=pltpu.PrefetchScalarGridSpec(
            num_scalar_prefetch=1,
            grid=(1,),
            in_specs=[hbm, hbm],
            out_specs=hbm,
            scratch_shapes=[
                pltpu.VMEM((TILES_DEV, PART, D), bf16),
                pltpu.SemaphoreType.DMA((TILES_DEV,)),
                pltpu.SemaphoreType.DMA((TILES_DEV,)),
            ],
        ),
        out_shape=pltpu.HBM((TILES_DEV, TILE, D), bf16),
        input_output_aliases={2: 0},
        name="home",
    )(table, part, done)


def exchange(part):
    return lax.all_to_all(part, "chain", split_axis=0, concat_axis=0, tiled=True)


def body(
    points, norm_gains, qkv_weight, proj_weight, up_weight, down_weight, dest_slot, owner_from
):
    rows = points.shape[0]
    axes = ("chain", "group")
    ring = lax.axis_size(axes)
    before = lax.ppermute(points[rows - HALF :], axes, [(i, (i + 1) % ring) for i in range(ring)])
    after = lax.ppermute(points[:HALF], axes, [((i + 1) % ring, i) for i in range(ring)])
    weights = (norm_gains, proj_weight, up_weight, down_weight)
    tiled = (TILES_DEV, TILE, D)
    x = points.reshape(tiled)
    q, keys, values = qkv_own(points, norm_gains, qkv_weight)
    q = q.reshape(tiled)
    packed, token = attention_a(
        "attention_a_middle", 0, lambda i: i + 1, dest_slot, x, q, keys, values, proj_weight, None
    )
    keys, values = qkv_halo(before, after, norm_gains, qkv_weight, keys, values, token)
    packed, token = attention_a(
        "attention_a_edges", 0, lambda i: 3 * i, dest_slot, x, q, keys, values, proj_weight, packed
    )
    early = exchange(packed)
    late = exchange(block_a(1, dest_slot, x, q, keys, values, weights, token))
    x0, q0, k0, v0 = forward_owner(owner_from, early, weights, qkv_weight)
    packed, token, x1, q1, k1, v1 = attention_b(
        owner_from, x0, q0, k0, v0, late, norm_gains, qkv_weight, proj_weight
    )
    early = exchange(packed)
    late = exchange(block_b(owner_from, x1, q1, [k0, k1], [v0, v1], weights, token))
    done = forward_home(dest_slot, early, weights)
    return home(dest_slot, late, done).reshape(rows, D)


def solution(mesh):
    placed = (
        P(("chain", "group"), None),
        P(),
        P(),
        P(),
        P(),
        P(),
        P(("chain", "group")),
        P(("chain", "group")),
    )
    return jax.shard_map(
        body, mesh=mesh, in_specs=placed, out_specs=P(("chain", "group"), None), check_vma=False
    )
```

```python
import functools

import jax
import jax.numpy as jnp
from jax import lax
from jax.experimental import pallas as pl
from jax.experimental.pallas import tpu as pltpu
from jax.sharding import PartitionSpec as P

D = 384
HEADS = 6
HEAD_DIM = 64
FF = 1536
PATCH = 1024
TILE = 128
TILES_DEV = 16
SLOTS = 24
PEERS = 32
PAIRS = HEADS // 2
CHUNKS = 2
PART = TILE // CHUNKS
PATCH_TILES = PATCH // TILE
UNIT_TILES = 4
HALF = PATCH // 2
HID = 256
FULL_VMEM = 65300 << 10

norm_epsilon = 1e-05
masked_score = -1000000000.0
query_scale = HEAD_DIM ** (-0.5) * 1.4426950408889634
f32 = jnp.float32
bf16 = jnp.bfloat16


def norm_rows(values, gain_row):
    center = values - jnp.mean(values, axis=-1, keepdims=True)
    spread = jnp.mean(center * center, axis=-1, keepdims=True)
    return (center * lax.rsqrt(spread + norm_epsilon) * gain_row).astype(bf16)


def gelu(x):
    return (0.5 * x) * (1.0 + lax.erf(x * 0.5 ** 0.5))


def dot(a, b):
    return jnp.dot(a, b, preferred_element_type=f32)


def dot_t(a, b):
    return lax.dot_general(a, b, (((1,), (1,)), ((), ())), preferred_element_type=f32)


def whole(shape):
    zeros = (0,) * len(shape)
    return pl.BlockSpec(shape, lambda *_: zeros)


def layer_of(shape, layer):
    zeros = (0,) * len(shape)
    return pl.BlockSpec((None, *shape), lambda *_: (layer, *zeros))


def qkv_rows(norms, w_ref, store):
    normed = norms[0]()
    for i in range(len(norms)):
        later = norms[i + 1]() if i + 1 < len(norms) else None
        store(i, dot(normed, w_ref[...]))
        normed = later


def now(i, units):
    return jnp.minimum(i, units - 1)


def prior(i):
    return jnp.maximum(i - 1, 0)


def qkv_own_kernel(x_ref, gains_ref, w_ref, q_ref, k_ref, v_ref):
    spans = [slice(i * HALF, (i + 1) * HALF) for i in range(x_ref.shape[0] // HALF)]
    norms = [lambda s=s: norm_rows(x_ref[s, :].astype(f32), gains_ref[0:1, :]) for s in spans]

    def store(i, out):
        q_ref[spans[i], :] = (out[:, :D] * query_scale).astype(bf16)
        k_ref[spans[i], :] = out[:, D : 2 * D].astype(bf16)
        v_ref[spans[i], :] = out[:, 2 * D :].astype(bf16)

    qkv_rows(norms, w_ref, store)


def qkv_own(points, gains, qkv_weight):
    rows = points.shape[0]
    block = pl.BlockSpec((PATCH, D), lambda i: (i, 0))
    return pl.pallas_call(
        qkv_own_kernel,
        grid=(rows // PATCH,),
        in_specs=[block, whole((4, D)), layer_of((D, 3 * D), 0)],
        out_specs=[block] * 3,
        out_shape=[pltpu.HBM((n, D), bf16) for n in (rows, rows + PATCH, rows + PATCH)],
        name="qkv_own",
    )(points, gains, qkv_weight)


def qkv_halo_kernel(a_ref, b_ref, gains_ref, w_ref, k_in, v_in, after_in, k_ref, v_ref):
    norms = [
        lambda r=r: norm_rows(r[...].astype(f32), gains_ref[0:1, :]) for r in (a_ref, b_ref)
    ]

    def store(i, out):
        span = slice(i * HALF, (i + 1) * HALF)
        k_ref[span, :] = out[:, :D].astype(bf16)
        v_ref[span, :] = out[:, D:].astype(bf16)

    qkv_rows(norms, w_ref.at[:, D:], store)


def qkv_halo(before, after, gains, qkv_weight, keys, values, earlier):
    last = keys.shape[0] // PATCH - 1
    ext = pltpu.HBM(keys.shape, bf16)
    return pl.pallas_call(
        qkv_halo_kernel,
        grid=(1,),
        in_specs=[
            whole((HALF, D)),
            whole((HALF, D)),
            whole((4, D)),
            layer_of((D, 3 * D), 0),
            pl.BlockSpec(memory_space=pltpu.HBM),
            pl.BlockSpec(memory_space=pltpu.HBM),
            pl.BlockSpec(memory_space=pltpu.HBM),
        ],
        out_specs=[pl.BlockSpec((PATCH, D), lambda i: (last, 0))] * 2,
        out_shape=[ext, ext],
        input_output_aliases={4: 0, 5: 1},
        compiler_params=pltpu.CompilerParams(vmem_limit_bytes=FULL_VMEM),
        name="qkv_halo",
    )(before, after, gains, qkv_weight, keys, values, earlier)


def gather_specs(count, repeat=1):
    def spec(t):
        return pl.BlockSpec(
            (None, PART, D),
            lambda i, table: (jnp.maximum(table[i // repeat * count + t], 0), 0, 0),
        )

    return [spec(t) for t in range(count)]


def live_rows(table_ref, step, tile_refs):
    tiles = []
    for t, tile_ref in enumerate(tile_refs):
        live = table_ref[step * len(tile_refs) + t] >= 0
        tiles.append(jnp.where(live, tile_ref[...].astype(f32), 0.0))
    return jnp.concatenate(tiles, axis=0)


def forward_rows(inner, normed, up_ref, down_ref):
    def rise(j):
        return dot(normed, up_ref[:, HID * j : HID * (j + 1)])

    total = None
    up = rise(0)
    for j in range(FF // HID):
        later = rise(j + 1) if j + 1 < FF // HID else None
        one = dot(gelu(up).astype(bf16), down_ref[HID * j : HID * (j + 1), :])
        total = one if total is None else total + one
        up = later
    return (inner.astype(f32) + total).astype(bf16)


def forward_owner_kernel(from_ref, *refs):
    part_refs, refs = refs[:UNIT_TILES], refs[UNIT_TILES:]
    gains_ref, up_ref, down_ref, w_ref, x_ref, q_ref, k_ref, v_ref = refs
    shape = (UNIT_TILES, PART, D)
    rows = live_rows(from_ref, pl.program_id(0), part_refs)
    outer = forward_rows(rows, norm_rows(rows, gains_ref[1:2, :]), up_ref, down_ref)
    x_ref[...] = outer.reshape(shape)
    out = dot(norm_rows(outer.astype(f32), gains_ref[2:3, :]), w_ref[...])
    q_ref[...] = (out[:, :D] * query_scale).astype(bf16).reshape(shape)
    k_ref[...] = out[:, D : 2 * D].astype(bf16).reshape(shape)
    v_ref[...] = out[:, 2 * D :].astype(bf16).reshape(shape)


def forward_owner(owner_from, part, weights, qkv_weight):
    gains, _, up_weight, down_weight = weights
    block = pl.BlockSpec((UNIT_TILES, PART, D), lambda i, *_: (i, 0, 0))
    return pl.pallas_call(
        forward_owner_kernel,
        grid_spec=pltpu.PrefetchScalarGridSpec(
            num_scalar_prefetch=1,
            grid=(SLOTS // UNIT_TILES,),
            in_specs=gather_specs(UNIT_TILES)
            + [
                whole((4, D)),
                layer_of((D, FF), 0),
                layer_of((FF, D), 0),
                layer_of((D, 3 * D), 1),
            ],
            out_specs=[block] * 4,
        ),
        out_shape=[pltpu.HBM((SLOTS, PART, D), bf16)] * 4,
        compiler_params=pltpu.CompilerParams(vmem_limit_bytes=FULL_VMEM),
        name="forward_owner",
    )(owner_from, *[part] * UNIT_TILES, gains, up_weight, down_weight, qkv_weight)


def attention_parts(masked, first_tile, table_ref, q_ref, k_refs, v_refs, mixed_ref):
    pieces = len(k_refs)
    count = UNIT_TILES * PART
    rows = PATCH // pieces
    lanes = lax.broadcasted_iota(jnp.int32, (1, 128), 1)
    low = lanes < HEAD_DIM
    picks = [low.astype(f32).astype(bf16), (~low).astype(f32).astype(bf16)]
    queries = q_ref[...].reshape(count, D)
    ones = jnp.ones((rows, 128), bf16)
    extra_q = extra_k = None
    if masked:
        base = first_tile // PATCH_TILES * PATCH_TILES
        extra_q = jnp.broadcast_to((lanes == 0).astype(f32).astype(bf16), (count, 128))
        marks = []
        for t in range(PATCH_TILES):
            mark = jnp.where(table_ref[base + t] >= 0, 0.0, masked_score)
            marks.append(jnp.full((rows // PATCH_TILES, 128), mark, f32).astype(bf16))
        extra_k = jnp.concatenate(marks, axis=0)

    def scores(h):
        cols = slice(128 * (h // 2), 128 * (h // 2) + 128)
        q = queries[:, cols] * picks[h % 2]
        if masked:
            q = jnp.concatenate([q, extra_q], axis=1)
        out = []
        for k_ref in k_refs:
            k = k_ref[...].reshape(rows, D)[:, cols]
            if masked:
                k = jnp.concatenate([k, extra_k], axis=1)
            out.append(dot_t(q, k))
        return out

    def soften(parts):
        peak = functools.reduce(
            jnp.maximum, [jnp.max(s, axis=-1, keepdims=True) for s in parts]
        )
        return [jnp.exp2(s - peak).astype(bf16) for s in parts]

    def mix(h, parts):
        cols = slice(128 * (h // 2), 128 * (h // 2) + 128)
        total = None
        for p, v_ref in zip(parts, v_refs):
            v = v_ref[...].reshape(rows, D)[:, cols]
            one = dot(p, jnp.concatenate([v, ones], axis=1))
            total = one if total is None else total + one
        own = (total[:, :128] / total[:, 128:]).astype(bf16) * picks[h % 2]
        if h % 2:
            own = own + mixed_ref[:, cols]
        mixed_ref[:, cols] = own

    return scores, soften, mix


def block_kernel(units, masked, whole_units, layer, pieces, table_ref, x_ref, q_ref, *refs):
    k_refs, refs = refs[:pieces], refs[pieces:]
    v_refs, refs = refs[:pieces], refs[pieces:]
    gains_ref, _, *sources, out_ref, mixed_ref, proj_ref, up_ref, down_ref, sems = refs
    step = pl.program_id(0)
    count = UNIT_TILES * PART
    fetches = [
        pltpu.make_async_copy(source.at[layer], target, sems.at[i])
        for i, (source, target) in enumerate(zip(sources, (proj_ref, up_ref, down_ref)))
    ]

    def attention_steps():
        scores, soften, mix = attention_parts(
            masked, step * UNIT_TILES, table_ref, q_ref, k_refs, v_refs, mixed_ref
        )
        s = scores(0)
        yield
        for h in range(HEADS):
            later = None
            if h + 1 < HEADS:
                later = scores(h + 1)
                yield
            weights = soften(s)
            yield
            mix(h, weights)
            yield
            s = later

    def forward_steps(mixed, result):
        base = x_ref[...].reshape(count, D).astype(f32)
        gain = gains_ref[2 * layer + 1 : 2 * layer + 2, :]
        inner = (base + dot(mixed, proj_ref[...])).astype(bf16)
        yield
        normed = norm_rows(inner.astype(f32), gain)
        yield

        def rise(j):
            return dot(normed, up_ref[:, HID * j : HID * (j + 1)])

        total = None
        up = rise(0)
        yield
        for j in range(FF // HID):
            later = None
            if j + 1 < FF // HID:
                later = rise(j + 1)
                yield
            one = dot(gelu(up).astype(bf16), down_ref[HID * j : HID * (j + 1), :])
            total = one if total is None else total + one
            yield
            up = later
        result.extend((inner, total))

    def weave(first, *others, delay=0):
        done = object()
        streams = [first]
        for _ in range(delay):
            next(first)
        streams = [first, *others]
        while streams:
            for stream in list(streams):
                if next(stream, done) is done:
                    streams.remove(stream)

    def emit(inner, total, unit):
        outer = (inner.astype(f32) + total).astype(bf16)
        for t in range(UNIT_TILES):
            slot = table_ref[unit * UNIT_TILES + t]

            @pl.when(slot >= 0)
            def _():
                out_ref[jnp.maximum(slot, 0)] = outer[t * PART : (t + 1) * PART]

    if whole_units:

        @pl.when(step == 0)
        def _():
            for fetch in fetches:
                fetch.start()

        weave(attention_steps())

        @pl.when(step == 0)
        def _():
            for fetch in fetches:
                fetch.wait()

        result = []
        weave(forward_steps(mixed_ref[...], result))
        emit(*result, step)
        return

    @pl.when(step == 0)
    def _():
        for fetch in fetches:
            fetch.start()
        weave(attention_steps())
        for fetch in fetches:
            fetch.wait()

    @pl.when((step > 0) & (step < units))
    def _():
        result = []
        weave(attention_steps(), forward_steps(mixed_ref[...], result))
        emit(*result, step - 1)

    @pl.when(step == units)
    def _():
        result = []
        weave(forward_steps(mixed_ref[...], result))
        emit(*result, step - 1)


def attention_kernel(place, masked, arriving, table_ref, x_ref, q_ref, k_ref, *refs):
    if arriving:
        v_ref, *refs = refs
        part_refs, refs = refs[:PATCH_TILES], refs[PATCH_TILES:]
        gains_ref, w_ref, proj_ref, *refs = refs
        out_ref, x1_ref, q1_ref, k1_ref, v1_ref, mixed_ref, tiles_ref, sems = refs
        k_refs, v_refs = [k_ref, k1_ref], [v_ref, v1_ref]
    else:
        k_refs, v_refs = [k_ref, refs[0]], refs[1:3]
        proj_ref = refs[3]
        out_ref, mixed_ref, tiles_ref, sems = refs[-4:]
    step = pl.program_id(0)
    units = pl.num_programs(0)
    count = UNIT_TILES * PART

    if arriving:

        @pl.when(step % 2 == 0)
        def _():
            shape = (PATCH_TILES, PART, D)
            rows = live_rows(table_ref, step // 2, part_refs)
            x1_ref[...] = rows.astype(bf16).reshape(shape)
            out = dot(norm_rows(rows, gains_ref[2:3, :]), w_ref[...])
            q1_ref[...] = (out[:, :D] * query_scale).astype(bf16).reshape(shape)
            k1_ref[...] = out[:, D : 2 * D].astype(bf16).reshape(shape)
            v1_ref[...] = out[:, 2 * D :].astype(bf16).reshape(shape)

    scores, soften, mix = attention_parts(
        masked, place(step) * UNIT_TILES, table_ref, q_ref, k_refs, v_refs, mixed_ref
    )
    s = scores(0)
    for h in range(HEADS):
        later = scores(h + 1) if h + 1 < HEADS else None
        mix(h, soften(s))
        s = later
    base = x_ref[...].reshape(count, D).astype(f32)
    inner = (base + dot(mixed_ref[...], proj_ref[...])).astype(bf16)
    tiles_ref[pl.ds(step * UNIT_TILES, UNIT_TILES)] = inner.reshape(UNIT_TILES, PART, D)

    def copy_of(unit, t, act):
        slot = table_ref[place(unit) * UNIT_TILES + t]

        @pl.when(slot >= 0)
        def _():
            i = unit * UNIT_TILES + t
            act(
                pltpu.make_async_copy(
                    tiles_ref.at[i], out_ref.at[jnp.maximum(slot, 0)], sems.at[i]
                )
            )

    for t in range(UNIT_TILES):
        copy_of(step, t, lambda copy: copy.start())

    @pl.when(step == units - 1)
    def _():
        @pl.loop(0, units)
        def _(unit):
            for t in range(UNIT_TILES):
                copy_of(unit, t, lambda copy: copy.wait())


def attention(name, args, specs, units, place, masked, arriving, packed):
    hbm = pl.BlockSpec(memory_space=pltpu.HBM)
    aliases = {}
    if packed is not None:
        aliases = {len(args): 0}
        args = [*args, packed]
        specs = [*specs, hbm]
    out_specs = [hbm]
    out_shape = [pltpu.HBM((PEERS, PART, D), bf16)]
    if arriving:
        out_specs += [pl.BlockSpec((PATCH_TILES, PART, D), lambda i, *_: (i // 2, 0, 0))] * 4
        out_shape += [pltpu.HBM((SLOTS, PART, D), bf16)] * 4
    return pl.pallas_call(
        functools.partial(attention_kernel, place, masked, arriving),
        grid_spec=pltpu.PrefetchScalarGridSpec(
            num_scalar_prefetch=1,
            grid=(units,),
            in_specs=specs,
            out_specs=out_specs,
            scratch_shapes=[
                pltpu.VMEM((UNIT_TILES * PART, D), bf16),
                pltpu.VMEM((units * UNIT_TILES, PART, D), bf16),
                pltpu.SemaphoreType.DMA((units * UNIT_TILES,)),
            ],
        ),
        out_shape=out_shape,
        input_output_aliases=aliases,
        compiler_params=pltpu.CompilerParams(vmem_limit_bytes=FULL_VMEM),
        name=name,
    )(*args)


def block(name, table, x, q, keys, values, specs, units, masked, whole_units, layer, weights, earlier):
    gains, *matrices = weights
    pieces = len(keys)
    count = UNIT_TILES * PART
    return pl.pallas_call(
        functools.partial(block_kernel, units, masked, whole_units, layer, pieces),
        grid_spec=pltpu.PrefetchScalarGridSpec(
            num_scalar_prefetch=1,
            grid=(units if whole_units else units + 1,),
            in_specs=specs
            + [whole((4, D)), pl.BlockSpec(memory_space=pltpu.HBM)]
            + [pl.BlockSpec(memory_space=pl.ANY)] * len(matrices),
            out_specs=whole((PEERS, PART, D)),
            scratch_shapes=[
                pltpu.VMEM((count, D), bf16),
                pltpu.VMEM((D, D), bf16),
                pltpu.VMEM((D, FF), bf16),
                pltpu.VMEM((FF, D), bf16),
                pltpu.SemaphoreType.DMA((len(matrices),)),
            ],
        ),
        out_shape=jax.ShapeDtypeStruct((PEERS, PART, D), bf16),
        compiler_params=pltpu.CompilerParams(vmem_limit_bytes=FULL_VMEM),
        name=name,
    )(table, x, q, *keys, *values, gains, earlier, *matrices)


def specs_a(chunk, x_place, place):
    shape = (UNIT_TILES, PART, D)
    own = TILES_DEV * TILE // HALF

    def first(i, *_):
        patch = (place(i) + 1) // 2
        return patch + patch // 2, 0

    def second(i, *_):
        patch = (place(i) + 1) // 2
        return jnp.where(patch == 1, 2, own + patch // 2), 0

    key_specs = [pl.BlockSpec((HALF, D), first), pl.BlockSpec((HALF, D), second)]
    return [
        pl.BlockSpec(shape, lambda i, *_: (x_place(i), chunk, 0)),
        pl.BlockSpec(shape, lambda i, *_: (place(i), chunk, 0)),
        *key_specs,
        *key_specs,
    ]


def attention_a(name, chunk, place, table, x, q, keys, values, proj, packed):
    args = [table, x, q, keys, keys, values, values, proj]
    specs = [*specs_a(chunk, place, place), layer_of((D, D), 0)]
    return attention(name, args, specs, 2, place, False, False, packed)


def block_a(chunk, table, x, q, keys, values, weights, earlier):
    units = TILES_DEV // UNIT_TILES
    specs = specs_a(chunk, prior, lambda i: now(i, units))
    return block(
        "block_a", table, x, q, [keys] * 2, [values] * 2, specs, units, False, False, 0, weights, earlier
    )


def specs_b(x_place, place):
    shape = (UNIT_TILES, PART, D)
    patch = (PATCH_TILES, PART, D)
    key_spec = pl.BlockSpec(patch, lambda i, *_: (place(i) // 2, 0, 0))
    return [
        pl.BlockSpec(shape, lambda i, *_: (x_place(i), 0, 0)),
        pl.BlockSpec(shape, lambda i, *_: (place(i), 0, 0)),
    ] + [key_spec] * (2 * CHUNKS)


def attention_b(table, x, q, keys, values, part, gains, qkv_weight, proj):
    def place(i):
        return i

    x_spec, q_spec, key_spec = specs_b(place, place)[:3]
    specs = [x_spec, q_spec, key_spec, key_spec, *gather_specs(PATCH_TILES, 2)]
    specs += [whole((4, D)), layer_of((D, 3 * D), 1), layer_of((D, D), 1)]
    args = [table, x, q, keys, values, *[part] * PATCH_TILES, gains, qkv_weight, proj]
    units = SLOTS // UNIT_TILES
    return attention("attention_b", args, specs, units, place, True, True, None)


def block_b(table, x, q, keys, values, weights, earlier):
    units = SLOTS // UNIT_TILES
    specs = specs_b(prior, lambda i: now(i, units))
    return block(
        "block_b", table, x, q, keys, values, specs, units, True, False, 1, weights, earlier
    )


def forward_home_kernel(table_ref, *refs):
    part_refs, refs = refs[:UNIT_TILES], refs[UNIT_TILES:]
    gains_ref, up_ref, down_ref, out_ref = refs
    rows = live_rows(table_ref, pl.program_id(0), part_refs)
    normed = norm_rows(rows, gains_ref[3:4, :])
    out_ref[...] = forward_rows(rows, normed, up_ref, down_ref).reshape(UNIT_TILES, PART, D)


def forward_home(table, part, weights):
    gains, _, up_weight, down_weight = weights
    return pl.pallas_call(
        forward_home_kernel,
        grid_spec=pltpu.PrefetchScalarGridSpec(
            num_scalar_prefetch=1,
            grid=(TILES_DEV // UNIT_TILES,),
            in_specs=gather_specs(UNIT_TILES)
            + [whole((4, D)), layer_of((D, FF), 1), layer_of((FF, D), 1)],
            out_specs=pl.BlockSpec((UNIT_TILES, PART, D), lambda i, *_: (i, 0, 0)),
        ),
        out_shape=pltpu.HBM((TILES_DEV, TILE, D), bf16),
        compiler_params=pltpu.CompilerParams(vmem_limit_bytes=FULL_VMEM),
        name="forward_home",
    )(table, *[part] * UNIT_TILES, gains, up_weight, down_weight)


def home_kernel(table_ref, part_ref, done_in, out_ref, tiles_ref, in_sems, out_sems):
    arriving = [
        pltpu.make_async_copy(part_ref.at[table_ref[t]], tiles_ref.at[t], in_sems.at[t])
        for t in range(TILES_DEV)
    ]
    leaving = [
        pltpu.make_async_copy(
            tiles_ref.at[t], out_ref.at[t, pl.ds(PART, PART)], out_sems.at[t]
        )
        for t in range(TILES_DEV)
    ]
    for copy in arriving:
        copy.start()
    for copy, onward in zip(arriving, leaving):
        copy.wait()
        onward.start()
    for onward in leaving:
        onward.wait()


def home(table, part, done):
    hbm = pl.BlockSpec(memory_space=pltpu.HBM)
    return pl.pallas_call(
        home_kernel,
        grid_spec=pltpu.PrefetchScalarGridSpec(
            num_scalar_prefetch=1,
            grid=(1,),
            in_specs=[hbm, hbm],
            out_specs=hbm,
            scratch_shapes=[
                pltpu.VMEM((TILES_DEV, PART, D), bf16),
                pltpu.SemaphoreType.DMA((TILES_DEV,)),
                pltpu.SemaphoreType.DMA((TILES_DEV,)),
            ],
        ),
        out_shape=pltpu.HBM((TILES_DEV, TILE, D), bf16),
        input_output_aliases={2: 0},
        name="home",
    )(table, part, done)


def exchange(part):
    return lax.all_to_all(part, "chain", split_axis=0, concat_axis=0, tiled=True)


def body(
    points, norm_gains, qkv_weight, proj_weight, up_weight, down_weight, dest_slot, owner_from
):
    rows = points.shape[0]
    axes = ("chain", "group")
    ring = lax.axis_size(axes)
    before = lax.ppermute(points[rows - HALF :], axes, [(i, (i + 1) % ring) for i in range(ring)])
    after = lax.ppermute(points[:HALF], axes, [((i + 1) % ring, i) for i in range(ring)])
    weights = (norm_gains, proj_weight, up_weight, down_weight)
    tiled = (TILES_DEV, TILE, D)
    x = points.reshape(tiled)
    q, keys, values = qkv_own(points, norm_gains, qkv_weight)
    q = q.reshape(tiled)
    (packed,) = attention_a(
        "attention_a_middle", 0, lambda i: i + 1, dest_slot, x, q, keys, values, proj_weight, None
    )
    keys, values = qkv_halo(before, after, norm_gains, qkv_weight, keys, values, packed)
    (packed,) = attention_a(
        "attention_a_edges", 0, lambda i: 3 * i, dest_slot, x, q, keys, values, proj_weight, packed
    )
    early = exchange(packed)
    late = exchange(block_a(1, dest_slot, x, q, keys, values, weights, packed))
    x0, q0, k0, v0 = forward_owner(owner_from, early, weights, qkv_weight)
    packed, x1, q1, k1, v1 = attention_b(
        owner_from, x0, q0, k0, v0, late, norm_gains, qkv_weight, proj_weight
    )
    early = exchange(packed)
    late = exchange(block_b(owner_from, x1, q1, [k0, k1], [v0, v1], weights, packed))
    done = forward_home(dest_slot, early, weights)
    return home(dest_slot, late, done).reshape(rows, D)


def solution(mesh):
    placed = (
        P(("chain", "group"), None),
        P(),
        P(),
        P(),
        P(),
        P(),
        P(("chain", "group")),
        P(("chain", "group")),
    )
    return jax.shard_map(
        body, mesh=mesh, in_specs=placed, out_specs=P(("chain", "group"), None), check_vma=False
    )
```

```python
import functools

import jax
import jax.numpy as jnp
from jax import lax
from jax.experimental import pallas as pl
from jax.experimental.pallas import tpu as pltpu
from jax.sharding import PartitionSpec as P

D = 384
HEADS = 6
HEAD_DIM = 64
FF = 1536
PATCH = 1024
TILE = 128
TILES_DEV = 16
SLOTS = 24
PEERS = 32
PAIRS = HEADS // 2
CHUNKS = 2
PART = TILE // CHUNKS
PATCH_TILES = PATCH // TILE
UNIT_TILES = 4
HALF = PATCH // 2
HID = 256
FULL_VMEM = 65000 << 10

norm_epsilon = 1e-05
masked_score = -1000000000.0
query_scale = HEAD_DIM ** (-0.5) * 1.4426950408889634
f32 = jnp.float32
bf16 = jnp.bfloat16


def norm_rows(values, gain_row):
    center = values - jnp.mean(values, axis=-1, keepdims=True)
    spread = jnp.mean(center * center, axis=-1, keepdims=True)
    return (center * lax.rsqrt(spread + norm_epsilon) * gain_row).astype(bf16)


def gelu(x):
    return (0.5 * x) * (1.0 + lax.erf(x * 0.5 ** 0.5))


def dot(a, b):
    return jnp.dot(a, b, preferred_element_type=f32)


def dot_t(a, b):
    return lax.dot_general(a, b, (((1,), (1,)), ((), ())), preferred_element_type=f32)


def whole(shape):
    zeros = (0,) * len(shape)
    return pl.BlockSpec(shape, lambda *_: zeros)


def layer_of(shape, layer):
    zeros = (0,) * len(shape)
    return pl.BlockSpec((None, *shape), lambda *_: (layer, *zeros))


def qkv_rows(norms, w_ref, store):
    normed = norms[0]()
    for i in range(len(norms)):
        later = norms[i + 1]() if i + 1 < len(norms) else None
        store(i, dot(normed, w_ref[...]))
        normed = later


def now(i, units):
    return jnp.minimum(i, units - 1)


def prior(i):
    return jnp.maximum(i - 1, 0)


def qkv_own_kernel(x_ref, gains_ref, w_ref, q_ref, k_ref, v_ref):
    spans = [slice(i * HALF, (i + 1) * HALF) for i in range(x_ref.shape[0] // HALF)]
    norms = [lambda s=s: norm_rows(x_ref[s, :].astype(f32), gains_ref[0:1, :]) for s in spans]

    def store(i, out):
        q_ref[spans[i], :] = (out[:, :D] * query_scale).astype(bf16)
        k_ref[spans[i], :] = out[:, D : 2 * D].astype(bf16)
        v_ref[spans[i], :] = out[:, 2 * D :].astype(bf16)

    qkv_rows(norms, w_ref, store)


def qkv_own(points, gains, qkv_weight):
    rows = points.shape[0]
    block = pl.BlockSpec((PATCH, D), lambda i: (i, 0))
    return pl.pallas_call(
        qkv_own_kernel,
        grid=(rows // PATCH,),
        in_specs=[block, whole((4, D)), layer_of((D, 3 * D), 0)],
        out_specs=[block] * 3,
        out_shape=[pltpu.HBM((n, D), bf16) for n in (rows, rows + PATCH, rows + PATCH)],
        name="qkv_own",
    )(points, gains, qkv_weight)


def qkv_halo_kernel(a_ref, b_ref, gains_ref, w_ref, k_in, v_in, after_in, k_ref, v_ref):
    norms = [
        lambda r=r: norm_rows(r[...].astype(f32), gains_ref[0:1, :]) for r in (a_ref, b_ref)
    ]

    def store(i, out):
        span = slice(i * HALF, (i + 1) * HALF)
        k_ref[span, :] = out[:, :D].astype(bf16)
        v_ref[span, :] = out[:, D:].astype(bf16)

    qkv_rows(norms, w_ref.at[:, D:], store)


def qkv_halo(before, after, gains, qkv_weight, keys, values, earlier):
    last = keys.shape[0] // PATCH - 1
    ext = pltpu.HBM(keys.shape, bf16)
    return pl.pallas_call(
        qkv_halo_kernel,
        grid=(1,),
        in_specs=[
            pl.BlockSpec(memory_space=pltpu.VMEM),
            pl.BlockSpec(memory_space=pltpu.VMEM),
            whole((4, D)),
            layer_of((D, 3 * D), 0),
            pl.BlockSpec(memory_space=pltpu.HBM),
            pl.BlockSpec(memory_space=pltpu.HBM),
            pl.BlockSpec(memory_space=pltpu.HBM),
        ],
        out_specs=[pl.BlockSpec((PATCH, D), lambda i: (last, 0))] * 2,
        out_shape=[ext, ext],
        input_output_aliases={4: 0, 5: 1},
        compiler_params=pltpu.CompilerParams(vmem_limit_bytes=24 << 20),
        name="qkv_halo",
    )(before, after, gains, qkv_weight, keys, values, earlier)


def gather_specs(count, repeat=1):
    def spec(t):
        return pl.BlockSpec(
            (None, PART, D),
            lambda i, table: (jnp.maximum(table[i // repeat * count + t], 0), 0, 0),
        )

    return [spec(t) for t in range(count)]


def live_rows(table_ref, step, tile_refs):
    tiles = []
    for t, tile_ref in enumerate(tile_refs):
        live = table_ref[step * len(tile_refs) + t] >= 0
        tiles.append(jnp.where(live, tile_ref[...].astype(f32), 0.0))
    return jnp.concatenate(tiles, axis=0)


def forward_rows(inner, normed, up_ref, down_ref):
    def rise(j):
        return dot(normed, up_ref[:, HID * j : HID * (j + 1)])

    total = None
    up = rise(0)
    for j in range(FF // HID):
        later = rise(j + 1) if j + 1 < FF // HID else None
        one = dot(gelu(up).astype(bf16), down_ref[HID * j : HID * (j + 1), :])
        total = one if total is None else total + one
        up = later
    return (inner.astype(f32) + total).astype(bf16)


def forward_owner_kernel(from_ref, *refs):
    part_refs, refs = refs[:UNIT_TILES], refs[UNIT_TILES:]
    gains_ref, up_ref, down_ref, w_ref, x_ref, q_ref, k_ref, v_ref = refs
    shape = (UNIT_TILES, PART, D)
    rows = live_rows(from_ref, pl.program_id(0), part_refs)
    outer = forward_rows(rows, norm_rows(rows, gains_ref[1:2, :]), up_ref, down_ref)
    x_ref[...] = outer.reshape(shape)
    out = dot(norm_rows(outer.astype(f32), gains_ref[2:3, :]), w_ref[...])
    q_ref[...] = (out[:, :D] * query_scale).astype(bf16).reshape(shape)
    k_ref[...] = out[:, D : 2 * D].astype(bf16).reshape(shape)
    v_ref[...] = out[:, 2 * D :].astype(bf16).reshape(shape)


def forward_owner(owner_from, part, weights, qkv_weight):
    gains, _, up_weight, down_weight = weights
    block = pl.BlockSpec((UNIT_TILES, PART, D), lambda i, *_: (i, 0, 0))
    return pl.pallas_call(
        forward_owner_kernel,
        grid_spec=pltpu.PrefetchScalarGridSpec(
            num_scalar_prefetch=1,
            grid=(SLOTS // UNIT_TILES,),
            in_specs=gather_specs(UNIT_TILES)
            + [
                whole((4, D)),
                layer_of((D, FF), 0),
                layer_of((FF, D), 0),
                layer_of((D, 3 * D), 1),
            ],
            out_specs=[block] * 4,
        ),
        out_shape=[pltpu.HBM((SLOTS, PART, D), bf16)] * 4,
        compiler_params=pltpu.CompilerParams(vmem_limit_bytes=FULL_VMEM),
        name="forward_owner",
    )(owner_from, *[part] * UNIT_TILES, gains, up_weight, down_weight, qkv_weight)


def attention_parts(masked, first_tile, table_ref, q_ref, k_refs, v_refs, mixed_ref):
    pieces = len(k_refs)
    count = UNIT_TILES * PART
    rows = PATCH // pieces
    lanes = lax.broadcasted_iota(jnp.int32, (1, 128), 1)
    low = lanes < HEAD_DIM
    picks = [low.astype(f32).astype(bf16), (~low).astype(f32).astype(bf16)]
    queries = q_ref[...].reshape(count, D)
    ones = jnp.ones((rows, 128), bf16)
    extra_q = extra_k = None
    if masked:
        base = first_tile // PATCH_TILES * PATCH_TILES
        extra_q = jnp.broadcast_to((lanes == 0).astype(f32).astype(bf16), (count, 128))
        marks = []
        for t in range(PATCH_TILES):
            mark = jnp.where(table_ref[base + t] >= 0, 0.0, masked_score)
            marks.append(jnp.full((rows // PATCH_TILES, 128), mark, f32).astype(bf16))
        extra_k = jnp.concatenate(marks, axis=0)

    def scores(h):
        cols = slice(128 * (h // 2), 128 * (h // 2) + 128)
        q = queries[:, cols] * picks[h % 2]
        if masked:
            q = jnp.concatenate([q, extra_q], axis=1)
        out = []
        for k_ref in k_refs:
            k = k_ref[...].reshape(rows, D)[:, cols]
            if masked:
                k = jnp.concatenate([k, extra_k], axis=1)
            out.append(dot_t(q, k))
        return out

    def soften(parts):
        peak = functools.reduce(
            jnp.maximum, [jnp.max(s, axis=-1, keepdims=True) for s in parts]
        )
        return [jnp.exp2(s - peak).astype(bf16) for s in parts]

    def mix(h, parts):
        cols = slice(128 * (h // 2), 128 * (h // 2) + 128)
        total = None
        for p, v_ref in zip(parts, v_refs):
            v = v_ref[...].reshape(rows, D)[:, cols]
            one = dot(p, jnp.concatenate([v, ones], axis=1))
            total = one if total is None else total + one
        own = (total[:, :128] / total[:, 128:]).astype(bf16) * picks[h % 2]
        if h % 2:
            own = own + mixed_ref[:, cols]
        mixed_ref[:, cols] = own

    return scores, soften, mix


def block_kernel(units, masked, whole_units, layer, pieces, table_ref, x_ref, q_ref, *refs):
    k_refs, refs = refs[:pieces], refs[pieces:]
    v_refs, refs = refs[:pieces], refs[pieces:]
    gains_ref, _, *sources, out_ref, mixed_ref, proj_ref, up_ref, down_ref, sems = refs
    step = pl.program_id(0)
    count = UNIT_TILES * PART
    fetches = [
        pltpu.make_async_copy(source.at[layer], target, sems.at[i])
        for i, (source, target) in enumerate(zip(sources, (proj_ref, up_ref, down_ref)))
    ]

    def attention_steps():
        scores, soften, mix = attention_parts(
            masked, step * UNIT_TILES, table_ref, q_ref, k_refs, v_refs, mixed_ref
        )
        s = scores(0)
        yield
        for h in range(HEADS):
            later = None
            if h + 1 < HEADS:
                later = scores(h + 1)
                yield
            weights = soften(s)
            yield
            mix(h, weights)
            yield
            s = later

    def forward_steps(mixed, result):
        base = x_ref[...].reshape(count, D).astype(f32)
        gain = gains_ref[2 * layer + 1 : 2 * layer + 2, :]
        inner = (base + dot(mixed, proj_ref[...])).astype(bf16)
        yield
        normed = norm_rows(inner.astype(f32), gain)
        yield

        def rise(j):
            return dot(normed, up_ref[:, HID * j : HID * (j + 1)])

        total = None
        up = rise(0)
        yield
        for j in range(FF // HID):
            later = None
            if j + 1 < FF // HID:
                later = rise(j + 1)
                yield
            one = dot(gelu(up).astype(bf16), down_ref[HID * j : HID * (j + 1), :])
            total = one if total is None else total + one
            yield
            up = later
        result.extend((inner, total))

    def weave(first, *others, delay=0):
        done = object()
        streams = [first]
        for _ in range(delay):
            next(first)
        streams = [first, *others]
        while streams:
            for stream in list(streams):
                if next(stream, done) is done:
                    streams.remove(stream)

    def emit(inner, total, unit):
        outer = (inner.astype(f32) + total).astype(bf16)
        for t in range(UNIT_TILES):
            slot = table_ref[unit * UNIT_TILES + t]

            @pl.when(slot >= 0)
            def _():
                out_ref[jnp.maximum(slot, 0)] = outer[t * PART : (t + 1) * PART]

    if whole_units:

        @pl.when(step == 0)
        def _():
            for fetch in fetches:
                fetch.start()

        weave(attention_steps())

        @pl.when(step == 0)
        def _():
            for fetch in fetches:
                fetch.wait()

        result = []
        weave(forward_steps(mixed_ref[...], result))
        emit(*result, step)
        return

    @pl.when(step == 0)
    def _():
        for fetch in fetches:
            fetch.start()
        weave(attention_steps())
        for fetch in fetches:
            fetch.wait()

    @pl.when((step > 0) & (step < units))
    def _():
        result = []
        weave(attention_steps(), forward_steps(mixed_ref[...], result))
        emit(*result, step - 1)

    @pl.when(step == units)
    def _():
        result = []
        weave(forward_steps(mixed_ref[...], result))
        emit(*result, step - 1)


def attention_kernel(place, masked, arriving, token, table_ref, before_ref, x_ref, q_ref, k_ref, *refs):
    if arriving:
        v_ref, *refs = refs
        part_refs, refs = refs[:PATCH_TILES], refs[PATCH_TILES:]
        gains_ref, w_ref, proj_ref, *refs = refs
        out_ref, x1_ref, q1_ref, k1_ref, v1_ref, mixed_ref, tiles_ref, sems = refs
        k_refs, v_refs = [k_ref, k1_ref], [v_ref, v1_ref]
    else:
        k_refs, v_refs = [k_ref, refs[0]], refs[1:3]
        proj_ref = refs[3]
        *refs, mixed_ref, tiles_ref, sems = refs[4:]
        out_ref = refs[-1]
        if token:
            out_ref, token_ref = refs[-2:]
            token_ref[...] = jnp.zeros_like(token_ref)
    step = pl.program_id(0)
    units = pl.num_programs(0)
    count = UNIT_TILES * PART

    if arriving:

        @pl.when(step % 2 == 0)
        def _():
            shape = (PATCH_TILES, PART, D)
            rows = live_rows(table_ref, step // 2, part_refs)
            x1_ref[...] = rows.astype(bf16).reshape(shape)
            out = dot(norm_rows(rows, gains_ref[2:3, :]), w_ref[...])
            q1_ref[...] = (out[:, :D] * query_scale).astype(bf16).reshape(shape)
            k1_ref[...] = out[:, D : 2 * D].astype(bf16).reshape(shape)
            v1_ref[...] = out[:, 2 * D :].astype(bf16).reshape(shape)

    scores, soften, mix = attention_parts(
        masked, place(step) * UNIT_TILES, table_ref, q_ref, k_refs, v_refs, mixed_ref.at[step % 2]
    )

    def join(unit, base_ref):
        base = base_ref[...].reshape(count, D).astype(f32)
        inner = (base + dot(mixed_ref[unit % 2], proj_ref[...])).astype(bf16)
        tiles_ref[pl.ds(unit * UNIT_TILES, UNIT_TILES)] = inner.reshape(UNIT_TILES, PART, D)

    s = scores(0)
    earlier = jnp.maximum(step - 1, 0)
    join(earlier, before_ref)
    for h in range(HEADS):
        later = scores(h + 1) if h + 1 < HEADS else None
        mix(h, soften(s))
        s = later

    def copy_of(unit, t, act):
        slot = table_ref[place(unit) * UNIT_TILES + t]

        @pl.when(slot >= 0)
        def _():
            i = unit * UNIT_TILES + t
            act(
                pltpu.make_async_copy(
                    tiles_ref.at[i], out_ref.at[jnp.maximum(slot, 0)], sems.at[i]
                )
            )

    @pl.when(step > 0)
    def _():
        for t in range(UNIT_TILES):
            copy_of(earlier, t, lambda copy: copy.start())

    @pl.when(step == units - 1)
    def _():
        join(step, x_ref)
        for t in range(UNIT_TILES):
            copy_of(step, t, lambda copy: copy.start())

        @pl.loop(0, units)
        def _(unit):
            for t in range(UNIT_TILES):
                copy_of(unit, t, lambda copy: copy.wait())


def attention(name, args, specs, units, place, masked, arriving, packed):
    token = packed is None and not arriving
    hbm = pl.BlockSpec(memory_space=pltpu.HBM)
    aliases = {}
    if packed is not None:
        aliases = {len(args): 0}
        args = [*args, packed]
        specs = [*specs, hbm]
    out_specs = [hbm]
    out_shape = [pltpu.HBM((PEERS, PART, D), bf16)]
    if token:
        out_specs.append(whole((8, 128)))
        out_shape.append(jax.ShapeDtypeStruct((8, 128), f32))
    if arriving:
        out_specs += [pl.BlockSpec((PATCH_TILES, PART, D), lambda i, *_: (i // 2, 0, 0))] * 4
        out_shape += [pltpu.HBM((SLOTS, PART, D), bf16)] * 4
    return pl.pallas_call(
        functools.partial(attention_kernel, place, masked, arriving, token),
        grid_spec=pltpu.PrefetchScalarGridSpec(
            num_scalar_prefetch=1,
            grid=(units,),
            in_specs=specs,
            out_specs=out_specs,
            scratch_shapes=[
                pltpu.VMEM((2, UNIT_TILES * PART, D), bf16),
                pltpu.VMEM((units * UNIT_TILES, PART, D), bf16),
                pltpu.SemaphoreType.DMA((units * UNIT_TILES,)),
            ],
        ),
        out_shape=out_shape,
        input_output_aliases=aliases,
        name=name,
    )(*args)


def block(name, table, x, q, keys, values, specs, units, masked, whole_units, layer, weights, earlier):
    gains, *matrices = weights
    pieces = len(keys)
    count = UNIT_TILES * PART
    return pl.pallas_call(
        functools.partial(block_kernel, units, masked, whole_units, layer, pieces),
        grid_spec=pltpu.PrefetchScalarGridSpec(
            num_scalar_prefetch=1,
            grid=(units if whole_units else units + 1,),
            in_specs=specs
            + [whole((4, D)), pl.BlockSpec(memory_space=pltpu.HBM)]
            + [pl.BlockSpec(memory_space=pl.ANY)] * len(matrices),
            out_specs=whole((PEERS, PART, D)),
            scratch_shapes=[
                pltpu.VMEM((count, D), bf16),
                pltpu.VMEM((D, D), bf16),
                pltpu.VMEM((D, FF), bf16),
                pltpu.VMEM((FF, D), bf16),
                pltpu.SemaphoreType.DMA((len(matrices),)),
            ],
        ),
        out_shape=jax.ShapeDtypeStruct((PEERS, PART, D), bf16),
        compiler_params=pltpu.CompilerParams(vmem_limit_bytes=FULL_VMEM),
        name=name,
    )(table, x, q, *keys, *values, gains, earlier, *matrices)


def specs_a(chunk, x_place, place):
    shape = (UNIT_TILES, PART, D)
    own = TILES_DEV * TILE // HALF

    def first(i, *_):
        patch = (place(i) + 1) // 2
        return patch + patch // 2, 0

    def second(i, *_):
        patch = (place(i) + 1) // 2
        return jnp.where(patch == 1, 2, own + patch // 2), 0

    key_specs = [pl.BlockSpec((HALF, D), first), pl.BlockSpec((HALF, D), second)]
    return [
        pl.BlockSpec(shape, lambda i, *_: (x_place(i), chunk, 0)),
        pl.BlockSpec(shape, lambda i, *_: (place(i), chunk, 0)),
        *key_specs,
        *key_specs,
    ]


def attention_a(name, chunk, place, table, x, q, keys, values, proj, packed):
    args = [table, x, x, q, keys, keys, values, values, proj]
    before = specs_a(chunk, lambda i: place(prior(i)), place)[0]
    specs = [before, *specs_a(chunk, place, place), layer_of((D, D), 0)]
    return attention(name, args, specs, 2, place, False, False, packed)


def block_a(chunk, table, x, q, keys, values, weights, earlier):
    units = TILES_DEV // UNIT_TILES
    specs = specs_a(chunk, prior, lambda i: now(i, units))
    return block(
        "block_a", table, x, q, [keys] * 2, [values] * 2, specs, units, False, False, 0, weights, earlier
    )


def specs_b(x_place, place):
    shape = (UNIT_TILES, PART, D)
    patch = (PATCH_TILES, PART, D)
    key_spec = pl.BlockSpec(patch, lambda i, *_: (place(i) // 2, 0, 0))
    return [
        pl.BlockSpec(shape, lambda i, *_: (x_place(i), 0, 0)),
        pl.BlockSpec(shape, lambda i, *_: (place(i), 0, 0)),
    ] + [key_spec] * (2 * CHUNKS)


def attention_b(table, x, q, keys, values, part, gains, qkv_weight, proj):
    def place(i):
        return i

    x_spec, q_spec, key_spec = specs_b(place, place)[:3]
    before = specs_b(prior, place)[0]
    specs = [before, x_spec, q_spec, key_spec, key_spec, *gather_specs(PATCH_TILES, 2)]
    specs += [whole((4, D)), layer_of((D, 3 * D), 1), layer_of((D, D), 1)]
    args = [table, x, x, q, keys, values, *[part] * PATCH_TILES, gains, qkv_weight, proj]
    units = SLOTS // UNIT_TILES
    return attention("attention_b", args, specs, units, place, True, True, None)


def block_b(table, x, q, keys, values, weights, earlier):
    units = SLOTS // UNIT_TILES
    specs = specs_b(prior, lambda i: now(i, units))
    return block(
        "block_b", table, x, q, keys, values, specs, units, True, False, 1, weights, earlier
    )


def forward_home_kernel(table_ref, *refs):
    part_refs, refs = refs[:UNIT_TILES], refs[UNIT_TILES:]
    gains_ref, up_ref, down_ref, out_ref = refs
    rows = live_rows(table_ref, pl.program_id(0), part_refs)
    normed = norm_rows(rows, gains_ref[3:4, :])
    out_ref[...] = forward_rows(rows, normed, up_ref, down_ref).reshape(UNIT_TILES, PART, D)


def forward_home(table, part, weights):
    gains, _, up_weight, down_weight = weights
    return pl.pallas_call(
        forward_home_kernel,
        grid_spec=pltpu.PrefetchScalarGridSpec(
            num_scalar_prefetch=1,
            grid=(TILES_DEV // UNIT_TILES,),
            in_specs=gather_specs(UNIT_TILES)
            + [whole((4, D)), layer_of((D, FF), 1), layer_of((FF, D), 1)],
            out_specs=pl.BlockSpec((UNIT_TILES, PART, D), lambda i, *_: (i, 0, 0)),
        ),
        out_shape=pltpu.HBM((TILES_DEV, TILE, D), bf16),
        compiler_params=pltpu.CompilerParams(vmem_limit_bytes=FULL_VMEM),
        name="forward_home",
    )(table, *[part] * UNIT_TILES, gains, up_weight, down_weight)


def home_kernel(table_ref, part_ref, done_in, out_ref, tiles_ref, in_sems, out_sems):
    arriving = [
        pltpu.make_async_copy(part_ref.at[table_ref[t]], tiles_ref.at[t], in_sems.at[t])
        for t in range(TILES_DEV)
    ]
    leaving = [
        pltpu.make_async_copy(
            tiles_ref.at[t], out_ref.at[t, pl.ds(PART, PART)], out_sems.at[t]
        )
        for t in range(TILES_DEV)
    ]
    for copy in arriving:
        copy.start()
    for copy, onward in zip(arriving, leaving):
        copy.wait()
        onward.start()
    for onward in leaving:
        onward.wait()


def home(table, part, done):
    hbm = pl.BlockSpec(memory_space=pltpu.HBM)
    return pl.pallas_call(
        home_kernel,
        grid_spec=pltpu.PrefetchScalarGridSpec(
            num_scalar_prefetch=1,
            grid=(1,),
            in_specs=[hbm, hbm],
            out_specs=hbm,
            scratch_shapes=[
                pltpu.VMEM((TILES_DEV, PART, D), bf16),
                pltpu.SemaphoreType.DMA((TILES_DEV,)),
                pltpu.SemaphoreType.DMA((TILES_DEV,)),
            ],
        ),
        out_shape=pltpu.HBM((TILES_DEV, TILE, D), bf16),
        input_output_aliases={2: 0},
        name="home",
    )(table, part, done)


def exchange(part):
    return lax.all_to_all(part, "chain", split_axis=0, concat_axis=0, tiled=True)


def body(
    points, norm_gains, qkv_weight, proj_weight, up_weight, down_weight, dest_slot, owner_from
):
    rows = points.shape[0]
    axes = ("chain", "group")
    ring = lax.axis_size(axes)
    before = lax.ppermute(points[rows - HALF :], axes, [(i, (i + 1) % ring) for i in range(ring)])
    after = lax.ppermute(points[:HALF], axes, [((i + 1) % ring, i) for i in range(ring)])
    weights = (norm_gains, proj_weight, up_weight, down_weight)
    tiled = (TILES_DEV, TILE, D)
    x = points.reshape(tiled)
    q, keys, values = qkv_own(points, norm_gains, qkv_weight)
    q = q.reshape(tiled)
    packed, token = attention_a(
        "attention_a_middle", 0, lambda i: i + 1, dest_slot, x, q, keys, values, proj_weight, None
    )
    keys, values = qkv_halo(before, after, norm_gains, qkv_weight, keys, values, token)
    (packed,) = attention_a(
        "attention_a_edges", 0, lambda i: 3 * i, dest_slot, x, q, keys, values, proj_weight, packed
    )
    early = exchange(packed)
    late = exchange(block_a(1, dest_slot, x, q, keys, values, weights, packed))
    x0, q0, k0, v0 = forward_owner(owner_from, early, weights, qkv_weight)
    packed, x1, q1, k1, v1 = attention_b(
        owner_from, x0, q0, k0, v0, late, norm_gains, qkv_weight, proj_weight
    )
    early = exchange(packed)
    late = exchange(block_b(owner_from, x1, q1, [k0, k1], [v0, v1], weights, packed))
    done = forward_home(dest_slot, early, weights)
    return home(dest_slot, late, done).reshape(rows, D)


def solution(mesh):
    placed = (
        P(("chain", "group"), None),
        P(),
        P(),
        P(),
        P(),
        P(),
        P(("chain", "group")),
        P(("chain", "group")),
    )
    return jax.shard_map(
        body, mesh=mesh, in_specs=placed, out_specs=P(("chain", "group"), None), check_vma=False
    )
```

```python
import functools

import jax
import jax.numpy as jnp
from jax import lax
from jax.experimental import pallas as pl
from jax.experimental.pallas import tpu as pltpu
from jax.sharding import PartitionSpec as P

D = 384
HEADS = 6
HEAD_DIM = 64
FF = 1536
PATCH = 1024
TILE = 128
TILES_DEV = 16
SLOTS = 24
PEERS = 32
PAIRS = HEADS // 2
CHUNKS = 2
PART = TILE // CHUNKS
PATCH_TILES = PATCH // TILE
UNIT_TILES = 4
HALF = PATCH // 2
HID = 256
FULL_VMEM = 65000 << 10

norm_epsilon = 1e-05
masked_score = -1000000000.0
query_scale = HEAD_DIM ** (-0.5) * 1.4426950408889634
f32 = jnp.float32
bf16 = jnp.bfloat16


def norm_rows(values, gain_row):
    center = values - jnp.mean(values, axis=-1, keepdims=True)
    spread = jnp.mean(center * center, axis=-1, keepdims=True)
    return (center * lax.rsqrt(spread + norm_epsilon) * gain_row).astype(bf16)


def gelu(x):
    return (0.5 * x) * (1.0 + lax.erf(x * 0.5 ** 0.5))


def dot(a, b):
    return jnp.dot(a, b, preferred_element_type=f32)


def dot_t(a, b):
    return lax.dot_general(a, b, (((1,), (1,)), ((), ())), preferred_element_type=f32)


def whole(shape):
    zeros = (0,) * len(shape)
    return pl.BlockSpec(shape, lambda *_: zeros)


def layer_of(shape, layer):
    zeros = (0,) * len(shape)
    return pl.BlockSpec((None, *shape), lambda *_: (layer, *zeros))


def qkv_rows(norms, w_ref, store):
    normed = norms[0]()
    for i in range(len(norms)):
        later = norms[i + 1]() if i + 1 < len(norms) else None
        store(i, dot(normed, w_ref[...]))
        normed = later


def now(i, units):
    return jnp.minimum(i, units - 1)


def prior(i):
    return jnp.maximum(i - 1, 0)


def qkv_own_kernel(x_ref, gains_ref, w_ref, q_ref, k_ref, v_ref):
    spans = [slice(i * HALF, (i + 1) * HALF) for i in range(x_ref.shape[0] // HALF)]
    norms = [lambda s=s: norm_rows(x_ref[s, :].astype(f32), gains_ref[0:1, :]) for s in spans]

    def store(i, out):
        q_ref[spans[i], :] = (out[:, :D] * query_scale).astype(bf16)
        k_ref[spans[i], :] = out[:, D : 2 * D].astype(bf16)
        v_ref[spans[i], :] = out[:, 2 * D :].astype(bf16)

    qkv_rows(norms, w_ref, store)


def qkv_own(points, gains, qkv_weight):
    rows = points.shape[0]
    block = pl.BlockSpec((PATCH, D), lambda i: (i, 0))
    return pl.pallas_call(
        qkv_own_kernel,
        grid=(rows // PATCH,),
        in_specs=[block, whole((4, D)), layer_of((D, 3 * D), 0)],
        out_specs=[block] * 3,
        out_shape=[pltpu.HBM((n, D), bf16) for n in (rows, rows + PATCH, rows + PATCH)],
        name="qkv_own",
    )(points, gains, qkv_weight)


def qkv_halo_kernel(a_ref, b_ref, gains_ref, w_ref, k_in, v_in, after_in, k_ref, v_ref):
    norms = [
        lambda r=r: norm_rows(r[...].astype(f32), gains_ref[0:1, :]) for r in (a_ref, b_ref)
    ]

    def store(i, out):
        span = slice(i * HALF, (i + 1) * HALF)
        k_ref[span, :] = out[:, :D].astype(bf16)
        v_ref[span, :] = out[:, D:].astype(bf16)

    qkv_rows(norms, w_ref.at[:, D:], store)


def qkv_halo(before, after, gains, qkv_weight, keys, values, earlier):
    last = keys.shape[0] // PATCH - 1
    ext = pltpu.HBM(keys.shape, bf16)
    return pl.pallas_call(
        qkv_halo_kernel,
        grid=(1,),
        in_specs=[
            pl.BlockSpec(memory_space=pltpu.VMEM),
            pl.BlockSpec(memory_space=pltpu.VMEM),
            whole((4, D)),
            layer_of((D, 3 * D), 0),
            pl.BlockSpec(memory_space=pltpu.HBM),
            pl.BlockSpec(memory_space=pltpu.HBM),
            pl.BlockSpec(memory_space=pltpu.HBM),
        ],
        out_specs=[pl.BlockSpec((PATCH, D), lambda i: (last, 0))] * 2,
        out_shape=[ext, ext],
        input_output_aliases={4: 0, 5: 1},
        compiler_params=pltpu.CompilerParams(vmem_limit_bytes=24 << 20),
        name="qkv_halo",
    )(before, after, gains, qkv_weight, keys, values, earlier)


def gather_specs(count, repeat=1):
    def spec(t):
        return pl.BlockSpec(
            (None, PART, D),
            lambda i, table: (jnp.maximum(table[i // repeat * count + t], 0), 0, 0),
        )

    return [spec(t) for t in range(count)]


def live_rows(table_ref, step, tile_refs):
    tiles = []
    for t, tile_ref in enumerate(tile_refs):
        live = table_ref[step * len(tile_refs) + t] >= 0
        tiles.append(jnp.where(live, tile_ref[...].astype(f32), 0.0))
    return jnp.concatenate(tiles, axis=0)


def forward_rows(inner, normed, up_ref, down_ref):
    def rise(j):
        return dot(normed, up_ref[:, HID * j : HID * (j + 1)])

    total = None
    up = rise(0)
    for j in range(FF // HID):
        later = rise(j + 1) if j + 1 < FF // HID else None
        one = dot(gelu(up).astype(bf16), down_ref[HID * j : HID * (j + 1), :])
        total = one if total is None else total + one
        up = later
    return (inner.astype(f32) + total).astype(bf16)


def forward_owner_kernel(from_ref, *refs):
    part_refs, refs = refs[:UNIT_TILES], refs[UNIT_TILES:]
    gains_ref, up_ref, down_ref, w_ref, x_ref, q_ref, k_ref, v_ref = refs
    shape = (UNIT_TILES, PART, D)
    rows = live_rows(from_ref, pl.program_id(0), part_refs)
    outer = forward_rows(rows, norm_rows(rows, gains_ref[1:2, :]), up_ref, down_ref)
    x_ref[...] = outer.reshape(shape)
    out = dot(norm_rows(outer.astype(f32), gains_ref[2:3, :]), w_ref[...])
    q_ref[...] = (out[:, :D] * query_scale).astype(bf16).reshape(shape)
    k_ref[...] = out[:, D : 2 * D].astype(bf16).reshape(shape)
    v_ref[...] = out[:, 2 * D :].astype(bf16).reshape(shape)


def forward_owner(owner_from, part, weights, qkv_weight):
    gains, _, up_weight, down_weight = weights
    block = pl.BlockSpec((UNIT_TILES, PART, D), lambda i, *_: (i, 0, 0))
    return pl.pallas_call(
        forward_owner_kernel,
        grid_spec=pltpu.PrefetchScalarGridSpec(
            num_scalar_prefetch=1,
            grid=(SLOTS // UNIT_TILES,),
            in_specs=gather_specs(UNIT_TILES)
            + [
                whole((4, D)),
                layer_of((D, FF), 0),
                layer_of((FF, D), 0),
                layer_of((D, 3 * D), 1),
            ],
            out_specs=[block] * 4,
        ),
        out_shape=[pltpu.HBM((SLOTS, PART, D), bf16)] * 4,
        compiler_params=pltpu.CompilerParams(vmem_limit_bytes=FULL_VMEM),
        name="forward_owner",
    )(owner_from, *[part] * UNIT_TILES, gains, up_weight, down_weight, qkv_weight)


def attention_parts(masked, first_tile, table_ref, q_ref, k_refs, v_refs, mixed_ref):
    pieces = len(k_refs)
    count = UNIT_TILES * PART
    rows = PATCH // pieces
    lanes = lax.broadcasted_iota(jnp.int32, (1, 128), 1)
    low = lanes < HEAD_DIM
    picks = [low.astype(f32).astype(bf16), (~low).astype(f32).astype(bf16)]
    queries = q_ref[...].reshape(count, D)
    ones = jnp.ones((rows, 128), bf16)
    extra_q = extra_k = None
    if masked:
        base = first_tile // PATCH_TILES * PATCH_TILES
        extra_q = jnp.broadcast_to((lanes == 0).astype(f32).astype(bf16), (count, 128))
        marks = []
        for t in range(PATCH_TILES):
            mark = jnp.where(table_ref[base + t] >= 0, 0.0, masked_score)
            marks.append(jnp.full((rows // PATCH_TILES, 128), mark, f32).astype(bf16))
        extra_k = jnp.concatenate(marks, axis=0)

    def scores(h):
        cols = slice(128 * (h // 2), 128 * (h // 2) + 128)
        q = queries[:, cols] * picks[h % 2]
        if masked:
            q = jnp.concatenate([q, extra_q], axis=1)
        out = []
        for k_ref in k_refs:
            k = k_ref[...].reshape(rows, D)[:, cols]
            if masked:
                k = jnp.concatenate([k, extra_k], axis=1)
            out.append(dot_t(q, k))
        return out

    def soften(parts):
        peak = functools.reduce(
            jnp.maximum, [jnp.max(s, axis=-1, keepdims=True) for s in parts]
        )
        return [jnp.exp2(s - peak).astype(bf16) for s in parts]

    def mix(h, parts):
        cols = slice(128 * (h // 2), 128 * (h // 2) + 128)
        total = None
        for p, v_ref in zip(parts, v_refs):
            v = v_ref[...].reshape(rows, D)[:, cols]
            one = dot(p, jnp.concatenate([v, ones], axis=1))
            total = one if total is None else total + one
        own = (total[:, :128] / total[:, 128:]).astype(bf16) * picks[h % 2]
        if h % 2:
            own = own + mixed_ref[:, cols]
        mixed_ref[:, cols] = own

    return scores, soften, mix


def block_kernel(units, masked, whole_units, layer, pieces, table_ref, x_ref, q_ref, *refs):
    k_refs, refs = refs[:pieces], refs[pieces:]
    v_refs, refs = refs[:pieces], refs[pieces:]
    gains_ref, _, *sources, out_ref, mixed_ref, proj_ref, up_ref, down_ref, sems = refs
    step = pl.program_id(0)
    count = UNIT_TILES * PART
    fetches = [
        pltpu.make_async_copy(source.at[layer], target, sems.at[i])
        for i, (source, target) in enumerate(zip(sources, (proj_ref, up_ref, down_ref)))
    ]

    def attention_steps():
        scores, soften, mix = attention_parts(
            masked, step * UNIT_TILES, table_ref, q_ref, k_refs, v_refs, mixed_ref
        )
        s = scores(0)
        yield
        for h in range(HEADS):
            later = None
            if h + 1 < HEADS:
                later = scores(h + 1)
                yield
            weights = soften(s)
            yield
            mix(h, weights)
            yield
            s = later

    def forward_steps(mixed, result):
        base = x_ref[...].reshape(count, D).astype(f32)
        gain = gains_ref[2 * layer + 1 : 2 * layer + 2, :]
        inner = (base + dot(mixed, proj_ref[...])).astype(bf16)
        yield
        normed = norm_rows(inner.astype(f32), gain)
        yield

        def rise(j):
            return dot(normed, up_ref[:, HID * j : HID * (j + 1)])

        total = None
        up = rise(0)
        yield
        for j in range(FF // HID):
            later = None
            if j + 1 < FF // HID:
                later = rise(j + 1)
                yield
            one = dot(gelu(up).astype(bf16), down_ref[HID * j : HID * (j + 1), :])
            total = one if total is None else total + one
            yield
            up = later
        result.extend((inner, total))

    def weave(first, *others, delay=0):
        done = object()
        streams = [first]
        for _ in range(delay):
            next(first)
        streams = [first, *others]
        while streams:
            for stream in list(streams):
                if next(stream, done) is done:
                    streams.remove(stream)

    def emit(inner, total, unit):
        outer = (inner.astype(f32) + total).astype(bf16)
        for t in range(UNIT_TILES):
            slot = table_ref[unit * UNIT_TILES + t]

            @pl.when(slot >= 0)
            def _():
                out_ref[jnp.maximum(slot, 0)] = outer[t * PART : (t + 1) * PART]

    if whole_units:

        @pl.when(step == 0)
        def _():
            for fetch in fetches:
                fetch.start()

        weave(attention_steps())

        @pl.when(step == 0)
        def _():
            for fetch in fetches:
                fetch.wait()

        result = []
        weave(forward_steps(mixed_ref[...], result))
        emit(*result, step)
        return

    @pl.when(step == 0)
    def _():
        for fetch in fetches:
            fetch.start()
        weave(attention_steps())
        for fetch in fetches:
            fetch.wait()

    @pl.when((step > 0) & (step < units))
    def _():
        result = []
        weave(attention_steps(), forward_steps(mixed_ref[...], result))
        emit(*result, step - 1)

    @pl.when(step == units)
    def _():
        result = []
        weave(forward_steps(mixed_ref[...], result))
        emit(*result, step - 1)


def attention_kernel(place, masked, arriving, token, table_ref, x_ref, q_ref, k_ref, *refs):
    if arriving:
        v_ref, *refs = refs
        part_refs, refs = refs[:PATCH_TILES], refs[PATCH_TILES:]
        gains_ref, w_ref, proj_ref, *refs = refs
        out_ref, x1_ref, q1_ref, k1_ref, v1_ref, mixed_ref, tiles_ref, sems = refs
        k_refs, v_refs = [k_ref, k1_ref], [v_ref, v1_ref]
    else:
        k_refs, v_refs = [k_ref, refs[0]], refs[1:3]
        proj_ref = refs[3]
        *refs, mixed_ref, tiles_ref, sems = refs[4:]
        out_ref = refs[-1]
        if token:
            out_ref, token_ref = refs[-2:]
            token_ref[...] = jnp.zeros_like(token_ref)
    step = pl.program_id(0)
    units = pl.num_programs(0)
    count = UNIT_TILES * PART

    if arriving:

        @pl.when(step % 2 == 0)
        def _():
            shape = (PATCH_TILES, PART, D)
            rows = live_rows(table_ref, step // 2, part_refs)
            x1_ref[...] = rows.astype(bf16).reshape(shape)
            out = dot(norm_rows(rows, gains_ref[2:3, :]), w_ref[...])
            q1_ref[...] = (out[:, :D] * query_scale).astype(bf16).reshape(shape)
            k1_ref[...] = out[:, D : 2 * D].astype(bf16).reshape(shape)
            v1_ref[...] = out[:, 2 * D :].astype(bf16).reshape(shape)

    scores, soften, mix = attention_parts(
        masked, place(step) * UNIT_TILES, table_ref, q_ref, k_refs, v_refs, mixed_ref
    )
    s = scores(0)
    for h in range(HEADS):
        later = scores(h + 1) if h + 1 < HEADS else None
        mix(h, soften(s))
        s = later
    base = x_ref[...].reshape(count, D).astype(f32)
    inner = (base + dot(mixed_ref[...], proj_ref[...])).astype(bf16)
    tiles_ref[pl.ds(step * UNIT_TILES, UNIT_TILES)] = inner.reshape(UNIT_TILES, PART, D)

    def copy_of(unit, t, act):
        slot = table_ref[place(unit) * UNIT_TILES + t]

        @pl.when(slot >= 0)
        def _():
            i = unit * UNIT_TILES + t
            act(
                pltpu.make_async_copy(
                    tiles_ref.at[i], out_ref.at[jnp.maximum(slot, 0)], sems.at[i]
                )
            )

    for t in range(UNIT_TILES):
        copy_of(step, t, lambda copy: copy.start())

    @pl.when(step == units - 1)
    def _():
        @pl.loop(0, units)
        def _(unit):
            for t in range(UNIT_TILES):
                copy_of(unit, t, lambda copy: copy.wait())


def attention(name, args, specs, units, place, masked, arriving, packed):
    token = packed is None and not arriving
    hbm = pl.BlockSpec(memory_space=pltpu.HBM)
    aliases = {}
    if packed is not None:
        aliases = {len(args): 0}
        args = [*args, packed]
        specs = [*specs, hbm]
    out_specs = [hbm]
    out_shape = [pltpu.HBM((PEERS, PART, D), bf16)]
    if token:
        out_specs.append(whole((8, 128)))
        out_shape.append(jax.ShapeDtypeStruct((8, 128), f32))
    if arriving:
        out_specs += [pl.BlockSpec((PATCH_TILES, PART, D), lambda i, *_: (i // 2, 0, 0))] * 4
        out_shape += [pltpu.HBM((SLOTS, PART, D), bf16)] * 4
    return pl.pallas_call(
        functools.partial(attention_kernel, place, masked, arriving, token),
        grid_spec=pltpu.PrefetchScalarGridSpec(
            num_scalar_prefetch=1,
            grid=(units,),
            in_specs=specs,
            out_specs=out_specs,
            scratch_shapes=[
                pltpu.VMEM((UNIT_TILES * PART, D), bf16),
                pltpu.VMEM((units * UNIT_TILES, PART, D), bf16),
                pltpu.SemaphoreType.DMA((units * UNIT_TILES,)),
            ],
        ),
        out_shape=out_shape,
        input_output_aliases=aliases,
        name=name,
    )(*args)


def block(name, table, x, q, keys, values, specs, units, masked, whole_units, layer, weights, earlier):
    gains, *matrices = weights
    pieces = len(keys)
    count = UNIT_TILES * PART
    return pl.pallas_call(
        functools.partial(block_kernel, units, masked, whole_units, layer, pieces),
        grid_spec=pltpu.PrefetchScalarGridSpec(
            num_scalar_prefetch=1,
            grid=(units if whole_units else units + 1,),
            in_specs=specs
            + [whole((4, D)), pl.BlockSpec(memory_space=pltpu.HBM)]
            + [pl.BlockSpec(memory_space=pl.ANY)] * len(matrices),
            out_specs=whole((PEERS, PART, D)),
            scratch_shapes=[
                pltpu.VMEM((count, D), bf16),
                pltpu.VMEM((D, D), bf16),
                pltpu.VMEM((D, FF), bf16),
                pltpu.VMEM((FF, D), bf16),
                pltpu.SemaphoreType.DMA((len(matrices),)),
            ],
        ),
        out_shape=jax.ShapeDtypeStruct((PEERS, PART, D), bf16),
        compiler_params=pltpu.CompilerParams(vmem_limit_bytes=FULL_VMEM),
        name=name,
    )(table, x, q, *keys, *values, gains, earlier, *matrices)


def specs_a(chunk, x_place, place):
    shape = (UNIT_TILES, PART, D)
    own = TILES_DEV * TILE // HALF

    def first(i, *_):
        patch = (place(i) + 1) // 2
        return patch + patch // 2, 0

    def second(i, *_):
        patch = (place(i) + 1) // 2
        return jnp.where(patch == 1, 2, own + patch // 2), 0

    key_specs = [pl.BlockSpec((HALF, D), first), pl.BlockSpec((HALF, D), second)]
    return [
        pl.BlockSpec(shape, lambda i, *_: (x_place(i), chunk, 0)),
        pl.BlockSpec(shape, lambda i, *_: (place(i), chunk, 0)),
        *key_specs,
        *key_specs,
    ]


def attention_a(name, chunk, place, table, x, q, keys, values, proj, packed):
    args = [table, x, q, keys, keys, values, values, proj]
    specs = [*specs_a(chunk, place, place), layer_of((D, D), 0)]
    return attention(name, args, specs, 2, place, False, False, packed)


def block_a(chunk, table, x, q, keys, values, weights, earlier):
    units = TILES_DEV // UNIT_TILES
    specs = specs_a(chunk, prior, lambda i: now(i, units))
    return block(
        "block_a", table, x, q, [keys] * 2, [values] * 2, specs, units, False, False, 0, weights, earlier
    )


def specs_b(x_place, place):
    shape = (UNIT_TILES, PART, D)
    patch = (PATCH_TILES, PART, D)
    key_spec = pl.BlockSpec(patch, lambda i, *_: (place(i) // 2, 0, 0))
    return [
        pl.BlockSpec(shape, lambda i, *_: (x_place(i), 0, 0)),
        pl.BlockSpec(shape, lambda i, *_: (place(i), 0, 0)),
    ] + [key_spec] * (2 * CHUNKS)


def attention_b(table, x, q, keys, values, part, gains, qkv_weight, proj):
    def place(i):
        return i

    x_spec, q_spec, key_spec = specs_b(place, place)[:3]
    specs = [x_spec, q_spec, key_spec, key_spec, *gather_specs(PATCH_TILES, 2)]
    specs += [whole((4, D)), layer_of((D, 3 * D), 1), layer_of((D, D), 1)]
    args = [table, x, q, keys, values, *[part] * PATCH_TILES, gains, qkv_weight, proj]
    units = SLOTS // UNIT_TILES
    return attention("attention_b", args, specs, units, place, True, True, None)


def block_b(table, x, q, keys, values, weights, earlier):
    units = SLOTS // UNIT_TILES
    specs = specs_b(prior, lambda i: now(i, units))
    return block(
        "block_b", table, x, q, keys, values, specs, units, True, False, 1, weights, earlier
    )


def forward_home_kernel(table_ref, *refs):
    part_refs, refs = refs[:UNIT_TILES], refs[UNIT_TILES:]
    gains_ref, up_ref, down_ref, out_ref = refs
    rows = live_rows(table_ref, pl.program_id(0), part_refs)
    normed = norm_rows(rows, gains_ref[3:4, :])
    out_ref[...] = forward_rows(rows, normed, up_ref, down_ref).reshape(UNIT_TILES, PART, D)


def forward_home(table, part, weights):
    gains, _, up_weight, down_weight = weights
    return pl.pallas_call(
        forward_home_kernel,
        grid_spec=pltpu.PrefetchScalarGridSpec(
            num_scalar_prefetch=1,
            grid=(TILES_DEV // UNIT_TILES,),
            in_specs=gather_specs(UNIT_TILES)
            + [whole((4, D)), layer_of((D, FF), 1), layer_of((FF, D), 1)],
            out_specs=pl.BlockSpec((UNIT_TILES, PART, D), lambda i, *_: (i, 0, 0)),
        ),
        out_shape=pltpu.HBM((TILES_DEV, TILE, D), bf16),
        compiler_params=pltpu.CompilerParams(vmem_limit_bytes=FULL_VMEM),
        name="forward_home",
    )(table, *[part] * UNIT_TILES, gains, up_weight, down_weight)


def home_kernel(table_ref, part_ref, done_in, out_ref, tiles_ref, in_sems, out_sems):
    arriving = [
        pltpu.make_async_copy(part_ref.at[table_ref[t]], tiles_ref.at[t], in_sems.at[t])
        for t in range(TILES_DEV)
    ]
    leaving = [
        pltpu.make_async_copy(
            tiles_ref.at[t], out_ref.at[t, pl.ds(PART, PART)], out_sems.at[t]
        )
        for t in range(TILES_DEV)
    ]
    for copy in arriving:
        copy.start()
    for copy, onward in zip(arriving, leaving):
        copy.wait()
        onward.start()
    for onward in leaving:
        onward.wait()


def home(table, part, done):
    hbm = pl.BlockSpec(memory_space=pltpu.HBM)
    return pl.pallas_call(
        home_kernel,
        grid_spec=pltpu.PrefetchScalarGridSpec(
            num_scalar_prefetch=1,
            grid=(1,),
            in_specs=[hbm, hbm],
            out_specs=hbm,
            scratch_shapes=[
                pltpu.VMEM((TILES_DEV, PART, D), bf16),
                pltpu.SemaphoreType.DMA((TILES_DEV,)),
                pltpu.SemaphoreType.DMA((TILES_DEV,)),
            ],
        ),
        out_shape=pltpu.HBM((TILES_DEV, TILE, D), bf16),
        input_output_aliases={2: 0},
        name="home",
    )(table, part, done)


def exchange(part):
    return lax.all_to_all(part, "chain", split_axis=0, concat_axis=0, tiled=True)


def body(
    points, norm_gains, qkv_weight, proj_weight, up_weight, down_weight, dest_slot, owner_from
):
    rows = points.shape[0]
    axes = ("chain", "group")
    ring = lax.axis_size(axes)
    before = lax.ppermute(points[rows - HALF :], axes, [(i, (i + 1) % ring) for i in range(ring)])
    after = lax.ppermute(points[:HALF], axes, [((i + 1) % ring, i) for i in range(ring)])
    weights = (norm_gains, proj_weight, up_weight, down_weight)
    tiled = (TILES_DEV, TILE, D)
    x = points.reshape(tiled)
    q, keys, values = qkv_own(points, norm_gains, qkv_weight)
    q = q.reshape(tiled)
    packed, token = attention_a(
        "attention_a_middle", 0, lambda i: i + 1, dest_slot, x, q, keys, values, proj_weight, None
    )
    keys, values = qkv_halo(before, after, norm_gains, qkv_weight, keys, values, token)
    (packed,) = attention_a(
        "attention_a_edges", 0, lambda i: 3 * i, dest_slot, x, q, keys, values, proj_weight, packed
    )
    early = exchange(packed)
    late = exchange(block_a(1, dest_slot, x, q, keys, values, weights, packed))
    x0, q0, k0, v0 = forward_owner(owner_from, early, weights, qkv_weight)
    packed, x1, q1, k1, v1 = attention_b(
        owner_from, x0, q0, k0, v0, late, norm_gains, qkv_weight, proj_weight
    )
    early = exchange(packed)
    late = exchange(block_b(owner_from, x1, q1, [k0, k1], [v0, v1], weights, packed))
    done = forward_home(dest_slot, early, weights)
    return home(dest_slot, late, done).reshape(rows, D)


def solution(mesh):
    placed = (
        P(("chain", "group"), None),
        P(),
        P(),
        P(),
        P(),
        P(),
        P(("chain", "group")),
        P(("chain", "group")),
    )
    return jax.shard_map(
        body, mesh=mesh, in_specs=placed, out_specs=P(("chain", "group"), None), check_vma=False
    )
```
